512 devices in a mesh: dp: 32 (over z, core), mp: 16 (over x, y).
Axes of the slice: x: 4, y: 4, z: 16, core: 2. Of those that a mesh axis runs over, the one named last changes fastest.
Arguments:
- hidden_in: bfloat16 [64, 512, 8192], P('dp', None, 'mp'), may hold values from -6 to 6
- query_act: bfloat16 [64, 512, 8192], P('dp', None, 'mp'), may hold values from -6 to 6
- key_act: bfloat16 [64, 512, 1024], P('dp'), may hold values from -6 to 6
- value_act: bfloat16 [64, 512, 1024], P('dp'), may hold values from -6 to 6
- ctx_grad: bfloat16 [64, 512, 8192], P('dp', None, 'mp'), may hold values from -6 to 6
- segment_ids: int32 [64, 512], P('dp'), may hold values from 0 to 3, never falling along the last dimension, each value on 1 to 256 neighbouring positions
- down_query: bfloat16 [8192, 128], P('mp'), may hold values from -0.0625 to 0.0625
- up_query: bfloat16 [128, 8192], P(None, 'mp'), may hold values from -0.5 to 0.5
- down_value: bfloat16 [8192, 128], P('mp'), may hold values from -0.0625 to 0.0625
- up_value: bfloat16 [128, 1024], replicated, may hold values from -0.5 to 0.5
- block_rows: int32 [3, 8192], P(None, 'mp'), may hold values from 0 to 63
- tile_rows: int32 [3, 8192], P(None, 'mp'), may hold values from 0 to 7
- block_value: int32 [1024], replicated, may hold values from 0 to 63
- tile_value: int32 [1024], replicated, may hold values from 0 to 7
- tile_bank: bfloat16 [8, 128, 128], replicated, may hold values from -0.5 to 0.5
- seed_feats: bfloat16 [1024, 8192], P('dp', 'mp'), may hold values from -6 to 6
Outputs:
- scores: float32 [64, 1024], P('dp', 'mp')
The draws below stay inside these ranges and needn't reach their ends.
All inputs are finite; a program needn't handle non-finite values.
Results may differ from the reference program's by a relative error of at most 0.022.
Values may be sent and summed in bfloat16 or wider, within the bound.
No kernel may reach another device: no remote copies, remote signals or barrier semaphores. Data moves between devices by JAX's collectives and lax.ppermute only.
A program may use at most 64 MiB of HBM per device.

```python
import math
import jax
import jax.numpy as jnp
import numpy as np
from jax import lax

D = 8192
H = 64
KVH = 8
DH = 128
R = 128
K = 8192
PB = 128
NT = 8
S = 512
KB = 64
CANDS = 64
SEEDS = 1024


def base_draw(key, full_shape):
    return jax.random.truncated_normal(key, -5.5, 5.5, full_shape, jnp.float32)


def draw_query_act(key, part):
    values_out = base_draw(jax.random.fold_in(key, 1), (CANDS, S, H, DH))
    return values_out.reshape(CANDS, S, H * DH).astype(jnp.bfloat16)


def draw_key_act(key, part):
    values_out = base_draw(jax.random.fold_in(key, 2), (CANDS, S, KVH, DH))
    return values_out.reshape(CANDS, S, KVH * DH).astype(jnp.bfloat16)


def with_ends(result, own_key, low, largest):
    longest = result.shape.index(max(result.shape))
    spots = []
    for shift in (0, 1):
        where = [jax.random.randint(jax.random.fold_in(own_key, axis), (), 0, length) for axis, length in enumerate(result.shape)]
        where[longest] = (where[longest] + shift) % result.shape[longest]
        spots.append(tuple(where))
    return result.at[spots[0]].set(low).at[spots[1]].set(largest)


def shard_levels(key, dims, shards, low, largest):
    level, own = 1.0, jax.random.fold_in(key, 6)
    for dim, blocks in shards:
        draws = jnp.exp(jax.random.uniform(jax.random.fold_in(own, dim), (blocks,), jnp.float32, low / len(shards), largest / len(shards)))
        level = level * jnp.repeat(draws, dims[dim] // blocks).reshape([-1 if axis == dim else 1 for axis in range(len(dims))])
    return level


def rank_table(number_of, skew):
    portions = [(1 << 20) // math.isqrt(standing ** skew) + 1 for standing in range(1, number_of + 1)]
    width = 1 + sum(portions) // (1 << 30)
    return np.cumsum(np.array([max(1, weight // width) for weight in portions]))


def skewed_ids(stream_key, dims, number_of, skew):
    listing = rank_table(number_of, skew)
    ticket = jax.random.randint(jax.random.fold_in(stream_key, 1), dims, 0, int(listing[number_of - 1]))
    rank = jnp.searchsorted(jnp.asarray(listing, jnp.int32), ticket, side="right")
    return jax.random.permutation(jax.random.fold_in(stream_key, 2), number_of)[rank].astype(jnp.int32)


def split_up(amount, total, reach, slope):
    loads = [(1 << 20) // math.isqrt(rank ** slope) + 1 for rank in range(2, amount + 1)]
    surplus, given = total - reach - (amount - 1), [1] * (amount - 1)
    while surplus > 0:
        candidates = [i for i in range(amount - 1) if given[i] < reach]
        pool, left = sum([loads[i] for i in candidates]), surplus
        for i in candidates:
            more = min(reach - given[i], max(1, left * loads[i] // pool), surplus)
            given[i] = given[i] + more
            surplus = surplus - more
    return np.array([reach] + given)


def uneven_parts(own_key, count, total, limit, lean):
    if count == 2:
        one = jax.random.randint(own_key, (), max(1, total - limit), min(limit, total - 1) + 1)
        return jnp.stack([one, total - one])
    lengths = jnp.asarray(split_up(count, total, limit, lean), jnp.int32)
    pairs = (count - 1) // 2
    source_of, sink = lengths[1:1 + 2 * pairs:2], lengths[2:2 + 2 * pairs:2]
    slack = jnp.minimum(source_of - 1, limit - sink)
    passed = jax.random.randint(jax.random.fold_in(own_key, 1), (pairs,), 0, 1 << 20) % (slack + 1)
    lengths = lengths.at[1:1 + 2 * pairs:2].set(source_of - passed).at[2:2 + 2 * pairs:2].set(sink + passed)
    return lengths[jax.random.permutation(jax.random.fold_in(own_key, 2), count)]


def normal_values(key, shape, width, bound, shards=(), held_as=jnp.bfloat16):
    level = shard_levels(key, shape, shards, -0.22, 0.18) if shards else 1.0
    result = jax.random.normal(key, shape, jnp.float32) * width * level
    return jnp.minimum(jnp.maximum(result, -bound), bound).astype(held_as)


def setup_inputs(seed: int = 0) -> dict:
    seeds = jax.random.split(jax.random.key(seed), 17)
    hidden_in = normal_values(seeds[0], (CANDS, S, D), 1.0, 6.0, ((0, 32), (2, 16)))
    query_act = draw_query_act(jax.random.fold_in(seeds[16], 71), 0)
    key_act = draw_key_act(jax.random.fold_in(seeds[16], 71), 0)
    value_act = normal_values(seeds[3], (CANDS, S, KVH * DH), 1.0, 6.0, ((0, 32),))
    ctx_grad = normal_values(seeds[4], (CANDS, S, H * DH), 1.0, 6.0, ((0, 32), (2, 16)))
    segment_ids = jax.vmap(lambda own: jnp.searchsorted(jnp.cumsum(uneven_parts(own, 4, S, S // 2, 1)), jnp.arange(S), side="right"))(jax.random.split(seeds[5], CANDS)).reshape((CANDS, S)).astype(jnp.int32)
    down_query = normal_values(seeds[6], (D, R), D ** -0.5, 0.0625, ((0, 16),))
    up_query = normal_values(seeds[7], (R, H * DH), R ** -0.5, 0.5, ((1, 16),))
    down_value = normal_values(seeds[8], (D, R), D ** -0.5, 0.0625, ((0, 16),))
    up_value = normal_values(seeds[9], (R, KVH * DH), R ** -0.5, 0.5)
    block_rows = with_ends(skewed_ids(seeds[10], (3, D), KB, 2), jax.random.fold_in(seeds[10], 3), 0, KB - 1).astype(jnp.int32)
    tile_rows = with_ends(jax.random.randint(seeds[11], (3, D), 0, NT), jax.random.fold_in(seeds[11], 1), 0, NT - 1).astype(jnp.int32)
    block_value = with_ends(skewed_ids(seeds[12], (KVH * DH,), KB, 2), jax.random.fold_in(seeds[12], 3), 0, KB - 1).astype(jnp.int32)
    tile_value = with_ends(jax.random.randint(seeds[13], (KVH * DH,), 0, NT), jax.random.fold_in(seeds[13], 1), 0, NT - 1).astype(jnp.int32)
    tile_bank = normal_values(seeds[14], (NT, R, PB), R ** -0.5, 0.5)
    seed_feats = normal_values(seeds[15], (SEEDS, K), 1.0, 6.0, ((0, 32), (1, 16)))
    return dict(hidden_in=hidden_in, query_act=query_act, key_act=key_act, value_act=value_act, ctx_grad=ctx_grad, segment_ids=segment_ids, down_query=down_query, up_query=up_query, down_value=down_value, up_value=up_value, block_rows=block_rows, tile_rows=tile_rows, block_value=block_value, tile_value=tile_value, tile_bank=tile_bank, seed_feats=seed_feats)


EPS = 1e-06

def rounded(value):
    return lax.optimization_barrier(value.astype(jnp.bfloat16)).astype(jnp.float32)

def reference(hidden_in, query_act, key_act, value_act, ctx_grad, segment_ids, down_query, up_query, down_value, up_value, block_rows, tile_rows, block_value, tile_value, tile_bank, seed_feats):
    head_group = H // KVH
    score_scale = 1.0 / math.sqrt(DH)
    both_down = jnp.concatenate([down_query, down_value], axis=1)
    bucket_ids = jnp.concatenate([(block_rows * NT + tile_rows).reshape(-1), block_value * NT + tile_value]).astype(jnp.int32)
    tile_table = tile_bank.astype(jnp.float32).reshape(NT * R, PB)
    position = jnp.arange(S, dtype=jnp.int32)
    causal = position[None, :] <= position[:, None]
    up_three = up_value.astype(jnp.float32).reshape(R, KVH, DH)

    def features(inputs):
        hidden, query, keyed, valued, grad_out, segment = inputs
        allowed = causal & (segment[:, None] == segment[None, :])
        lowrank_in = jnp.dot(hidden, both_down, preferred_element_type=jnp.float32).astype(jnp.bfloat16)
        query_h = query.reshape(S, H, DH).astype(jnp.float32)
        key_h = jnp.repeat(keyed.reshape(S, KVH, DH), head_group, axis=1).astype(jnp.float32)
        value_h = jnp.repeat(valued.reshape(S, KVH, DH), head_group, axis=1).astype(jnp.float32)
        grad_h = grad_out.reshape(S, H, DH).astype(jnp.float32)
        logits = jnp.einsum('qhd,khd->hqk', query_h, key_h) * score_scale
        logits = jnp.where(allowed[None], logits, -1e+30)
        row_top = lax.optimization_barrier(jnp.max(logits, axis=-1, keepdims=True))
        exp_terms = jnp.exp(logits - row_top)
        attn_probs = exp_terms / lax.optimization_barrier(jnp.sum(exp_terms, axis=-1, keepdims=True))
        value_grad = jnp.einsum('hqk,qhd->khd', rounded(attn_probs), grad_h).astype(jnp.bfloat16)
        prob_grad = jnp.einsum('qhd,khd->hqk', grad_h, value_h)
        row_delta = lax.optimization_barrier(jnp.sum(attn_probs * prob_grad, axis=-1, keepdims=True))
        logit_grad = rounded(attn_probs * (prob_grad - row_delta))
        query_grad = (jnp.einsum('hqk,khd->qhd', logit_grad, key_h) * score_scale).astype(jnp.bfloat16)
        query_flat = query_grad.reshape(S, H * DH)
        value_five = value_grad.reshape(S, KVH, head_group, DH).astype(jnp.float32)
        back_query = jnp.dot(query_flat, up_query.T, preferred_element_type=jnp.float32)
        back_value = jnp.einsum('skgd,rkd->sr', value_five, up_three)
        lowrank_back = jnp.concatenate([back_query, back_value], axis=1).astype(jnp.bfloat16)
        grad_down = jnp.dot(hidden.T, lowrank_back, preferred_element_type=jnp.float32)
        grad_upq = jnp.dot(lowrank_in[:, :R].T, query_flat, preferred_element_type=jnp.float32)
        grad_upv = jnp.einsum('sr,skgd->rkd', lowrank_in[:, R:].astype(jnp.float32), value_five).reshape(R, KVH * DH)
        grad_rows = jnp.concatenate([grad_down[:, :R], grad_down[:, R:], grad_upq.T, grad_upv.T], axis=0)
        block_sums = jax.ops.segment_sum(grad_rows, bucket_ids, num_segments=KB * NT)
        projected = jnp.dot(block_sums.reshape(KB, NT * R), tile_table, precision=lax.Precision.HIGHEST)
        return projected.reshape(K)
    feats = lax.map(features, (hidden_in, query_act, key_act, value_act, ctx_grad, segment_ids))
    feat_square = lax.optimization_barrier(jnp.sum(feats * feats, axis=1))
    numerator = jnp.dot(feats.astype(jnp.bfloat16), seed_feats.T, preferred_element_type=jnp.float32)
    return numerator * lax.rsqrt(feat_square / K + EPS)[:, None] * K ** (-0.5)
```

```python
import math

import jax
import jax.numpy as jnp
from jax import lax
from jax.experimental import pallas as pl
from jax.experimental.pallas import tpu as pltpu
from jax.sharding import PartitionSpec as P

H = 64
KVH = 8
DH = 128
R = 128
K = 8192
PB = 128
NT = 8
S = 512
KB = 64
EPS = 1e-06
LONGEST = 256
ROWS = 128
F32 = jnp.float32
BF16 = jnp.bfloat16


def dot_nn(a, b):
    return lax.dot_general(a, b, (((1,), (0,)), ((), ())), preferred_element_type=F32)


def dot_nt(a, b):
    return lax.dot_general(a, b, (((1,), (1,)), ((), ())), preferred_element_type=F32)


def attention_kernel(
    kv_index,
    hidden_ref,
    query_ref,
    grad_ref,
    key_ref,
    value_ref,
    segment_ref,
    down_query_ref,
    down_value_ref,
    up_query_ref,
    up_value_ref,
    send_ref,
    query_grad_ref,
    value_grad_ref,
    value_sum,
):
    cand = pl.program_id(0)
    parts = send_ref.shape[0]
    chunk = send_ref.shape[2]
    quarter = R // chunk
    heads = query_ref.shape[2] // DH
    score_scale = 1.0 / math.sqrt(DH)
    exp_scale = score_scale * math.log2(math.e)

    down = jnp.concatenate([down_query_ref[...].T, down_value_ref[...].T], axis=0)
    lowrank_in = dot_nt(down, hidden_ref[0])
    send_ref[0 : 2 * quarter, 0] = lowrank_in.astype(BF16).reshape(2 * quarter, chunk, S)

    segment_row = segment_ref[pl.ds(cand, 1), :].astype(F32)
    segment_col = jnp.broadcast_to(segment_row, (8, S)).T[:, 0:1]
    key = key_ref[0]
    value = value_ref[0]
    key_t = key.T
    value_sum[...] = jnp.zeros_like(value_sum)

    for block in range(S // ROWS):
        first = block * ROWS
        low = max(0, (first - LONGEST + 1) // ROWS * ROWS)
        high = first + ROWS
        width = high - low
        key_pos = low + lax.broadcasted_iota(jnp.int32, (width, ROWS), 0)
        row_pos = first + lax.broadcasted_iota(jnp.int32, (width, ROWS), 1)
        allowed = (key_pos <= row_pos) & (
            segment_col[low:high] == segment_row[:, first:high]
        )
        bias = jnp.where(allowed, 0.0, -1e30)
        for head in range(heads):
            cols = slice(head * DH, (head + 1) * DH)
            grad = grad_ref[0, first:high, cols]
            logits = dot_nt(key[low:high], query_ref[0, first:high, cols]) + bias
            row_top = jnp.max(logits, axis=0, keepdims=True)
            exp_terms = jnp.exp2((logits - row_top) * exp_scale)
            probs = exp_terms * (1.0 / jnp.sum(exp_terms, axis=0, keepdims=True))
            prob_grad = dot_nt(value[low:high], grad)
            row_delta = jnp.sum(probs * prob_grad, axis=0, keepdims=True)
            logit_grad = (probs * (prob_grad - row_delta)).astype(BF16)
            value_sum[low:high] += dot_nn(probs.astype(BF16), grad)
            query_grad = dot_nn(key_t[:, low:high], logit_grad) * score_scale
            query_grad_ref[0, cols, first:high] = query_grad.astype(BF16)

    value_grad = value_sum[...].astype(BF16)
    value_grad_ref[0] = value_grad
    back_query = dot_nn(up_query_ref[...], query_grad_ref[0])
    back_value = dot_nt(up_value_ref[...], value_grad)
    send_ref[2 * quarter : 3 * quarter, 0] = back_query.astype(BF16).reshape(quarter, chunk, S)
    send_ref[3 * quarter : parts, 0] = back_value.astype(BF16).reshape(quarter, chunk, S)


def sum_kernel(parts_ref, out_ref):
    total = jnp.sum(parts_ref[...].astype(F32), axis=0)
    out_ref[...] = jnp.broadcast_to(total.astype(BF16)[None], out_ref.shape)


def feature_kernel(
    kv_index,
    lowrank_ref,
    hidden_ref,
    query_grad_ref,
    value_grad_ref,
    block_ref,
    tile_ref,
    block_value_ref,
    tile_value_ref,
    bank_ref,
    out_ref,
):
    cands = hidden_ref.shape[0]
    kv = kv_index[0]
    pieces = [[], [], [], []]
    for cand in range(cands):
        lowrank = lowrank_ref[:, cand].reshape(4 * R, S)
        down = dot_nn(lowrank[2 * R :], hidden_ref[cand])
        pieces[0].append(down[:R])
        pieces[1].append(down[R:])
        pieces[2].append(dot_nt(lowrank[:R], query_grad_ref[cand]))
        pieces[3].append(dot_nn(lowrank[R : 2 * R], value_grad_ref[cand]))
    buckets = KB * NT
    sums = jnp.zeros((buckets, cands * R), F32)
    for kind in range(4):
        if kind < 3:
            ids = tile_ref[kind : kind + 1, :] * KB + block_ref[kind : kind + 1, :]
        else:
            ids = tile_value_ref[pl.ds(kv, 1), :] * KB + block_value_ref[pl.ds(kv, 1), :]
        rows = jnp.concatenate(pieces[kind], axis=0).astype(BF16)
        where = lax.broadcasted_iota(jnp.int32, (buckets, rows.shape[1]), 0)
        chosen = jnp.where(where == ids, 1.0, 0.0).astype(BF16)
        sums = sums + dot_nt(chosen, rows)
    wide = jnp.concatenate(
        [
            jnp.concatenate(
                [sums[t * KB : (t + 1) * KB, c * R : (c + 1) * R] for t in range(NT)], axis=1
            )
            for c in range(cands)
        ],
        axis=0,
    )
    high = wide.astype(BF16)
    low = (wide - high.astype(F32)).astype(BF16)
    bank = bank_ref[...].reshape(NT * R, PB)
    feats = dot_nn(high, bank) + dot_nn(low, bank)
    out_ref[...] = jnp.broadcast_to(feats.astype(BF16)[None], out_ref.shape)


def score_kernel(parts_ref, seeds_ref, out_ref):
    cands = out_ref.shape[0]
    seeds = out_ref.shape[1]
    feats = jnp.sum(parts_ref[...].astype(F32), axis=0)
    per_part = seeds_ref.shape[2] // PB
    totals = [jnp.zeros((seeds, PB), F32) for _ in range(cands)]
    for block in range(KB):
        at = block % per_part * PB
        seed = seeds_ref[block // per_part, :, at : at + PB].astype(F32)
        for c in range(cands):
            row = c * KB + block
            totals[c] = totals[c] + feats[row : row + 1] * seed
    for c in range(cands):
        mine = feats[c * KB : (c + 1) * KB]
        square = jnp.sum(jnp.sum(mine * mine, axis=0, keepdims=True), axis=1, keepdims=True)
        numerator = jnp.sum(totals[c].T, axis=0, keepdims=True)
        out_ref[c : c + 1, :] = numerator * lax.rsqrt(square / K + EPS) * K ** (-0.5)


VMEM = pl.BlockSpec(memory_space=pltpu.VMEM)
SMEM = pl.BlockSpec(memory_space=pltpu.SMEM)
PARAMS = pltpu.CompilerParams(vmem_limit_bytes=40 << 20)


def local(
    hidden_in,
    query_act,
    key_act,
    value_act,
    ctx_grad,
    segment_ids,
    down_query,
    up_query,
    down_value,
    up_value,
    block_rows,
    tile_rows,
    block_value,
    tile_value,
    tile_bank,
    seed_feats,
):
    model_index = lax.axis_index("mp")
    data_size = lax.axis_size("dp")
    model_size = lax.axis_size("mp")
    cands, seq_len, width = query_act.shape
    heads = width // DH
    kv = (model_index * heads // (H // KVH)).astype(jnp.int32)
    kv_index = kv.reshape(1)
    seeds_dev = seed_feats.shape[0]
    out_seeds = data_size * seeds_dev // model_size

    seed_moved = lax.ppermute(
        seed_feats,
        ("dp", "mp"),
        [
            (d * model_size + m, (m * 2 + d % 2) * model_size + d // 2)
            for d in range(data_size)
            for m in range(model_size)
        ],
    )
    seed_pair = lax.all_gather(
        seed_moved,
        "dp",
        axis=0,
        tiled=True,
        axis_index_groups=[[2 * z, 2 * z + 1] for z in range(data_size // 2)],
    )
    seeds_all = lax.all_gather(
        seed_pair,
        "dp",
        axis=0,
        tiled=False,
        axis_index_groups=[[2 * z + core for z in range(data_size // 2)] for core in range(2)],
    )

    chunk = 4 * R // model_size

    def per_cand(*shape):
        return pl.BlockSpec((1, *shape), lambda c, kv_ref: (c, 0, 0))

    def whole(*shape):
        return pl.BlockSpec(shape, lambda c, kv_ref: (0,) * len(shape))

    send, query_grad, value_grad = pl.pallas_call(
        attention_kernel,
        name="attention_backward",
        out_shape=(
            jax.ShapeDtypeStruct((model_size, cands, chunk, seq_len), BF16),
            jax.ShapeDtypeStruct((cands, width, seq_len), BF16),
            jax.ShapeDtypeStruct((cands, seq_len, DH), BF16),
        ),
        grid_spec=pltpu.PrefetchScalarGridSpec(
            num_scalar_prefetch=1,
            grid=(cands,),
            in_specs=[
                per_cand(seq_len, hidden_in.shape[2]),
                per_cand(seq_len, width),
                per_cand(seq_len, width),
                pl.BlockSpec((1, seq_len, DH), lambda c, kv_ref: (c, 0, kv_ref[0])),
                pl.BlockSpec((1, seq_len, DH), lambda c, kv_ref: (c, 0, kv_ref[0])),
                whole(cands, seq_len),
                whole(*down_query.shape),
                whole(*down_value.shape),
                whole(*up_query.shape),
                pl.BlockSpec((R, DH), lambda c, kv_ref: (0, kv_ref[0])),
            ],
            out_specs=[
                pl.BlockSpec((model_size, 1, chunk, seq_len), lambda c, kv_ref: (0, c, 0, 0)),
                per_cand(width, seq_len),
                per_cand(seq_len, DH),
            ],
            scratch_shapes=[pltpu.VMEM((seq_len, DH), F32)],
        ),
        compiler_params=PARAMS,
        cost_estimate=pl.CostEstimate(
            flops=5_000_000_000, bytes_accessed=8_000_000, transcendentals=2_000_000
        ),
    )(
        kv_index,
        hidden_in,
        query_act,
        ctx_grad,
        key_act,
        value_act,
        segment_ids,
        down_query,
        down_value,
        up_query,
        up_value,
    )

    received = lax.all_to_all(send, "mp", 0, 0, tiled=True)
    summed = pl.pallas_call(
        sum_kernel,
        name="lowrank_sum",
        out_shape=jax.ShapeDtypeStruct(received.shape, BF16),
        in_specs=[VMEM],
        out_specs=VMEM,
        compiler_params=PARAMS,
    )(received)
    lowrank = lax.all_to_all(summed, "mp", 0, 0, tiled=True)

    feat_parts = pl.pallas_call(
        feature_kernel,
        name="partial_features",
        out_shape=jax.ShapeDtypeStruct((model_size, cands * KB, PB), BF16),
        in_specs=[SMEM] + [VMEM] * 9,
        out_specs=VMEM,
        compiler_params=PARAMS,
    )(
        kv_index,
        lowrank,
        hidden_in,
        query_grad,
        value_grad,
        block_rows,
        tile_rows,
        block_value.reshape(KVH, DH),
        tile_value.reshape(KVH, DH),
        tile_bank,
    )
    feat_all = lax.all_to_all(feat_parts, "mp", 0, 0, tiled=True)

    return pl.pallas_call(
        score_kernel,
        name="scores",
        out_shape=jax.ShapeDtypeStruct((cands, out_seeds), F32),
        in_specs=[VMEM, VMEM],
        out_specs=VMEM,
        compiler_params=PARAMS,
    )(feat_all, seeds_all)


def solution(mesh):
    return jax.shard_map(
        local,
        mesh=mesh,
        in_specs=(
            P("dp", None, "mp"),
            P("dp", None, "mp"),
            P("dp", None, None),
            P("dp", None, None),
            P("dp", None, "mp"),
            P("dp", None),
            P("mp", None),
            P(None, "mp"),
            P("mp", None),
            P(),
            P(None, "mp"),
            P(None, "mp"),
            P(),
            P(),
            P(),
            P("dp", "mp"),
        ),
        out_specs=P("dp", "mp"),
        check_vma=False,
    )
```

```python
import math

import jax
import jax.numpy as jnp
from jax import lax
from jax.experimental import pallas as pl
from jax.experimental.pallas import tpu as pltpu
from jax.sharding import PartitionSpec as P

H = 64
KVH = 8
DH = 128
R = 128
K = 8192
PB = 128
NT = 8
S = 512
KB = 64
EPS = 1e-06
LONGEST = 256
ROWS = 128
F32 = jnp.float32
BF16 = jnp.bfloat16


def dot_nn(a, b):
    return lax.dot_general(a, b, (((1,), (0,)), ((), ())), preferred_element_type=F32)


def dot_nt(a, b):
    return lax.dot_general(a, b, (((1,), (1,)), ((), ())), preferred_element_type=F32)


def attention_kernel(
    kv_index,
    hidden_ref,
    query_ref,
    grad_ref,
    key_ref,
    value_ref,
    segment_ref,
    down_query_ref,
    down_value_ref,
    up_query_ref,
    up_value_ref,
    send_ref,
    query_grad_ref,
    value_grad_ref,
    value_sum,
):
    cand = pl.program_id(0)
    parts = send_ref.shape[0]
    chunk = send_ref.shape[2]
    quarter = R // chunk
    heads = query_ref.shape[2] // DH
    score_scale = 1.0 / math.sqrt(DH)
    exp_scale = score_scale * math.log2(math.e)

    down = jnp.concatenate([down_query_ref[...].T, down_value_ref[...].T], axis=0)
    lowrank_in = dot_nt(down, hidden_ref[0])
    send_ref[0 : 2 * quarter, 0] = lowrank_in.astype(BF16).reshape(2 * quarter, chunk, S)

    segment_row = segment_ref[pl.ds(cand, 1), :].astype(F32)
    segment_col = jnp.broadcast_to(segment_row, (8, S)).T[:, 0:1]
    key = key_ref[0]
    value = value_ref[0]
    key_t = key.T
    value_sum[...] = jnp.zeros_like(value_sum)

    for block in range(S // ROWS):
        first = block * ROWS
        low = max(0, (first - LONGEST + 1) // ROWS * ROWS)
        high = first + ROWS
        width = high - low
        key_pos = low + lax.broadcasted_iota(jnp.int32, (width, ROWS), 0)
        row_pos = first + lax.broadcasted_iota(jnp.int32, (width, ROWS), 1)
        allowed = (key_pos <= row_pos) & (
            segment_col[low:high] == segment_row[:, first:high]
        )
        bias = jnp.where(allowed, 0.0, -1e30)
        for head in range(heads):
            cols = slice(head * DH, (head + 1) * DH)
            grad = grad_ref[0, first:high, cols]
            logits = dot_nt(key[low:high], query_ref[0, first:high, cols]) + bias
            row_top = jnp.max(logits, axis=0, keepdims=True)
            exp_terms = jnp.exp2((logits - row_top) * exp_scale)
            probs = exp_terms * (1.0 / jnp.sum(exp_terms, axis=0, keepdims=True))
            prob_grad = dot_nt(value[low:high], grad)
            row_delta = jnp.sum(probs * prob_grad, axis=0, keepdims=True)
            logit_grad = (probs * (prob_grad - row_delta)).astype(BF16)
            value_sum[low:high] += dot_nn(probs.astype(BF16), grad)
            query_grad = dot_nn(key_t[:, low:high], logit_grad) * score_scale
            query_grad_ref[0, cols, first:high] = query_grad.astype(BF16)

    value_grad = value_sum[...].astype(BF16)
    value_grad_ref[0] = value_grad
    back_query = dot_nn(up_query_ref[...], query_grad_ref[0])
    back_value = dot_nt(up_value_ref[...], value_grad)
    send_ref[2 * quarter : 3 * quarter, 0] = back_query.astype(BF16).reshape(quarter, chunk, S)
    send_ref[3 * quarter : parts, 0] = back_value.astype(BF16).reshape(quarter, chunk, S)


def sum_kernel(parts_ref, out_ref):
    total = jnp.sum(parts_ref[...].astype(F32), axis=0)
    out_ref[...] = jnp.broadcast_to(total.astype(BF16)[None], out_ref.shape)


def feature_kernel(
    kv_index,
    lowrank_ref,
    hidden_ref,
    query_grad_ref,
    value_grad_ref,
    block_ref,
    tile_ref,
    block_value_ref,
    tile_value_ref,
    bank_ref,
    out_ref,
):
    cands = hidden_ref.shape[0]
    kv = kv_index[0]
    pieces = [[], [], [], []]
    for cand in range(cands):
        lowrank = lowrank_ref[:, cand].reshape(4 * R, S)
        down = dot_nn(lowrank[2 * R :], hidden_ref[cand])
        pieces[0].append(down[:R])
        pieces[1].append(down[R:])
        pieces[2].append(dot_nt(lowrank[:R], query_grad_ref[cand]))
        pieces[3].append(dot_nn(lowrank[R : 2 * R], value_grad_ref[cand]))
    buckets = KB * NT
    sums = jnp.zeros((buckets, cands * R), F32)
    for kind in range(4):
        if kind < 3:
            ids = tile_ref[kind : kind + 1, :] * KB + block_ref[kind : kind + 1, :]
        else:
            ids = tile_value_ref[pl.ds(kv, 1), :] * KB + block_value_ref[pl.ds(kv, 1), :]
        rows = jnp.concatenate(pieces[kind], axis=0).astype(BF16)
        where = lax.broadcasted_iota(jnp.int32, (buckets, rows.shape[1]), 0)
        chosen = jnp.where(where == ids, 1.0, 0.0).astype(BF16)
        sums = sums + dot_nt(chosen, rows)
    wide = jnp.concatenate(
        [
            jnp.concatenate(
                [sums[t * KB : (t + 1) * KB, c * R : (c + 1) * R] for t in range(NT)], axis=1
            )
            for c in range(cands)
        ],
        axis=0,
    )
    high = wide.astype(BF16)
    low = (wide - high.astype(F32)).astype(BF16)
    bank = bank_ref[...].reshape(NT * R, PB)
    feats = dot_nn(high, bank) + dot_nn(low, bank)
    out_ref[...] = jnp.broadcast_to(feats.astype(BF16)[None], out_ref.shape)


def score_kernel(core_index, parts_ref, mine_ref, other_ref, out_ref):
    cands = out_ref.shape[0]
    seeds = mine_ref.shape[1]
    feats = jnp.sum(parts_ref[...].astype(F32), axis=0)
    per_part = mine_ref.shape[2] // PB
    totals = [[jnp.zeros((seeds, PB), F32) for _ in range(2)] for _ in range(cands)]
    for block in range(KB):
        at = block % per_part * PB
        for half, seeds_ref in enumerate((mine_ref, other_ref)):
            seed = seeds_ref[block // per_part, :, at : at + PB].astype(F32)
            for c in range(cands):
                row = c * KB + block
                totals[c][half] = totals[c][half] + feats[row : row + 1] * seed
    first_core = core_index[0] == 0
    for c in range(cands):
        mine = feats[c * KB : (c + 1) * KB]
        square = jnp.sum(jnp.sum(mine * mine, axis=0, keepdims=True), axis=1, keepdims=True)
        here, there = totals[c]
        ordered = jnp.concatenate(
            [jnp.where(first_core, here, there), jnp.where(first_core, there, here)], axis=0
        )
        numerator = jnp.sum(ordered.T, axis=0, keepdims=True)
        out_ref[c : c + 1, :] = numerator * lax.rsqrt(square / K + EPS) * K ** (-0.5)


VMEM = pl.BlockSpec(memory_space=pltpu.VMEM)
SMEM = pl.BlockSpec(memory_space=pltpu.SMEM)
PARAMS = pltpu.CompilerParams(vmem_limit_bytes=40 << 20)


def local(
    hidden_in,
    query_act,
    key_act,
    value_act,
    ctx_grad,
    segment_ids,
    down_query,
    up_query,
    down_value,
    up_value,
    block_rows,
    tile_rows,
    block_value,
    tile_value,
    tile_bank,
    seed_feats,
):
    model_index = lax.axis_index("mp")
    data_size = lax.axis_size("dp")
    model_size = lax.axis_size("mp")
    cands, seq_len, width = query_act.shape
    heads = width // DH
    kv = (model_index * heads // (H // KVH)).astype(jnp.int32)
    kv_index = kv.reshape(1)
    seeds_dev = seed_feats.shape[0]
    out_seeds = data_size * seeds_dev // model_size

    seed_moved = lax.ppermute(
        seed_feats,
        ("dp", "mp"),
        [
            (d * model_size + m, (m * 2 + d % 2) * model_size + d // 2)
            for d in range(data_size)
            for m in range(model_size)
        ],
    )
    chunk = 4 * R // model_size

    def per_cand(*shape):
        return pl.BlockSpec((1, *shape), lambda c, kv_ref: (c, 0, 0))

    def whole(*shape):
        return pl.BlockSpec(shape, lambda c, kv_ref: (0,) * len(shape))

    send, query_grad, value_grad = pl.pallas_call(
        attention_kernel,
        name="attention_backward",
        out_shape=(
            jax.ShapeDtypeStruct((model_size, cands, chunk, seq_len), BF16),
            jax.ShapeDtypeStruct((cands, width, seq_len), BF16),
            jax.ShapeDtypeStruct((cands, seq_len, DH), BF16),
        ),
        grid_spec=pltpu.PrefetchScalarGridSpec(
            num_scalar_prefetch=1,
            grid=(cands,),
            in_specs=[
                per_cand(seq_len, hidden_in.shape[2]),
                per_cand(seq_len, width),
                per_cand(seq_len, width),
                pl.BlockSpec((1, seq_len, DH), lambda c, kv_ref: (c, 0, kv_ref[0])),
                pl.BlockSpec((1, seq_len, DH), lambda c, kv_ref: (c, 0, kv_ref[0])),
                whole(cands, seq_len),
                whole(*down_query.shape),
                whole(*down_value.shape),
                whole(*up_query.shape),
                pl.BlockSpec((R, DH), lambda c, kv_ref: (0, kv_ref[0])),
            ],
            out_specs=[
                pl.BlockSpec((model_size, 1, chunk, seq_len), lambda c, kv_ref: (0, c, 0, 0)),
                per_cand(width, seq_len),
                per_cand(seq_len, DH),
            ],
            scratch_shapes=[pltpu.VMEM((seq_len, DH), F32)],
        ),
        compiler_params=pltpu.CompilerParams(vmem_limit_bytes=60 << 20),
        cost_estimate=pl.CostEstimate(
            flops=5_000_000_000, bytes_accessed=8_000_000, transcendentals=2_000_000
        ),
    )(
        kv_index,
        hidden_in,
        query_act,
        ctx_grad,
        key_act,
        value_act,
        segment_ids,
        down_query,
        down_value,
        up_query,
        up_value,
    )

    send, seed_moved = lax.optimization_barrier((send, seed_moved))
    received = lax.all_to_all(send, "mp", 0, 0, tiled=True)
    levels = data_size // 2
    seeds_core = lax.all_to_all(
        jnp.broadcast_to(seed_moved[None], (levels, *seed_moved.shape)),
        "dp",
        0,
        0,
        tiled=True,
        axis_index_groups=[[2 * z + core for z in range(levels)] for core in range(2)],
    )
    seeds_other = lax.ppermute(seeds_core, "dp", [(d, d ^ 1) for d in range(data_size)])
    core_index = (lax.axis_index("dp") % 2).astype(jnp.int32).reshape(1)
    summed = pl.pallas_call(
        sum_kernel,
        name="lowrank_sum",
        out_shape=jax.ShapeDtypeStruct(received.shape, BF16),
        in_specs=[VMEM],
        out_specs=VMEM,
        compiler_params=PARAMS,
    )(received)
    lowrank = lax.all_to_all(summed, "mp", 0, 0, tiled=True)

    feat_parts = pl.pallas_call(
        feature_kernel,
        name="partial_features",
        out_shape=jax.ShapeDtypeStruct((model_size, cands * KB, PB), BF16),
        in_specs=[SMEM] + [VMEM] * 9,
        out_specs=VMEM,
        compiler_params=PARAMS,
    )(
        kv_index,
        lowrank,
        hidden_in,
        query_grad,
        value_grad,
        block_rows,
        tile_rows,
        block_value.reshape(KVH, DH),
        tile_value.reshape(KVH, DH),
        tile_bank,
    )
    feat_all = lax.all_to_all(feat_parts, "mp", 0, 0, tiled=True)

    return pl.pallas_call(
        score_kernel,
        name="scores",
        out_shape=jax.ShapeDtypeStruct((cands, out_seeds), F32),
        in_specs=[SMEM, VMEM, VMEM, VMEM],
        out_specs=VMEM,
        compiler_params=PARAMS,
    )(core_index, feat_all, seeds_core, seeds_other)


def solution(mesh):
    return jax.shard_map(
        local,
        mesh=mesh,
        in_specs=(
            P("dp", None, "mp"),
            P("dp", None, "mp"),
            P("dp", None, None),
            P("dp", None, None),
            P("dp", None, "mp"),
            P("dp", None),
            P("mp", None),
            P(None, "mp"),
            P("mp", None),
            P(),
            P(None, "mp"),
            P(None, "mp"),
            P(),
            P(),
            P(),
            P("dp", "mp"),
        ),
        out_specs=P("dp", "mp"),
        check_vma=False,
    )
```

```python
import math

import jax
import jax.numpy as jnp
from jax import lax
from jax.experimental import pallas as pl
from jax.experimental.pallas import tpu as pltpu
from jax.sharding import PartitionSpec as P

H = 64
KVH = 8
DH = 128
R = 128
K = 8192
PB = 128
NT = 8
S = 512
KB = 64
EPS = 1e-06
LONGEST = 256
ROWS = 128
F32 = jnp.float32
BF16 = jnp.bfloat16


def dot_nn(a, b):
    return lax.dot_general(a, b, (((1,), (0,)), ((), ())), preferred_element_type=F32)


def dot_nt(a, b):
    return lax.dot_general(a, b, (((1,), (1,)), ((), ())), preferred_element_type=F32)


def attention_kernel(
    kv_index,
    hidden_ref,
    query_ref,
    grad_ref,
    key_ref,
    value_ref,
    segment_ref,
    down_query_ref,
    down_value_ref,
    up_query_ref,
    up_value_ref,
    send_ref,
    query_grad_ref,
    value_grad_ref,
    value_sum,
):
    cand = pl.program_id(0)
    parts = send_ref.shape[0]
    chunk = send_ref.shape[2]
    quarter = R // chunk
    heads = query_ref.shape[2] // DH
    score_scale = 1.0 / math.sqrt(DH)
    exp_scale = score_scale * math.log2(math.e)

    down = jnp.concatenate([down_query_ref[...].T, down_value_ref[...].T], axis=0)
    lowrank_in = dot_nt(down, hidden_ref[0])
    send_ref[0 : 2 * quarter, 0] = lowrank_in.astype(BF16).reshape(2 * quarter, chunk, S)

    segment_row = segment_ref[pl.ds(cand, 1), :].astype(F32)
    segment_col = jnp.broadcast_to(segment_row, (8, S)).T[:, 0:1]
    key = key_ref[0]
    value = value_ref[0]
    key_t = key.T
    value_sum[...] = jnp.zeros_like(value_sum)

    for block in range(S // ROWS):
        first = block * ROWS
        low = max(0, (first - LONGEST + 1) // ROWS * ROWS)
        high = first + ROWS
        width = high - low
        key_pos = low + lax.broadcasted_iota(jnp.int32, (width, ROWS), 0)
        row_pos = first + lax.broadcasted_iota(jnp.int32, (width, ROWS), 1)
        allowed = (key_pos <= row_pos) & (
            segment_col[low:high] == segment_row[:, first:high]
        )
        bias = jnp.where(allowed, 0.0, -1e30)
        for head in range(heads):
            cols = slice(head * DH, (head + 1) * DH)
            grad = grad_ref[0, first:high, cols]
            logits = dot_nt(key[low:high], query_ref[0, first:high, cols]) + bias
            row_top = jnp.max(logits, axis=0, keepdims=True)
            exp_terms = jnp.exp2((logits - row_top) * exp_scale)
            probs = exp_terms * (1.0 / jnp.sum(exp_terms, axis=0, keepdims=True))
            prob_grad = dot_nt(value[low:high], grad)
            row_delta = jnp.sum(probs * prob_grad, axis=0, keepdims=True)
            logit_grad = (probs * (prob_grad - row_delta)).astype(BF16)
            value_sum[low:high] += dot_nn(probs.astype(BF16), grad)
            query_grad = dot_nn(key_t[:, low:high], logit_grad) * score_scale
            query_grad_ref[0, cols, first:high] = query_grad.astype(BF16)

    value_grad = value_sum[...].astype(BF16)
    value_grad_ref[0] = value_grad
    back_query = dot_nn(up_query_ref[...], query_grad_ref[0])
    back_value = dot_nt(up_value_ref[...], value_grad)
    send_ref[2 * quarter : 3 * quarter, 0] = back_query.astype(BF16).reshape(quarter, chunk, S)
    send_ref[3 * quarter : parts, 0] = back_value.astype(BF16).reshape(quarter, chunk, S)


def sum_kernel(parts_ref, out_ref):
    total = jnp.sum(parts_ref[...].astype(F32), axis=0)
    out_ref[...] = jnp.broadcast_to(total.astype(BF16)[None], out_ref.shape)


def feature_kernel(
    kv_index,
    lowrank_ref,
    hidden_ref,
    query_grad_ref,
    value_grad_ref,
    block_ref,
    tile_ref,
    block_value_ref,
    tile_value_ref,
    bank_ref,
    out_ref,
):
    cands = hidden_ref.shape[0]
    kv = kv_index[0]
    pieces = [[], [], [], []]
    for cand in range(cands):
        lowrank = lowrank_ref[:, cand].reshape(4 * R, S)
        down = dot_nn(lowrank[2 * R :], hidden_ref[cand])
        pieces[0].append(down[:R])
        pieces[1].append(down[R:])
        pieces[2].append(dot_nt(lowrank[:R], query_grad_ref[cand]))
        pieces[3].append(dot_nn(lowrank[R : 2 * R], value_grad_ref[cand]))
    buckets = KB * NT
    sums = jnp.zeros((buckets, cands * R), F32)
    for kind in range(4):
        if kind < 3:
            ids = tile_ref[kind : kind + 1, :] * KB + block_ref[kind : kind + 1, :]
        else:
            ids = tile_value_ref[pl.ds(kv, 1), :] * KB + block_value_ref[pl.ds(kv, 1), :]
        rows = jnp.concatenate(pieces[kind], axis=0).astype(BF16)
        where = lax.broadcasted_iota(jnp.int32, (buckets, rows.shape[1]), 0)
        chosen = jnp.where(where == ids, 1.0, 0.0).astype(BF16)
        sums = sums + dot_nt(chosen, rows)
    wide = jnp.concatenate(
        [
            jnp.concatenate(
                [sums[t * KB : (t + 1) * KB, c * R : (c + 1) * R] for t in range(NT)], axis=1
            )
            for c in range(cands)
        ],
        axis=0,
    )
    high = wide.astype(BF16)
    low = (wide - high.astype(F32)).astype(BF16)
    bank = bank_ref[...].reshape(NT * R, PB)
    feats = dot_nn(high, bank) + dot_nn(low, bank)
    out_ref[...] = jnp.broadcast_to(feats.astype(BF16)[None], out_ref.shape)


def score_kernel(place, parts_ref, *refs):
    mine_refs, other_refs, (out_ref, feats_ref) = refs[:4], refs[4:8], refs[8:]
    cands = out_ref.shape[0]
    fours, seeds, depth = mine_refs[0].shape
    levels = 4 * fours
    per_part = depth // PB
    feats_ref[...] = jnp.sum(parts_ref[...].astype(F32), axis=0)
    totals = [[jnp.zeros((seeds, PB), F32) for _ in range(2)] for _ in range(cands)]
    for at in range(levels):
        source = (place[1] + (2 * levels - NEAR[at // 4] - 4 * (at % 4))) % levels
        for part in range(per_part):
            feat = [
                feats_ref[pl.ds(c * KB + source * per_part + part, 1), :] for c in range(cands)
            ]
            for half, seeds_ref in enumerate((mine_refs[at // 4], other_refs[at // 4])):
                seed = seeds_ref[at % 4, :, part * PB : (part + 1) * PB].astype(F32)
                for c in range(cands):
                    totals[c][half] = totals[c][half] + feat[c] * seed
    first_core = place[0] == 0
    for c in range(cands):
        mine = feats_ref[c * KB : (c + 1) * KB]
        square = jnp.sum(jnp.sum(mine * mine, axis=0, keepdims=True), axis=1, keepdims=True)
        here, there = totals[c]
        ordered = jnp.concatenate(
            [jnp.where(first_core, here, there), jnp.where(first_core, there, here)], axis=0
        )
        numerator = jnp.sum(ordered.T, axis=0, keepdims=True)
        out_ref[c : c + 1, :] = numerator * lax.rsqrt(square / K + EPS) * K ** (-0.5)


VMEM = pl.BlockSpec(memory_space=pltpu.VMEM)
SMEM = pl.BlockSpec(memory_space=pltpu.SMEM)
PARAMS = pltpu.CompilerParams(vmem_limit_bytes=40 << 20)


def local(
    hidden_in,
    query_act,
    key_act,
    value_act,
    ctx_grad,
    segment_ids,
    down_query,
    up_query,
    down_value,
    up_value,
    block_rows,
    tile_rows,
    block_value,
    tile_value,
    tile_bank,
    seed_feats,
):
    model_index = lax.axis_index("mp")
    data_size = lax.axis_size("dp")
    model_size = lax.axis_size("mp")
    cands, seq_len, width = query_act.shape
    heads = width // DH
    kv = (model_index * heads // (H // KVH)).astype(jnp.int32)
    kv_index = kv.reshape(1)
    seeds_dev = seed_feats.shape[0]
    out_seeds = data_size * seeds_dev // model_size

    seed_moved = lax.ppermute(
        seed_feats,
        ("dp", "mp"),
        [
            (d * model_size + m, (m * 2 + d % 2) * model_size + d // 2)
            for d in range(data_size)
            for m in range(model_size)
        ],
    )
    chunk = 4 * R // model_size

    def per_cand(*shape):
        return pl.BlockSpec((1, *shape), lambda c, kv_ref: (c, 0, 0))

    def whole(*shape):
        return pl.BlockSpec(shape, lambda c, kv_ref: (0,) * len(shape))

    send, query_grad, value_grad = pl.pallas_call(
        attention_kernel,
        name="attention_backward",
        out_shape=(
            jax.ShapeDtypeStruct((model_size, cands, chunk, seq_len), BF16),
            jax.ShapeDtypeStruct((cands, width, seq_len), BF16),
            jax.ShapeDtypeStruct((cands, seq_len, DH), BF16),
        ),
        grid_spec=pltpu.PrefetchScalarGridSpec(
            num_scalar_prefetch=1,
            grid=(cands,),
            in_specs=[
                per_cand(seq_len, hidden_in.shape[2]),
                per_cand(seq_len, width),
                per_cand(seq_len, width),
                pl.BlockSpec((1, seq_len, DH), lambda c, kv_ref: (c, 0, kv_ref[0])),
                pl.BlockSpec((1, seq_len, DH), lambda c, kv_ref: (c, 0, kv_ref[0])),
                whole(cands, seq_len),
                whole(*down_query.shape),
                whole(*down_value.shape),
                whole(*up_query.shape),
                pl.BlockSpec((R, DH), lambda c, kv_ref: (0, kv_ref[0])),
            ],
            out_specs=[
                pl.BlockSpec((model_size, 1, chunk, seq_len), lambda c, kv_ref: (0, c, 0, 0)),
                per_cand(width, seq_len),
                per_cand(seq_len, DH),
            ],
            scratch_shapes=[pltpu.VMEM((seq_len, DH), F32)],
        ),
        compiler_params=pltpu.CompilerParams(vmem_limit_bytes=60 << 20),
        cost_estimate=pl.CostEstimate(
            flops=5_000_000_000, bytes_accessed=8_000_000, transcendentals=2_000_000
        ),
    )(
        kv_index,
        hidden_in,
        query_act,
        ctx_grad,
        key_act,
        value_act,
        segment_ids,
        down_query,
        down_value,
        up_query,
        up_value,
    )

    send, seed_moved = lax.optimization_barrier((send, seed_moved))
    received = lax.all_to_all(send, "mp", 0, 0, tiled=True)
    far = [seed_moved] + [move_z(seed_moved, 4 * j, data_size) for j in range(1, 4)]
    received, *far = lax.optimization_barrier((received, *far))
    summed = pl.pallas_call(
        sum_kernel,
        name="lowrank_sum",
        out_shape=jax.ShapeDtypeStruct(received.shape, BF16),
        in_specs=[VMEM],
        out_specs=VMEM,
        compiler_params=PARAMS,
    )(received)
    lowrank = lax.all_to_all(summed, "mp", 0, 0, tiled=True)
    four = jnp.stack(far)
    near = [four] + [move_z(four, e, data_size) for e in NEAR[1:]]
    lowrank, *near = lax.optimization_barrier((lowrank, *near))

    feat_parts = pl.pallas_call(
        feature_kernel,
        name="partial_features",
        out_shape=jax.ShapeDtypeStruct((model_size, cands * KB, PB), BF16),
        in_specs=[SMEM] + [VMEM] * 9,
        out_specs=VMEM,
        compiler_params=PARAMS,
    )(
        kv_index,
        lowrank,
        hidden_in,
        query_grad,
        value_grad,
        block_rows,
        tile_rows,
        block_value.reshape(KVH, DH),
        tile_value.reshape(KVH, DH),
        tile_bank,
    )
    feat_parts, *near = lax.optimization_barrier((feat_parts, *near))
    feat_all = lax.all_to_all(feat_parts, "mp", 0, 0, tiled=True)
    swap = [(d, d ^ 1) for d in range(data_size)]
    other = [lax.ppermute(four, "dp", swap) for four in near]
    place = jnp.stack([lax.axis_index("dp") % 2, lax.axis_index("dp") // 2]).astype(jnp.int32)

    return pl.pallas_call(
        score_kernel,
        name="scores",
        out_shape=jax.ShapeDtypeStruct((cands, out_seeds), F32),
        in_specs=[SMEM] + [VMEM] * 9,
        out_specs=VMEM,
        scratch_shapes=[pltpu.VMEM((cands * KB, PB), F32)],
        compiler_params=PARAMS,
    )(place, feat_all, *near, *other)


NEAR = (0, 1, 2, -1)


def move_z(block, steps, data_size):
    return lax.ppermute(
        block, "dp", [(d, (d + 2 * steps) % data_size) for d in range(data_size)]
    )


def solution(mesh):
    return jax.shard_map(
        local,
        mesh=mesh,
        in_specs=(
            P("dp", None, "mp"),
            P("dp", None, "mp"),
            P("dp", None, None),
            P("dp", None, None),
            P("dp", None, "mp"),
            P("dp", None),
            P("mp", None),
            P(None, "mp"),
            P("mp", None),
            P(),
            P(None, "mp"),
            P(None, "mp"),
            P(),
            P(),
            P(),
            P("dp", "mp"),
        ),
        out_specs=P("dp", "mp"),
        check_vma=False,
    )
```

```python
import math

import jax
import jax.numpy as jnp
from jax import lax
from jax.experimental import pallas as pl
from jax.experimental.pallas import tpu as pltpu
from jax.sharding import PartitionSpec as P

H = 64
KVH = 8
DH = 128
R = 128
K = 8192
PB = 128
NT = 8
S = 512
KB = 64
EPS = 1e-06
LONGEST = 256
ROWS = 128
F32 = jnp.float32
BF16 = jnp.bfloat16


def dot_nn(a, b):
    return lax.dot_general(a, b, (((1,), (0,)), ((), ())), preferred_element_type=F32)


def dot_nt(a, b):
    return lax.dot_general(a, b, (((1,), (1,)), ((), ())), preferred_element_type=F32)


def attention_kernel(
    kv_index,
    hidden_ref,
    query_ref,
    grad_ref,
    key_ref,
    value_ref,
    segment_ref,
    down_query_ref,
    down_value_ref,
    up_query_ref,
    up_value_ref,
    send_ref,
    query_grad_ref,
    value_grad_ref,
    value_sum,
):
    cand = pl.program_id(0)
    parts = send_ref.shape[0]
    chunk = send_ref.shape[2]
    quarter = R // chunk
    heads = query_ref.shape[2] // DH
    score_scale = 1.0 / math.sqrt(DH)
    exp_scale = score_scale * math.log2(math.e)

    down = jnp.concatenate([down_query_ref[...].T, down_value_ref[...].T], axis=0)
    lowrank_in = dot_nt(down, hidden_ref[0])
    send_ref[0 : 2 * quarter, 0] = lowrank_in.astype(BF16).reshape(2 * quarter, chunk, S)

    segment_row = segment_ref[pl.ds(cand, 1), :].astype(F32)
    segment_col = jnp.broadcast_to(segment_row, (8, S)).T[:, 0:1]
    key = key_ref[0]
    value = value_ref[0]
    key_t = key.T
    value_sum[...] = jnp.zeros_like(value_sum)

    for block in range(S // ROWS):
        first = block * ROWS
        low = max(0, (first - LONGEST + 1) // ROWS * ROWS)
        high = first + ROWS
        width = high - low
        key_pos = low + lax.broadcasted_iota(jnp.int32, (width, ROWS), 0)
        row_pos = first + lax.broadcasted_iota(jnp.int32, (width, ROWS), 1)
        allowed = (key_pos <= row_pos) & (
            segment_col[low:high] == segment_row[:, first:high]
        )
        bias = jnp.where(allowed, 0.0, -1e30)
        for head in range(heads):
            cols = slice(head * DH, (head + 1) * DH)
            grad = grad_ref[0, first:high, cols]
            logits = dot_nt(key[low:high], query_ref[0, first:high, cols]) + bias
            row_top = jnp.max(logits, axis=0, keepdims=True)
            exp_terms = jnp.exp2((logits - row_top) * exp_scale)
            probs = exp_terms * (1.0 / jnp.sum(exp_terms, axis=0, keepdims=True))
            prob_grad = dot_nt(value[low:high], grad)
            row_delta = jnp.sum(probs * prob_grad, axis=0, keepdims=True)
            logit_grad = (probs * (prob_grad - row_delta)).astype(BF16)
            value_sum[low:high] += dot_nn(probs.astype(BF16), grad)
            query_grad = dot_nn(key_t[:, low:high], logit_grad) * score_scale
            query_grad_ref[0, cols, first:high] = query_grad.astype(BF16)

    value_grad = value_sum[...].astype(BF16)
    value_grad_ref[0] = value_grad
    back_query = dot_nn(up_query_ref[...], query_grad_ref[0])
    back_value = dot_nt(up_value_ref[...], value_grad)
    send_ref[2 * quarter : 3 * quarter, 0] = back_query.astype(BF16).reshape(quarter, chunk, S)
    send_ref[3 * quarter : parts, 0] = back_value.astype(BF16).reshape(quarter, chunk, S)


def sum_kernel(parts_ref, out_ref):
    total = jnp.sum(parts_ref[...].astype(F32), axis=0)
    out_ref[...] = jnp.broadcast_to(total.astype(BF16)[None], out_ref.shape)


def feature_kernel(
    kv_index,
    lowrank_ref,
    hidden_ref,
    query_grad_ref,
    value_grad_ref,
    block_ref,
    tile_ref,
    block_value_ref,
    tile_value_ref,
    bank_ref,
    out_ref,
):
    cands = hidden_ref.shape[0]
    kv = kv_index[0]
    pieces = [[], [], [], []]
    for cand in range(cands):
        lowrank = lowrank_ref[:, cand].reshape(4 * R, S)
        down = dot_nn(lowrank[2 * R :], hidden_ref[cand])
        pieces[0].append(down[:R])
        pieces[1].append(down[R:])
        pieces[2].append(dot_nt(lowrank[:R], query_grad_ref[cand]))
        pieces[3].append(dot_nn(lowrank[R : 2 * R], value_grad_ref[cand]))
    buckets = KB * NT
    sums = jnp.zeros((buckets, cands * R), F32)
    for kind in range(4):
        if kind < 3:
            ids = tile_ref[kind : kind + 1, :] * KB + block_ref[kind : kind + 1, :]
        else:
            ids = tile_value_ref[pl.ds(kv, 1), :] * KB + block_value_ref[pl.ds(kv, 1), :]
        rows = jnp.concatenate(pieces[kind], axis=0).astype(BF16)
        where = lax.broadcasted_iota(jnp.int32, (buckets, rows.shape[1]), 0)
        chosen = jnp.where(where == ids, 1.0, 0.0).astype(BF16)
        sums = sums + dot_nt(chosen, rows)
    wide = jnp.concatenate(
        [
            jnp.concatenate(
                [sums[t * KB : (t + 1) * KB, c * R : (c + 1) * R] for t in range(NT)], axis=1
            )
            for c in range(cands)
        ],
        axis=0,
    )
    high = wide.astype(BF16)
    low = (wide - high.astype(F32)).astype(BF16)
    bank = bank_ref[...].reshape(NT * R, PB)
    feats = dot_nn(high, bank) + dot_nn(low, bank)
    out_ref[...] = jnp.broadcast_to(feats.astype(BF16)[None], out_ref.shape)


def score_kernel(parts_ref, seeds_ref, out_ref):
    cands = out_ref.shape[0]
    seeds = out_ref.shape[1]
    feats = jnp.sum(parts_ref[...].astype(F32), axis=0)
    per_part = seeds_ref.shape[2] // PB
    totals = [jnp.zeros((seeds, PB), F32) for _ in range(cands)]
    for block in range(KB):
        at = block % per_part * PB
        seed = seeds_ref[block // per_part, :, at : at + PB].astype(F32)
        for c in range(cands):
            row = c * KB + block
            totals[c] = totals[c] + feats[row : row + 1] * seed
    for c in range(cands):
        mine = feats[c * KB : (c + 1) * KB]
        square = jnp.sum(jnp.sum(mine * mine, axis=0, keepdims=True), axis=1, keepdims=True)
        numerator = jnp.sum(totals[c].T, axis=0, keepdims=True)
        out_ref[c : c + 1, :] = numerator * lax.rsqrt(square / K + EPS) * K ** (-0.5)


VMEM = pl.BlockSpec(memory_space=pltpu.VMEM)
SMEM = pl.BlockSpec(memory_space=pltpu.SMEM)
PARAMS = pltpu.CompilerParams(vmem_limit_bytes=40 << 20)


def local(
    hidden_in,
    query_act,
    key_act,
    value_act,
    ctx_grad,
    segment_ids,
    down_query,
    up_query,
    down_value,
    up_value,
    block_rows,
    tile_rows,
    block_value,
    tile_value,
    tile_bank,
    seed_feats,
):
    model_index = lax.axis_index("mp")
    data_size = lax.axis_size("dp")
    model_size = lax.axis_size("mp")
    cands, seq_len, width = query_act.shape
    heads = width // DH
    kv = (model_index * heads // (H // KVH)).astype(jnp.int32)
    kv_index = kv.reshape(1)
    seeds_dev = seed_feats.shape[0]
    out_seeds = data_size * seeds_dev // model_size

    seed_moved = lax.ppermute(
        seed_feats,
        ("dp", "mp"),
        [
            (d * model_size + m, (m * 2 + d % 2) * model_size + d // 2)
            for d in range(data_size)
            for m in range(model_size)
        ],
    )
    chunk = 4 * R // model_size

    def per_cand(*shape):
        return pl.BlockSpec((1, *shape), lambda c, kv_ref: (c, 0, 0))

    def whole(*shape):
        return pl.BlockSpec(shape, lambda c, kv_ref: (0,) * len(shape))

    send, query_grad, value_grad = pl.pallas_call(
        attention_kernel,
        name="attention_backward",
        out_shape=(
            jax.ShapeDtypeStruct((model_size, cands, chunk, seq_len), BF16),
            jax.ShapeDtypeStruct((cands, width, seq_len), BF16),
            jax.ShapeDtypeStruct((cands, seq_len, DH), BF16),
        ),
        grid_spec=pltpu.PrefetchScalarGridSpec(
            num_scalar_prefetch=1,
            grid=(cands,),
            in_specs=[
                per_cand(seq_len, hidden_in.shape[2]),
                per_cand(seq_len, width),
                per_cand(seq_len, width),
                pl.BlockSpec((1, seq_len, DH), lambda c, kv_ref: (c, 0, kv_ref[0])),
                pl.BlockSpec((1, seq_len, DH), lambda c, kv_ref: (c, 0, kv_ref[0])),
                whole(cands, seq_len),
                whole(*down_query.shape),
                whole(*down_value.shape),
                whole(*up_query.shape),
                pl.BlockSpec((R, DH), lambda c, kv_ref: (0, kv_ref[0])),
            ],
            out_specs=[
                pl.BlockSpec((model_size, 1, chunk, seq_len), lambda c, kv_ref: (0, c, 0, 0)),
                per_cand(width, seq_len),
                per_cand(seq_len, DH),
            ],
            scratch_shapes=[pltpu.VMEM((seq_len, DH), F32)],
        ),
        compiler_params=pltpu.CompilerParams(vmem_limit_bytes=60 << 20),
        cost_estimate=pl.CostEstimate(
            flops=5_000_000_000, bytes_accessed=8_000_000, transcendentals=2_000_000
        ),
    )(
        kv_index,
        hidden_in,
        query_act,
        ctx_grad,
        key_act,
        value_act,
        segment_ids,
        down_query,
        down_value,
        up_query,
        up_value,
    )

    send, seed_moved = lax.optimization_barrier((send, seed_moved))
    pairs = data_size // 4
    seed_pair = lax.all_gather(
        seed_moved,
        "dp",
        axis=0,
        tiled=True,
        axis_index_groups=[[4 * i + j for j in range(4)] for i in range(pairs)],
    )
    send, seed_pair = lax.optimization_barrier((send, seed_pair))
    seeds_all = lax.all_gather(
        seed_pair,
        "dp",
        axis=0,
        tiled=True,
        axis_index_groups=[[4 * i + j for i in range(pairs)] for j in range(4)],
    ).reshape(model_size, out_seeds, seed_feats.shape[1])
    received = lax.all_to_all(send, "mp", 0, 0, tiled=True)
    summed = pl.pallas_call(
        sum_kernel,
        name="lowrank_sum",
        out_shape=jax.ShapeDtypeStruct(received.shape, BF16),
        in_specs=[VMEM],
        out_specs=VMEM,
        compiler_params=PARAMS,
    )(received)
    lowrank = lax.all_to_all(summed, "mp", 0, 0, tiled=True)

    feat_parts = pl.pallas_call(
        feature_kernel,
        name="partial_features",
        out_shape=jax.ShapeDtypeStruct((model_size, cands * KB, PB), BF16),
        in_specs=[SMEM] + [VMEM] * 9,
        out_specs=VMEM,
        compiler_params=PARAMS,
    )(
        kv_index,
        lowrank,
        hidden_in,
        query_grad,
        value_grad,
        block_rows,
        tile_rows,
        block_value.reshape(KVH, DH),
        tile_value.reshape(KVH, DH),
        tile_bank,
    )
    feat_all = lax.all_to_all(feat_parts, "mp", 0, 0, tiled=True)

    return pl.pallas_call(
        score_kernel,
        name="scores",
        out_shape=jax.ShapeDtypeStruct((cands, out_seeds), F32),
        in_specs=[VMEM, VMEM],
        out_specs=VMEM,
        compiler_params=PARAMS,
    )(feat_all, seeds_all)


def solution(mesh):
    return jax.shard_map(
        local,
        mesh=mesh,
        in_specs=(
            P("dp", None, "mp"),
            P("dp", None, "mp"),
            P("dp", None, None),
            P("dp", None, None),
            P("dp", None, "mp"),
            P("dp", None),
            P("mp", None),
            P(None, "mp"),
            P("mp", None),
            P(),
            P(None, "mp"),
            P(None, "mp"),
            P(),
            P(),
            P(),
            P("dp", "mp"),
        ),
        out_specs=P("dp", "mp"),
        check_vma=False,
    )
```

```python
import math

import jax
import jax.numpy as jnp
from jax import lax
from jax.experimental import pallas as pl
from jax.experimental.pallas import tpu as pltpu
from jax.sharding import PartitionSpec as P

H = 64
KVH = 8
DH = 128
R = 128
K = 8192
PB = 128
NT = 8
S = 512
KB = 64
EPS = 1e-06
LONGEST = 256
ROWS = 128
F32 = jnp.float32
BF16 = jnp.bfloat16


def dot_nn(a, b):
    return lax.dot_general(a, b, (((1,), (0,)), ((), ())), preferred_element_type=F32)


def dot_nt(a, b):
    return lax.dot_general(a, b, (((1,), (1,)), ((), ())), preferred_element_type=F32)


def attention_kernel(
    kv_index,
    hidden_ref,
    query_ref,
    grad_ref,
    key_ref,
    value_ref,
    segment_ref,
    down_query_ref,
    down_value_ref,
    up_query_ref,
    up_value_ref,
    send_ref,
    query_grad_ref,
    value_grad_ref,
    value_sum,
):
    cand = pl.program_id(0)
    parts = send_ref.shape[0]
    chunk = send_ref.shape[2]
    quarter = R // chunk
    heads = query_ref.shape[2] // DH
    score_scale = 1.0 / math.sqrt(DH)
    exp_scale = score_scale * math.log2(math.e)

    down = jnp.concatenate([down_query_ref[...].T, down_value_ref[...].T], axis=0)
    lowrank_in = dot_nt(down, hidden_ref[0])
    send_ref[0 : 2 * quarter, 0] = lowrank_in.astype(BF16).reshape(2 * quarter, chunk, S)

    segment_row = segment_ref[pl.ds(cand, 1), :].astype(F32)
    segment_col = jnp.broadcast_to(segment_row, (8, S)).T[:, 0:1]
    key = key_ref[0]
    value = value_ref[0]
    key_t = key.T
    value_sum[...] = jnp.zeros_like(value_sum)

    for block in range(S // ROWS):
        first = block * ROWS
        low = max(0, (first - LONGEST + 1) // ROWS * ROWS)
        high = first + ROWS
        width = high - low
        key_pos = low + lax.broadcasted_iota(jnp.int32, (width, ROWS), 0)
        row_pos = first + lax.broadcasted_iota(jnp.int32, (width, ROWS), 1)
        allowed = (key_pos <= row_pos) & (
            segment_col[low:high] == segment_row[:, first:high]
        )
        bias = jnp.where(allowed, 0.0, -1e30)
        for head in range(heads):
            cols = slice(head * DH, (head + 1) * DH)
            grad = grad_ref[0, first:high, cols]
            logits = dot_nt(key[low:high], query_ref[0, first:high, cols]) + bias
            row_top = jnp.max(logits, axis=0, keepdims=True)
            exp_terms = jnp.exp2((logits - row_top) * exp_scale)
            probs = exp_terms * (1.0 / jnp.sum(exp_terms, axis=0, keepdims=True))
            prob_grad = dot_nt(value[low:high], grad)
            row_delta = jnp.sum(probs * prob_grad, axis=0, keepdims=True)
            logit_grad = (probs * (prob_grad - row_delta)).astype(BF16)
            value_sum[low:high] += dot_nn(probs.astype(BF16), grad)
            query_grad = dot_nn(key_t[:, low:high], logit_grad) * score_scale
            query_grad_ref[0, cols, first:high] = query_grad.astype(BF16)

    value_grad = value_sum[...].astype(BF16)
    value_grad_ref[0] = value_grad
    back_query = dot_nn(up_query_ref[...], query_grad_ref[0])
    back_value = dot_nt(up_value_ref[...], value_grad)
    send_ref[2 * quarter : 3 * quarter, 0] = back_query.astype(BF16).reshape(quarter, chunk, S)
    send_ref[3 * quarter : parts, 0] = back_value.astype(BF16).reshape(quarter, chunk, S)


def sum_kernel(parts_ref, out_ref):
    total = jnp.sum(parts_ref[...].astype(F32), axis=0)
    out_ref[...] = jnp.broadcast_to(total.astype(BF16)[None], out_ref.shape)


def feature_kernel(
    kv_index,
    lowrank_ref,
    hidden_ref,
    query_grad_ref,
    value_grad_ref,
    block_ref,
    tile_ref,
    block_value_ref,
    tile_value_ref,
    bank_ref,
    out_ref,
):
    cands = hidden_ref.shape[0]
    kv = kv_index[0]
    pieces = [[], [], [], []]
    for cand in range(cands):
        lowrank = lowrank_ref[:, cand].reshape(4 * R, S)
        down = dot_nn(lowrank[2 * R :], hidden_ref[cand])
        pieces[0].append(down[:R])
        pieces[1].append(down[R:])
        pieces[2].append(dot_nt(lowrank[:R], query_grad_ref[cand]))
        pieces[3].append(dot_nn(lowrank[R : 2 * R], value_grad_ref[cand]))
    buckets = KB * NT
    sums = jnp.zeros((buckets, cands * R), F32)
    for kind in range(4):
        if kind < 3:
            ids = tile_ref[kind : kind + 1, :] * KB + block_ref[kind : kind + 1, :]
        else:
            ids = tile_value_ref[pl.ds(kv, 1), :] * KB + block_value_ref[pl.ds(kv, 1), :]
        rows = jnp.concatenate(pieces[kind], axis=0).astype(BF16)
        where = lax.broadcasted_iota(jnp.int32, (buckets, rows.shape[1]), 0)
        chosen = jnp.where(where == ids, 1.0, 0.0).astype(BF16)
        sums = sums + dot_nt(chosen, rows)
    wide = jnp.concatenate(
        [
            jnp.concatenate(
                [sums[t * KB : (t + 1) * KB, c * R : (c + 1) * R] for t in range(NT)], axis=1
            )
            for c in range(cands)
        ],
        axis=0,
    )
    high = wide.astype(BF16)
    low = (wide - high.astype(F32)).astype(BF16)
    bank = bank_ref[...].reshape(NT * R, PB)
    feats = dot_nn(high, bank) + dot_nn(low, bank)
    out_ref[...] = jnp.broadcast_to(feats.astype(BF16)[None], out_ref.shape)


def score_kernel(place, parts_ref, *refs):
    mine_refs, other_refs, (out_ref, feats_ref) = refs[:2], refs[2:4], refs[4:]
    cands = out_ref.shape[0]
    eights, seeds, depth = mine_refs[0].shape
    per_part = depth // PB
    feats_ref[...] = jnp.sum(parts_ref[...].astype(F32), axis=0)
    totals = [[jnp.zeros((seeds, PB), F32) for _ in range(2)] for _ in range(cands)]
    for at in range(2 * eights):
        source = place[1] ^ (at % 2 * 8 + at // 2 % 2 * 4 + at // 4 % 2 * 2 + at // 8)
        for part in range(per_part):
            feat = [
                feats_ref[pl.ds(c * KB + source * per_part + part, 1), :] for c in range(cands)
            ]
            for half, seeds_ref in enumerate((mine_refs[at // eights], other_refs[at // eights])):
                seed = seeds_ref[at % eights, :, part * PB : (part + 1) * PB].astype(F32)
                for c in range(cands):
                    totals[c][half] = totals[c][half] + feat[c] * seed
    first_core = place[0] == 0
    for c in range(cands):
        mine = feats_ref[c * KB : (c + 1) * KB]
        square = jnp.sum(jnp.sum(mine * mine, axis=0, keepdims=True), axis=1, keepdims=True)
        here, there = totals[c]
        ordered = jnp.concatenate(
            [jnp.where(first_core, here, there), jnp.where(first_core, there, here)], axis=0
        )
        numerator = jnp.sum(ordered.T, axis=0, keepdims=True)
        out_ref[c : c + 1, :] = numerator * lax.rsqrt(square / K + EPS) * K ** (-0.5)


VMEM = pl.BlockSpec(memory_space=pltpu.VMEM)
SMEM = pl.BlockSpec(memory_space=pltpu.SMEM)
PARAMS = pltpu.CompilerParams(vmem_limit_bytes=40 << 20)


def local(
    hidden_in,
    query_act,
    key_act,
    value_act,
    ctx_grad,
    segment_ids,
    down_query,
    up_query,
    down_value,
    up_value,
    block_rows,
    tile_rows,
    block_value,
    tile_value,
    tile_bank,
    seed_feats,
):
    model_index = lax.axis_index("mp")
    data_size = lax.axis_size("dp")
    model_size = lax.axis_size("mp")
    cands, seq_len, width = query_act.shape
    heads = width // DH
    kv = (model_index * heads // (H // KVH)).astype(jnp.int32)
    kv_index = kv.reshape(1)
    seeds_dev = seed_feats.shape[0]
    out_seeds = data_size * seeds_dev // model_size

    levels = data_size // 2

    def to_column(flip):
        return lax.ppermute(
            seed_feats,
            ("dp", "mp"),
            [
                (d * model_size + m, ((m ^ flip) * 2 + d % 2) * model_size + d // 2)
                for d in range(data_size)
                for m in range(model_size)
            ],
        )

    def from_level(block, flip):
        return lax.ppermute(block, "dp", [(d, d ^ (2 * flip)) for d in range(data_size)])

    seed_near, seed_far = to_column(0), to_column(levels // 2)
    chunk = 4 * R // model_size

    def per_cand(*shape):
        return pl.BlockSpec((1, *shape), lambda c, kv_ref: (c, 0, 0))

    def whole(*shape):
        return pl.BlockSpec(shape, lambda c, kv_ref: (0,) * len(shape))

    send, query_grad, value_grad = pl.pallas_call(
        attention_kernel,
        name="attention_backward",
        out_shape=(
            jax.ShapeDtypeStruct((model_size, cands, chunk, seq_len), BF16),
            jax.ShapeDtypeStruct((cands, width, seq_len), BF16),
            jax.ShapeDtypeStruct((cands, seq_len, DH), BF16),
        ),
        grid_spec=pltpu.PrefetchScalarGridSpec(
            num_scalar_prefetch=1,
            grid=(cands,),
            in_specs=[
                per_cand(seq_len, hidden_in.shape[2]),
                per_cand(seq_len, width),
                per_cand(seq_len, width),
                pl.BlockSpec((1, seq_len, DH), lambda c, kv_ref: (c, 0, kv_ref[0])),
                pl.BlockSpec((1, seq_len, DH), lambda c, kv_ref: (c, 0, kv_ref[0])),
                whole(cands, seq_len),
                whole(*down_query.shape),
                whole(*down_value.shape),
                whole(*up_query.shape),
                pl.BlockSpec((R, DH), lambda c, kv_ref: (0, kv_ref[0])),
            ],
            out_specs=[
                pl.BlockSpec((model_size, 1, chunk, seq_len), lambda c, kv_ref: (0, c, 0, 0)),
                per_cand(width, seq_len),
                per_cand(seq_len, DH),
            ],
            scratch_shapes=[pltpu.VMEM((seq_len, DH), F32)],
        ),
        compiler_params=pltpu.CompilerParams(vmem_limit_bytes=60 << 20),
        cost_estimate=pl.CostEstimate(
            flops=5_000_000_000, bytes_accessed=8_000_000, transcendentals=2_000_000
        ),
    )(
        kv_index,
        hidden_in,
        query_act,
        ctx_grad,
        key_act,
        value_act,
        segment_ids,
        down_query,
        down_value,
        up_query,
        up_value,
    )

    send, seed_near, seed_far = lax.optimization_barrier((send, seed_near, seed_far))
    received = lax.all_to_all(send, "mp", 0, 0, tiled=True)
    two = jnp.stack([seed_near, seed_far])
    two_more = from_level(two, 4)
    received, two, two_more = lax.optimization_barrier((received, two, two_more))
    summed = pl.pallas_call(
        sum_kernel,
        name="lowrank_sum",
        out_shape=jax.ShapeDtypeStruct(received.shape, BF16),
        in_specs=[VMEM],
        out_specs=VMEM,
        compiler_params=PARAMS,
    )(received)
    lowrank = lax.all_to_all(summed, "mp", 0, 0, tiled=True)
    four = jnp.concatenate([two, two_more])
    four_more = from_level(four, 2)
    lowrank, four, four_more = lax.optimization_barrier((lowrank, four, four_more))
    eight = jnp.concatenate([four, four_more])
    eight_more = from_level(eight, 1)

    feat_parts = pl.pallas_call(
        feature_kernel,
        name="partial_features",
        out_shape=jax.ShapeDtypeStruct((model_size, cands * KB, PB), BF16),
        in_specs=[SMEM] + [VMEM] * 9,
        out_specs=VMEM,
        compiler_params=PARAMS,
    )(
        kv_index,
        lowrank,
        hidden_in,
        query_grad,
        value_grad,
        block_rows,
        tile_rows,
        block_value.reshape(KVH, DH),
        tile_value.reshape(KVH, DH),
        tile_bank,
    )
    feat_parts, eight = lax.optimization_barrier((feat_parts, eight))
    feat_all = lax.all_to_all(feat_parts, "mp", 0, 0, tiled=True)
    swap = [(d, d ^ 1) for d in range(data_size)]
    other = [lax.ppermute(part, "dp", swap) for part in (eight, eight_more)]
    place = jnp.stack([lax.axis_index("dp") % 2, lax.axis_index("dp") // 2]).astype(jnp.int32)

    return pl.pallas_call(
        score_kernel,
        name="scores",
        out_shape=jax.ShapeDtypeStruct((cands, out_seeds), F32),
        in_specs=[SMEM] + [VMEM] * 5,
        out_specs=VMEM,
        scratch_shapes=[pltpu.VMEM((cands * KB, PB), F32)],
        compiler_params=PARAMS,
    )(place, feat_all, eight, eight_more, *other)


def solution(mesh):
    return jax.shard_map(
        local,
        mesh=mesh,
        in_specs=(
            P("dp", None, "mp"),
            P("dp", None, "mp"),
            P("dp", None, None),
            P("dp", None, None),
            P("dp", None, "mp"),
            P("dp", None),
            P("mp", None),
            P(None, "mp"),
            P("mp", None),
            P(),
            P(None, "mp"),
            P(None, "mp"),
            P(),
            P(),
            P(),
            P("dp", "mp"),
        ),
        out_specs=P("dp", "mp"),
        check_vma=False,
    )
```

```python
import math

import jax
import jax.numpy as jnp
from jax import lax
from jax.experimental import pallas as pl
from jax.experimental.pallas import tpu as pltpu
from jax.sharding import PartitionSpec as P

H = 64
KVH = 8
DH = 128
R = 128
K = 8192
PB = 128
NT = 8
S = 512
KB = 64
EPS = 1e-06
LONGEST = 256
ROWS = 128
CHUNK = 32
F32 = jnp.float32
BF16 = jnp.bfloat16


def dot_nn(a, b):
    return lax.dot_general(a, b, (((1,), (0,)), ((), ())), preferred_element_type=F32)


def dot_nt(a, b):
    return lax.dot_general(a, b, (((1,), (1,)), ((), ())), preferred_element_type=F32)


def attention_kernel(
    kv_index,
    hidden_ref,
    query_ref,
    grad_ref,
    key_ref,
    value_ref,
    segment_ref,
    down_query_ref,
    down_value_ref,
    up_query_ref,
    up_value_ref,
    send_ref,
    head_grad_ref,
    value_sum,
    down_t,
    bias_ref,
    logit_ref,
    prob_grad_ref,
    prob_ref,
    logit_grad_ref,
):
    cand = pl.program_id(0)
    parts = send_ref.shape[0]
    chunk = send_ref.shape[2]
    quarter = R // chunk
    heads = query_ref.shape[2] // DH
    score_scale = 1.0 / math.sqrt(DH)
    exp_scale = score_scale * math.log2(math.e)

    @pl.when(cand == 0)
    def _():
        down_t[:R] = down_query_ref[...].T
        down_t[R:] = down_value_ref[...].T

    lowrank_in = dot_nt(down_t[...], hidden_ref[0])
    send_ref[0 : 2 * quarter, 0] = lowrank_in.astype(BF16).reshape(2 * quarter, chunk, S)

    segment_row = segment_ref[pl.ds(cand, 1), :].astype(F32)
    segment_col = jnp.broadcast_to(segment_row, (8, S)).T[:, 0:1]
    key_t = key_ref[0].T
    value_sum[...] = jnp.zeros_like(value_sum)

    for block in range(S // ROWS):
        first = block * ROWS
        low = max(0, (first - LONGEST + 1) // ROWS * ROWS)
        high = first + ROWS
        width = high - low
        for at in range(0, width, ROWS):
            allowed = segment_col[low + at : low + at + ROWS] == segment_row[:, first:high]
            if low + at == first:
                key_pos = lax.broadcasted_iota(jnp.int32, (ROWS, ROWS), 0)
                row_pos = lax.broadcasted_iota(jnp.int32, (ROWS, ROWS), 1)
                allowed = allowed & (key_pos <= row_pos)
            bias_ref[block, at : at + ROWS] = jnp.where(allowed, 0.0, -1e30)
    for block in range(S // ROWS):
        first = block * ROWS
        low = max(0, (first - LONGEST + 1) // ROWS * ROWS)
        high = first + ROWS
        width = high - low
        slot = block % 2

        def stacked(ref):
            return jnp.concatenate(
                [ref[0, first:high, h * DH : (h + 1) * DH] for h in range(heads)], axis=0
            )

        grad = stacked(grad_ref)
        logit_ref[slot, :width] = dot_nt(key_ref[0, low:high], stacked(query_ref))
        prob_grad_ref[slot, :width] = dot_nt(value_ref[0, low:high], grad)

        def logits(at):
            bias = bias_ref[block, at : at + CHUNK]
            return logit_ref[slot, at : at + CHUNK] + jnp.concatenate([bias] * heads, axis=1)

        lanes = heads * ROWS
        top = jnp.full((8, lanes), -3e38, F32)
        for at in range(0, width, CHUNK):
            top = jnp.maximum(top, jnp.max(logits(at).reshape(CHUNK // 8, 8, lanes), axis=0))
        row_top = jnp.max(top, axis=0, keepdims=True)
        total = jnp.zeros((8, lanes), F32)
        delta = jnp.zeros((8, lanes), F32)
        for at in range(0, width, CHUNK):
            terms = jnp.exp2((logits(at) - row_top) * exp_scale)
            total = total + jnp.sum(terms.reshape(CHUNK // 8, 8, lanes), axis=0)
            weighted = terms * prob_grad_ref[slot, at : at + CHUNK]
            delta = delta + jnp.sum(weighted.reshape(CHUNK // 8, 8, lanes), axis=0)
            logit_ref[slot, at : at + CHUNK] = terms
        inverse = 1.0 / jnp.sum(total, axis=0, keepdims=True)
        row_delta = jnp.sum(delta, axis=0, keepdims=True) * inverse
        for at in range(0, width, CHUNK):
            probs = logit_ref[slot, at : at + CHUNK] * inverse
            prob_ref[slot, at : at + CHUNK] = probs.astype(BF16)
            logit_grad_ref[slot, at : at + CHUNK] = (
                probs * (prob_grad_ref[slot, at : at + CHUNK] - row_delta)
            ).astype(BF16)
        value_sum[low:high] += dot_nn(prob_ref[slot, :width], grad)
        query_grad = dot_nn(key_t[:, low:high], logit_grad_ref[slot, :width]) * score_scale
        query_grad = query_grad.astype(BF16)
        for h in range(heads):
            head_grad_ref[0, h * DH : (h + 1) * DH, first:high] = query_grad[
                :, h * ROWS : (h + 1) * ROWS
            ]

    value_grad = value_sum[...].T.astype(BF16)
    head_grad_ref[0, heads * DH :] = value_grad
    back_query = dot_nn(up_query_ref[...], head_grad_ref[0, : heads * DH])
    back_value = dot_nn(up_value_ref[...], value_grad)
    send_ref[2 * quarter : 3 * quarter, 0] = back_query.astype(BF16).reshape(quarter, chunk, S)
    send_ref[3 * quarter : parts, 0] = back_value.astype(BF16).reshape(quarter, chunk, S)


def sum_kernel(parts_ref, out_ref):
    total = jnp.sum(parts_ref[...].astype(F32), axis=0)
    out_ref[...] = jnp.broadcast_to(total.astype(BF16)[None], out_ref.shape)


def feature_kernel(
    kv_index,
    lowrank_ref,
    hidden_ref,
    head_grad_ref,
    block_ref,
    tile_ref,
    block_value_ref,
    tile_value_ref,
    bank_hbm,
    out_ref,
    bank_ref,
    bank_sem,
):
    bank_copy = pltpu.make_async_copy(bank_hbm, bank_ref, bank_sem)
    bank_copy.start()
    cands = hidden_ref.shape[0]
    width = head_grad_ref.shape[1] - DH
    kv = kv_index[0]
    pieces = [[], [], [], []]
    for cand in range(cands):
        lowrank = lowrank_ref[:, cand].reshape(4 * R, S)
        down = dot_nn(lowrank[2 * R :], hidden_ref[cand])
        pieces[0].append(down[:R])
        pieces[1].append(down[R:])
        pieces[2].append(dot_nt(lowrank[:R], head_grad_ref[cand, :width]))
        pieces[3].append(dot_nt(lowrank[R : 2 * R], head_grad_ref[cand, width:]))
    buckets = KB * NT
    sums = jnp.zeros((buckets, cands * R), F32)
    for kind in range(4):
        if kind < 3:
            ids = tile_ref[kind : kind + 1, :] * KB + block_ref[kind : kind + 1, :]
        else:
            ids = tile_value_ref[pl.ds(kv, 1), :] * KB + block_value_ref[pl.ds(kv, 1), :]
        rows = jnp.concatenate(pieces[kind], axis=0).astype(BF16)
        where = lax.broadcasted_iota(jnp.int32, (buckets, rows.shape[1]), 0)
        chosen = jnp.where(where == ids, 1.0, 0.0).astype(BF16)
        sums = sums + dot_nt(chosen, rows)
    wide = jnp.concatenate(
        [
            jnp.concatenate(
                [sums[t * KB : (t + 1) * KB, c * R : (c + 1) * R] for t in range(NT)], axis=1
            )
            for c in range(cands)
        ],
        axis=0,
    )
    high = wide.astype(BF16)
    low = (wide - high.astype(F32)).astype(BF16)
    bank_copy.wait()
    bank = bank_ref[...].reshape(NT * R, PB)
    feats = dot_nn(high, bank) + dot_nn(low, bank)
    out_ref[...] = jnp.broadcast_to(feats.astype(BF16)[None], out_ref.shape)


def score_kernel(place, parts_ref, *refs):
    mine_refs, other_refs, (out_ref, feats_ref) = refs[:4], refs[4:8], refs[8:]
    cands = out_ref.shape[0]
    fours, seeds, depth = mine_refs[0].shape
    per_part = depth // PB
    feats_ref[...] = jnp.sum(parts_ref[...].astype(F32), axis=0)
    totals = [[jnp.zeros((seeds, PB), F32) for _ in range(2)] for _ in range(cands)]
    for at in range(4 * fours):
        source = place[1] ^ (at % 2 * 8 + at // 2 % 2 * 4 + at // 4 % 2 * 2 + at // 8)
        for part in range(per_part):
            feat = [
                feats_ref[pl.ds(c * KB + source * per_part + part, 1), :] for c in range(cands)
            ]
            for half, seeds_ref in enumerate((mine_refs[at // fours], other_refs[at // fours])):
                seed = seeds_ref[at % fours, :, part * PB : (part + 1) * PB].astype(F32)
                for c in range(cands):
                    totals[c][half] = totals[c][half] + feat[c] * seed
    first_core = place[0] == 0
    for c in range(cands):
        mine = feats_ref[c * KB : (c + 1) * KB]
        square = jnp.sum(jnp.sum(mine * mine, axis=0, keepdims=True), axis=1, keepdims=True)
        here, there = totals[c]
        ordered = jnp.concatenate(
            [jnp.where(first_core, here, there), jnp.where(first_core, there, here)], axis=0
        )
        numerator = jnp.sum(ordered.T, axis=0, keepdims=True)
        out_ref[c : c + 1, :] = numerator * lax.rsqrt(square / K + EPS) * K ** (-0.5)


VMEM = pl.BlockSpec(memory_space=pltpu.VMEM)
SMEM = pl.BlockSpec(memory_space=pltpu.SMEM)
PARAMS = pltpu.CompilerParams(vmem_limit_bytes=24 << 20)


def local(
    hidden_in,
    query_act,
    key_act,
    value_act,
    ctx_grad,
    segment_ids,
    down_query,
    up_query,
    down_value,
    up_value,
    block_rows,
    tile_rows,
    block_value,
    tile_value,
    tile_bank,
    seed_feats,
):
    model_index = lax.axis_index("mp")
    data_size = lax.axis_size("dp")
    model_size = lax.axis_size("mp")
    cands, seq_len, width = query_act.shape
    heads = width // DH
    kv = (model_index * heads // (H // KVH)).astype(jnp.int32)
    kv_index = kv.reshape(1)
    seeds_dev = seed_feats.shape[0]
    out_seeds = data_size * seeds_dev // model_size

    levels = data_size // 2

    def to_column(flip):
        return lax.ppermute(
            seed_feats,
            ("dp", "mp"),
            [
                (d * model_size + m, ((m ^ flip) * 2 + d % 2) * model_size + d // 2)
                for d in range(data_size)
                for m in range(model_size)
            ],
        )

    def from_level(block, flip):
        return lax.ppermute(block, "dp", [(d, d ^ (2 * flip)) for d in range(data_size)])

    def from_core(block):
        return lax.ppermute(block, "dp", [(d, d ^ 1) for d in range(data_size)])

    seed_near, seed_far = to_column(0), to_column(levels // 2)
    chunk = 4 * R // model_size
    span = LONGEST + ROWS

    def per_cand(*shape):
        return pl.BlockSpec((1, *shape), lambda c, kv_ref: (c, 0, 0))

    def whole(*shape):
        return pl.BlockSpec(shape, lambda c, kv_ref: (0,) * len(shape))

    send, head_grad = pl.pallas_call(
        attention_kernel,
        name="attention_backward",
        out_shape=(
            jax.ShapeDtypeStruct((model_size, cands, chunk, seq_len), BF16),
            jax.ShapeDtypeStruct((cands, width + DH, seq_len), BF16),
        ),
        grid_spec=pltpu.PrefetchScalarGridSpec(
            num_scalar_prefetch=1,
            grid=(cands,),
            in_specs=[
                per_cand(seq_len, hidden_in.shape[2]),
                per_cand(seq_len, width),
                per_cand(seq_len, width),
                pl.BlockSpec((1, seq_len, DH), lambda c, kv_ref: (c, 0, kv_ref[0])),
                pl.BlockSpec((1, seq_len, DH), lambda c, kv_ref: (c, 0, kv_ref[0])),
                whole(cands, seq_len),
                whole(*down_query.shape),
                whole(*down_value.shape),
                whole(*up_query.shape),
                pl.BlockSpec((R, DH), lambda c, kv_ref: (0, kv_ref[0])),
            ],
            out_specs=[
                pl.BlockSpec((model_size, 1, chunk, seq_len), lambda c, kv_ref: (0, c, 0, 0)),
                per_cand(width + DH, seq_len),
            ],
            scratch_shapes=[
                pltpu.VMEM((seq_len, DH), F32),
                pltpu.VMEM((2 * R, hidden_in.shape[2]), BF16),
                pltpu.VMEM((seq_len // ROWS, span, ROWS), F32),
                pltpu.VMEM((2, span, heads * ROWS), F32),
                pltpu.VMEM((2, span, heads * ROWS), F32),
                pltpu.VMEM((2, span, heads * ROWS), BF16),
                pltpu.VMEM((2, span, heads * ROWS), BF16),
            ],
        ),
        compiler_params=pltpu.CompilerParams(vmem_limit_bytes=60 << 20),
        cost_estimate=pl.CostEstimate(
            flops=5_000_000_000, bytes_accessed=8_000_000, transcendentals=2_000_000
        ),
    )(
        kv_index,
        hidden_in,
        query_act,
        ctx_grad,
        key_act,
        value_act,
        segment_ids,
        down_query,
        down_value,
        up_query,
        up_value,
    )

    send, seed_near, seed_far = lax.optimization_barrier((send, seed_near, seed_far))
    received = lax.all_to_all(send, "mp", 0, 0, tiled=True)
    two = jnp.stack([seed_near, seed_far])
    two_more = from_level(two, 4)
    received, two, two_more = lax.optimization_barrier((received, two, two_more))
    summed = pl.pallas_call(
        sum_kernel,
        name="lowrank_sum",
        out_shape=jax.ShapeDtypeStruct(received.shape, BF16),
        in_specs=[VMEM],
        out_specs=VMEM,
        compiler_params=PARAMS,
    )(received)
    lowrank = lax.all_to_all(summed, "mp", 0, 0, tiled=True)
    four = jnp.concatenate([two, two_more])
    fours = [four, from_level(four, 2), from_level(four, 1)]
    others = [from_core(four)]
    lowrank, *both = lax.optimization_barrier((lowrank, *fours, *others))
    fours, others = both[:3], both[3:]
    fours.append(from_level(fours[1], 1))

    feat_parts = pl.pallas_call(
        feature_kernel,
        name="partial_features",
        out_shape=jax.ShapeDtypeStruct((model_size, cands * KB, PB), BF16),
        in_specs=[SMEM] + [VMEM] * 7 + [pl.BlockSpec(memory_space=pltpu.HBM)],
        out_specs=VMEM,
        scratch_shapes=[pltpu.VMEM(tile_bank.shape, BF16), pltpu.SemaphoreType.DMA],
        compiler_params=PARAMS,
    )(
        kv_index,
        lowrank,
        hidden_in,
        head_grad,
        block_rows,
        tile_rows,
        block_value.reshape(KVH, DH),
        tile_value.reshape(KVH, DH),
        tile_bank,
    )
    feat_parts, *fours[1:3] = lax.optimization_barrier((feat_parts, *fours[1:3]))
    feat_all = lax.all_to_all(feat_parts, "mp", 0, 0, tiled=True)
    others += [from_core(part) for part in fours[1:]]
    place = jnp.stack([lax.axis_index("dp") % 2, lax.axis_index("dp") // 2]).astype(jnp.int32)

    return pl.pallas_call(
        score_kernel,
        name="scores",
        out_shape=jax.ShapeDtypeStruct((cands, out_seeds), F32),
        in_specs=[SMEM] + [VMEM] * 9,
        out_specs=VMEM,
        scratch_shapes=[pltpu.VMEM((cands * KB, PB), F32)],
        compiler_params=PARAMS,
    )(place, feat_all, *fours, *others)


def solution(mesh):
    return jax.shard_map(
        local,
        mesh=mesh,
        in_specs=(
            P("dp", None, "mp"),
            P("dp", None, "mp"),
            P("dp", None, None),
            P("dp", None, None),
            P("dp", None, "mp"),
            P("dp", None),
            P("mp", None),
            P(None, "mp"),
            P("mp", None),
            P(),
            P(None, "mp"),
            P(None, "mp"),
            P(),
            P(),
            P(),
            P("dp", "mp"),
        ),
        out_specs=P("dp", "mp"),
        check_vma=False,
    )
```

```python
import math

import jax
import jax.numpy as jnp
from jax import lax
from jax.experimental import pallas as pl
from jax.experimental.pallas import tpu as pltpu
from jax.sharding import PartitionSpec as P

H = 64
KVH = 8
DH = 128
R = 128
K = 8192
PB = 128
NT = 8
S = 512
KB = 64
EPS = 1e-06
LONGEST = 256
ROWS = 128
CHUNK = 32
F32 = jnp.float32
BF16 = jnp.bfloat16


def dot_nn(a, b):
    return lax.dot_general(a, b, (((1,), (0,)), ((), ())), preferred_element_type=F32)


def dot_nt(a, b):
    return lax.dot_general(a, b, (((1,), (1,)), ((), ())), preferred_element_type=F32)


def attention_kernel(
    kv_index,
    hidden_ref,
    query_ref,
    grad_ref,
    key_ref,
    value_ref,
    segment_ref,
    down_query_ref,
    down_value_ref,
    up_query_ref,
    up_value_ref,
    block_ref,
    tile_ref,
    block_value_ref,
    tile_value_ref,
    bank_ref,
    send_ref,
    packed_ref,
    value_sum,
    down_t,
    bias_ref,
    logit_ref,
    prob_grad_ref,
    prob_ref,
    logit_grad_ref,
):
    cand = pl.program_id(0)
    parts = send_ref.shape[0]
    chunk = send_ref.shape[2]
    quarter = R // chunk
    heads = query_ref.shape[2] // DH
    score_scale = 1.0 / math.sqrt(DH)
    exp_scale = score_scale * math.log2(math.e)

    @pl.when(cand == 0)
    def _():
        down_t[:R] = down_query_ref[...].T
        down_t[R:] = down_value_ref[...].T

    width = heads * DH
    kv = kv_index[0]
    for tile in range(bank_ref.shape[0]):
        packed_ref[0, width + DH : width + 2 * DH, tile * PB : (tile + 1) * PB] = bank_ref[tile]
    ids = [
        block_ref[...],
        jnp.concatenate([block_value_ref[pl.ds(kv, 1), :]] * heads, axis=1),
        tile_ref[...],
        jnp.concatenate([tile_value_ref[pl.ds(kv, 1), :]] * heads, axis=1),
        jnp.zeros((8, width), jnp.int32),
    ]
    ids = jnp.concatenate(ids, axis=0).astype(F32).astype(BF16)
    packed_ref[0, width + 2 * DH :] = ids

    lowrank_in = dot_nt(down_t[...], hidden_ref[0])
    send_ref[0 : 2 * quarter, 0] = lowrank_in.astype(BF16).reshape(2 * quarter, chunk, S)

    segment_row = segment_ref[pl.ds(cand, 1), :].astype(F32)
    segment_col = jnp.broadcast_to(segment_row, (8, S)).T[:, 0:1]
    key_t = key_ref[0].T
    value_sum[...] = jnp.zeros_like(value_sum)

    for block in range(S // ROWS):
        first = block * ROWS
        low = max(0, (first - LONGEST + 1) // ROWS * ROWS)
        high = first + ROWS
        reach = high - low
        for at in range(0, reach, ROWS):
            allowed = segment_col[low + at : low + at + ROWS] == segment_row[:, first:high]
            if low + at == first:
                key_pos = lax.broadcasted_iota(jnp.int32, (ROWS, ROWS), 0)
                row_pos = lax.broadcasted_iota(jnp.int32, (ROWS, ROWS), 1)
                allowed = allowed & (key_pos <= row_pos)
            bias_ref[block, at : at + ROWS] = jnp.where(allowed, 0.0, -1e30)
    for block in range(S // ROWS):
        first = block * ROWS
        low = max(0, (first - LONGEST + 1) // ROWS * ROWS)
        high = first + ROWS
        reach = high - low
        slot = block % 2

        def stacked(ref):
            return jnp.concatenate(
                [ref[0, first:high, h * DH : (h + 1) * DH] for h in range(heads)], axis=0
            )

        grad = stacked(grad_ref)
        logit_ref[slot, :reach] = dot_nt(key_ref[0, low:high], stacked(query_ref))
        prob_grad_ref[slot, :reach] = dot_nt(value_ref[0, low:high], grad)

        def logits(at):
            bias = bias_ref[block, at : at + CHUNK]
            return logit_ref[slot, at : at + CHUNK] + jnp.concatenate([bias] * heads, axis=1)

        lanes = heads * ROWS
        top = jnp.full((8, lanes), -3e38, F32)
        for at in range(0, reach, CHUNK):
            top = jnp.maximum(top, jnp.max(logits(at).reshape(CHUNK // 8, 8, lanes), axis=0))
        row_top = jnp.max(top, axis=0, keepdims=True)
        total = jnp.zeros((8, lanes), F32)
        delta = jnp.zeros((8, lanes), F32)
        for at in range(0, reach, CHUNK):
            terms = jnp.exp2((logits(at) - row_top) * exp_scale)
            total = total + jnp.sum(terms.reshape(CHUNK // 8, 8, lanes), axis=0)
            weighted = terms * prob_grad_ref[slot, at : at + CHUNK]
            delta = delta + jnp.sum(weighted.reshape(CHUNK // 8, 8, lanes), axis=0)
            logit_ref[slot, at : at + CHUNK] = terms
        inverse = 1.0 / jnp.sum(total, axis=0, keepdims=True)
        row_delta = jnp.sum(delta, axis=0, keepdims=True) * inverse
        for at in range(0, reach, CHUNK):
            probs = logit_ref[slot, at : at + CHUNK] * inverse
            prob_ref[slot, at : at + CHUNK] = probs.astype(BF16)
            logit_grad_ref[slot, at : at + CHUNK] = (
                probs * (prob_grad_ref[slot, at : at + CHUNK] - row_delta)
            ).astype(BF16)
        value_sum[low:high] += dot_nn(prob_ref[slot, :reach], grad)
        query_grad = dot_nn(key_t[:, low:high], logit_grad_ref[slot, :reach]) * score_scale
        query_grad = query_grad.astype(BF16)
        for h in range(heads):
            packed_ref[0, h * DH : (h + 1) * DH, first:high] = query_grad[
                :, h * ROWS : (h + 1) * ROWS
            ]

    value_grad = value_sum[...].T.astype(BF16)
    packed_ref[0, width : width + DH] = value_grad
    back_query = dot_nn(up_query_ref[...], packed_ref[0, :width])
    back_value = dot_nn(up_value_ref[...], value_grad)
    send_ref[2 * quarter : 3 * quarter, 0] = back_query.astype(BF16).reshape(quarter, chunk, S)
    send_ref[3 * quarter : parts, 0] = back_value.astype(BF16).reshape(quarter, chunk, S)


def sum_kernel(parts_ref, out_ref):
    total = jnp.sum(parts_ref[...].astype(F32), axis=0)
    out_ref[...] = jnp.broadcast_to(total.astype(BF16)[None], out_ref.shape)


def feature_kernel(lowrank_ref, hidden_ref, packed_ref, out_ref):
    cands = hidden_ref.shape[0]
    width = hidden_ref.shape[2]
    values = slice(width, width + DH)
    tile_rows = slice(width + DH, width + 2 * DH)
    pieces = [[], [], [], []]
    for cand in range(cands):
        lowrank = lowrank_ref[:, cand].reshape(4 * R, S)
        down = dot_nn(lowrank[2 * R :], hidden_ref[cand])
        pieces[0].append(down[:R])
        pieces[1].append(down[R:])
        pieces[2].append(dot_nt(lowrank[:R], packed_ref[cand, :width]))
        pieces[3].append(dot_nt(lowrank[R : 2 * R], packed_ref[cand, values]))
    buckets = KB * NT
    ids = packed_ref[0, width + 2 * DH :].astype(F32)
    ids = (ids[4:8] * KB + ids[0:4]).astype(jnp.int32)
    sums = jnp.zeros((buckets, cands * R), F32)
    for kind in range(4):
        rows = jnp.concatenate(pieces[kind], axis=0).astype(BF16)
        count = rows.shape[1]
        where = lax.broadcasted_iota(jnp.int32, (buckets, count), 0)
        chosen = jnp.where(where == ids[kind : kind + 1, :count], 1.0, 0.0).astype(BF16)
        sums = sums + dot_nt(chosen, rows)
    wide = jnp.concatenate(
        [
            jnp.concatenate(
                [sums[t * KB : (t + 1) * KB, c * R : (c + 1) * R] for t in range(NT)], axis=1
            )
            for c in range(cands)
        ],
        axis=0,
    )
    high = wide.astype(BF16)
    low = (wide - high.astype(F32)).astype(BF16)
    tiles = NT // cands
    bank = jnp.concatenate(
        [
            packed_ref[c, tile_rows, t * PB : (t + 1) * PB]
            for c in range(cands)
            for t in range(tiles)
        ],
        axis=0,
    )
    feats = dot_nn(high, bank) + dot_nn(low, bank)
    out_ref[...] = jnp.broadcast_to(feats.astype(BF16)[None], out_ref.shape)


def score_kernel(place, parts_ref, *refs):
    mine_refs, other_refs, (out_ref, feats_ref) = refs[:2], refs[2:4], refs[4:]
    cands = out_ref.shape[0]
    eights, seeds, depth = mine_refs[0].shape
    per_part = depth // PB
    feats_ref[...] = jnp.sum(parts_ref[...].astype(F32), axis=0)
    totals = [[jnp.zeros((seeds, PB), F32) for _ in range(2)] for _ in range(cands)]
    for at in range(2 * eights):
        source = place[1] ^ (at % 2 * 8 + at // 2 % 2 * 4 + at // 4 % 2 * 2 + at // 8)
        for part in range(per_part):
            feat = [
                feats_ref[pl.ds(c * KB + source * per_part + part, 1), :] for c in range(cands)
            ]
            for half, seeds_ref in enumerate((mine_refs[at // eights], other_refs[at // eights])):
                seed = seeds_ref[at % eights, :, part * PB : (part + 1) * PB].astype(F32)
                for c in range(cands):
                    totals[c][half] = totals[c][half] + feat[c] * seed
    first_core = place[0] == 0
    for c in range(cands):
        mine = feats_ref[c * KB : (c + 1) * KB]
        square = jnp.sum(jnp.sum(mine * mine, axis=0, keepdims=True), axis=1, keepdims=True)
        here, there = totals[c]
        ordered = jnp.concatenate(
            [jnp.where(first_core, here, there), jnp.where(first_core, there, here)], axis=0
        )
        numerator = jnp.sum(ordered.T, axis=0, keepdims=True)
        out_ref[c : c + 1, :] = numerator * lax.rsqrt(square / K + EPS) * K ** (-0.5)


VMEM = pl.BlockSpec(memory_space=pltpu.VMEM)
SMEM = pl.BlockSpec(memory_space=pltpu.SMEM)
PARAMS = pltpu.CompilerParams(vmem_limit_bytes=40 << 20)


def local(
    hidden_in,
    query_act,
    key_act,
    value_act,
    ctx_grad,
    segment_ids,
    down_query,
    up_query,
    down_value,
    up_value,
    block_rows,
    tile_rows,
    block_value,
    tile_value,
    tile_bank,
    seed_feats,
):
    model_index = lax.axis_index("mp")
    data_size = lax.axis_size("dp")
    model_size = lax.axis_size("mp")
    cands, seq_len, width = query_act.shape
    heads = width // DH
    kv = (model_index * heads // (H // KVH)).astype(jnp.int32)
    kv_index = kv.reshape(1)
    seeds_dev = seed_feats.shape[0]
    out_seeds = data_size * seeds_dev // model_size

    levels = data_size // 2

    def to_column(flip):
        return lax.ppermute(
            seed_feats,
            ("dp", "mp"),
            [
                (d * model_size + m, ((m ^ flip) * 2 + d % 2) * model_size + d // 2)
                for d in range(data_size)
                for m in range(model_size)
            ],
        )

    def from_level(block, flip):
        return lax.ppermute(block, "dp", [(d, d ^ (2 * flip)) for d in range(data_size)])

    def from_core(block):
        return lax.ppermute(block, "dp", [(d, d ^ 1) for d in range(data_size)])

    seed_near, seed_far = to_column(0), to_column(levels // 2)
    chunk = 4 * R // model_size
    span = LONGEST + ROWS
    packed_rows = width + 2 * DH + 16
    tiles = NT // cands

    def per_cand(*shape):
        return pl.BlockSpec((1, *shape), lambda c, kv_ref: (c, 0, 0))

    def whole(*shape):
        return pl.BlockSpec(shape, lambda c, kv_ref: (0,) * len(shape))

    send, packed = pl.pallas_call(
        attention_kernel,
        name="attention_backward",
        out_shape=(
            jax.ShapeDtypeStruct((model_size, cands, chunk, seq_len), BF16),
            jax.ShapeDtypeStruct((cands, packed_rows, seq_len), BF16),
        ),
        grid_spec=pltpu.PrefetchScalarGridSpec(
            num_scalar_prefetch=1,
            grid=(cands,),
            in_specs=[
                per_cand(seq_len, hidden_in.shape[2]),
                per_cand(seq_len, width),
                per_cand(seq_len, width),
                pl.BlockSpec((1, seq_len, DH), lambda c, kv_ref: (c, 0, kv_ref[0])),
                pl.BlockSpec((1, seq_len, DH), lambda c, kv_ref: (c, 0, kv_ref[0])),
                whole(cands, seq_len),
                whole(*down_query.shape),
                whole(*down_value.shape),
                whole(*up_query.shape),
                pl.BlockSpec((R, DH), lambda c, kv_ref: (0, kv_ref[0])),
                whole(*block_rows.shape),
                whole(*tile_rows.shape),
                whole(KVH, DH),
                whole(KVH, DH),
                pl.BlockSpec((tiles, R, PB), lambda c, kv_ref: (c, 0, 0)),
            ],
            out_specs=[
                pl.BlockSpec((model_size, 1, chunk, seq_len), lambda c, kv_ref: (0, c, 0, 0)),
                per_cand(packed_rows, seq_len),
            ],
            scratch_shapes=[
                pltpu.VMEM((seq_len, DH), F32),
                pltpu.VMEM((2 * R, hidden_in.shape[2]), BF16),
                pltpu.VMEM((seq_len // ROWS, span, ROWS), F32),
                pltpu.VMEM((2, span, heads * ROWS), F32),
                pltpu.VMEM((2, span, heads * ROWS), F32),
                pltpu.VMEM((2, span, heads * ROWS), BF16),
                pltpu.VMEM((2, span, heads * ROWS), BF16),
            ],
        ),
        compiler_params=pltpu.CompilerParams(vmem_limit_bytes=60 << 20),
        cost_estimate=pl.CostEstimate(
            flops=5_000_000_000, bytes_accessed=8_000_000, transcendentals=2_000_000
        ),
    )(
        kv_index,
        hidden_in,
        query_act,
        ctx_grad,
        key_act,
        value_act,
        segment_ids,
        down_query,
        down_value,
        up_query,
        up_value,
        block_rows,
        tile_rows,
        block_value.reshape(KVH, DH),
        tile_value.reshape(KVH, DH),
        tile_bank,
    )

    send, seed_near, seed_far = lax.optimization_barrier((send, seed_near, seed_far))
    received = lax.all_to_all(send, "mp", 0, 0, tiled=True)
    two = jnp.stack([seed_near, seed_far])
    two_more = from_level(two, 4)
    received, two, two_more = lax.optimization_barrier((received, two, two_more))
    summed = pl.pallas_call(
        sum_kernel,
        name="lowrank_sum",
        out_shape=jax.ShapeDtypeStruct(received.shape, BF16),
        in_specs=[VMEM],
        out_specs=VMEM,
        compiler_params=PARAMS,
    )(received)
    lowrank = lax.all_to_all(summed, "mp", 0, 0, tiled=True)
    four = jnp.concatenate([two, two_more])
    four_more = from_level(four, 2)
    lowrank, four, four_more = lax.optimization_barrier((lowrank, four, four_more))
    eight = jnp.concatenate([four, four_more])
    eight_more = from_level(eight, 1)

    feat_parts = pl.pallas_call(
        feature_kernel,
        name="partial_features",
        out_shape=jax.ShapeDtypeStruct((model_size, cands * KB, PB), BF16),
        in_specs=[VMEM] * 3,
        out_specs=VMEM,
        compiler_params=PARAMS,
    )(lowrank, hidden_in, packed)
    feat_parts, eight = lax.optimization_barrier((feat_parts, eight))
    feat_all = lax.all_to_all(feat_parts, "mp", 0, 0, tiled=True)
    other = [from_core(part) for part in (eight, eight_more)]
    place = jnp.stack([lax.axis_index("dp") % 2, lax.axis_index("dp") // 2]).astype(jnp.int32)

    return pl.pallas_call(
        score_kernel,
        name="scores",
        out_shape=jax.ShapeDtypeStruct((cands, out_seeds), F32),
        in_specs=[SMEM] + [VMEM] * 5,
        out_specs=VMEM,
        scratch_shapes=[pltpu.VMEM((cands * KB, PB), F32)],
        compiler_params=PARAMS,
    )(place, feat_all, eight, eight_more, *other)


def solution(mesh):
    return jax.shard_map(
        local,
        mesh=mesh,
        in_specs=(
            P("dp", None, "mp"),
            P("dp", None, "mp"),
            P("dp", None, None),
            P("dp", None, None),
            P("dp", None, "mp"),
            P("dp", None),
            P("mp", None),
            P(None, "mp"),
            P("mp", None),
            P(),
            P(None, "mp"),
            P(None, "mp"),
            P(),
            P(),
            P(),
            P("dp", "mp"),
        ),
        out_specs=P("dp", "mp"),
        check_vma=False,
    )
```

```python
import math

import jax
import jax.numpy as jnp
from jax import lax
from jax.experimental import pallas as pl
from jax.experimental.pallas import tpu as pltpu
from jax.sharding import PartitionSpec as P

H = 64
KVH = 8
DH = 128
R = 128
K = 8192
PB = 128
NT = 8
S = 512
KB = 64
EPS = 1e-06
LONGEST = 256
ROWS = 128
CHUNK = 32
F32 = jnp.float32
BF16 = jnp.bfloat16


def dot_nn(a, b):
    return lax.dot_general(a, b, (((1,), (0,)), ((), ())), preferred_element_type=F32)


def dot_nt(a, b):
    return lax.dot_general(a, b, (((1,), (1,)), ((), ())), preferred_element_type=F32)


def attention_kernel(
    kv_index,
    hidden_ref,
    query_ref,
    grad_ref,
    key_ref,
    value_ref,
    segment_ref,
    down_query_ref,
    down_value_ref,
    up_query_ref,
    up_value_ref,
    block_ref,
    tile_ref,
    block_value_ref,
    tile_value_ref,
    bank_ref,
    send_ref,
    packed_ref,
    value_sum,
    down_t,
    bias_ref,
    logit_ref,
    prob_grad_ref,
    prob_ref,
    logit_grad_ref,
):
    cand = pl.program_id(0)
    parts = send_ref.shape[0]
    chunk = send_ref.shape[2]
    quarter = R // chunk
    heads = query_ref.shape[2] // DH
    score_scale = 1.0 / math.sqrt(DH)
    exp_scale = score_scale * math.log2(math.e)

    @pl.when(cand == 0)
    def _():
        down_t[:R] = down_query_ref[...].T
        down_t[R:] = down_value_ref[...].T

    width = heads * DH
    kv = kv_index[0]
    for tile in range(bank_ref.shape[0]):
        packed_ref[0, width + DH : width + 2 * DH, tile * PB : (tile + 1) * PB] = bank_ref[tile]
    ids = [
        block_ref[...],
        jnp.concatenate([block_value_ref[pl.ds(kv, 1), :]] * heads, axis=1),
        tile_ref[...],
        jnp.concatenate([tile_value_ref[pl.ds(kv, 1), :]] * heads, axis=1),
        jnp.zeros((8, width), jnp.int32),
    ]
    ids = jnp.concatenate(ids, axis=0).astype(F32).astype(BF16)
    packed_ref[0, width + 2 * DH :] = ids

    lowrank_in = dot_nt(down_t[...], hidden_ref[0])
    send_ref[0 : 2 * quarter, 0] = lowrank_in.astype(BF16).reshape(2 * quarter, chunk, S)

    segment_row = segment_ref[pl.ds(cand, 1), :].astype(F32)
    segment_col = jnp.broadcast_to(segment_row, (8, S)).T[:, 0:1]
    key_t = key_ref[0].T
    value_sum[...] = jnp.zeros_like(value_sum)

    for block in range(S // ROWS):
        first = block * ROWS
        low = max(0, (first - LONGEST + 1) // ROWS * ROWS)
        high = first + ROWS
        reach = high - low
        for at in range(0, reach, ROWS):
            allowed = segment_col[low + at : low + at + ROWS] == segment_row[:, first:high]
            if low + at == first:
                key_pos = lax.broadcasted_iota(jnp.int32, (ROWS, ROWS), 0)
                row_pos = lax.broadcasted_iota(jnp.int32, (ROWS, ROWS), 1)
                allowed = allowed & (key_pos <= row_pos)
            bias_ref[block, at : at + ROWS] = jnp.where(allowed, 0.0, -1e30)
    for block in range(S // ROWS):
        first = block * ROWS
        low = max(0, (first - LONGEST + 1) // ROWS * ROWS)
        high = first + ROWS
        reach = high - low
        slot = block % 2

        def stacked(ref):
            return jnp.concatenate(
                [ref[0, first:high, h * DH : (h + 1) * DH] for h in range(heads)], axis=0
            )

        grad = stacked(grad_ref)
        logit_ref[slot, :reach] = dot_nt(key_ref[0, low:high], stacked(query_ref))
        prob_grad_ref[slot, :reach] = dot_nt(value_ref[0, low:high], grad)

        def logits(at):
            bias = bias_ref[block, at : at + CHUNK]
            return logit_ref[slot, at : at + CHUNK] + jnp.concatenate([bias] * heads, axis=1)

        lanes = heads * ROWS
        top = jnp.full((8, lanes), -3e38, F32)
        for at in range(0, reach, CHUNK):
            top = jnp.maximum(top, jnp.max(logits(at).reshape(CHUNK // 8, 8, lanes), axis=0))
        row_top = jnp.max(top, axis=0, keepdims=True)
        total = jnp.zeros((8, lanes), F32)
        delta = jnp.zeros((8, lanes), F32)
        for at in range(0, reach, CHUNK):
            terms = jnp.exp2((logits(at) - row_top) * exp_scale)
            total = total + jnp.sum(terms.reshape(CHUNK // 8, 8, lanes), axis=0)
            weighted = terms * prob_grad_ref[slot, at : at + CHUNK]
            delta = delta + jnp.sum(weighted.reshape(CHUNK // 8, 8, lanes), axis=0)
            logit_ref[slot, at : at + CHUNK] = terms
        inverse = 1.0 / jnp.sum(total, axis=0, keepdims=True)
        row_delta = jnp.sum(delta, axis=0, keepdims=True) * inverse
        for at in range(0, reach, CHUNK):
            probs = logit_ref[slot, at : at + CHUNK] * inverse
            prob_ref[slot, at : at + CHUNK] = probs.astype(BF16)
            logit_grad_ref[slot, at : at + CHUNK] = (
                probs * (prob_grad_ref[slot, at : at + CHUNK] - row_delta)
            ).astype(BF16)
        value_sum[low:high] += dot_nn(prob_ref[slot, :reach], grad)
        query_grad = dot_nn(key_t[:, low:high], logit_grad_ref[slot, :reach]) * score_scale
        query_grad = query_grad.astype(BF16)
        for h in range(heads):
            packed_ref[0, h * DH : (h + 1) * DH, first:high] = query_grad[
                :, h * ROWS : (h + 1) * ROWS
            ]

    value_grad = value_sum[...].T.astype(BF16)
    packed_ref[0, width : width + DH] = value_grad
    back_query = dot_nn(up_query_ref[...], packed_ref[0, :width])
    back_value = dot_nn(up_value_ref[...], value_grad)
    send_ref[2 * quarter : 3 * quarter, 0] = back_query.astype(BF16).reshape(quarter, chunk, S)
    send_ref[3 * quarter : parts, 0] = back_value.astype(BF16).reshape(quarter, chunk, S)


def sum_kernel(parts_ref, out_ref):
    total = jnp.sum(parts_ref[...].astype(F32), axis=0)
    out_ref[...] = jnp.broadcast_to(total.astype(BF16)[None], out_ref.shape)


def feature_kernel(lowrank_ref, hidden_ref, packed_ref, out_ref):
    cands = hidden_ref.shape[0]
    width = hidden_ref.shape[2]
    values = slice(width, width + DH)
    tile_rows = slice(width + DH, width + 2 * DH)
    pieces = [[], [], [], []]
    for cand in range(cands):
        lowrank = lowrank_ref[:, cand].reshape(4 * R, S)
        down = dot_nn(lowrank[2 * R :], hidden_ref[cand])
        pieces[0].append(down[:R])
        pieces[1].append(down[R:])
        pieces[2].append(dot_nt(lowrank[:R], packed_ref[cand, :width]))
        pieces[3].append(dot_nt(lowrank[R : 2 * R], packed_ref[cand, values]))
    buckets = KB * NT
    ids = packed_ref[0, width + 2 * DH :].astype(F32)
    ids = (ids[4:8] * KB + ids[0:4]).astype(jnp.int32)
    sums = jnp.zeros((buckets, cands * R), F32)
    for kind in range(4):
        rows = jnp.concatenate(pieces[kind], axis=0).astype(BF16)
        count = rows.shape[1]
        where = lax.broadcasted_iota(jnp.int32, (buckets, count), 0)
        chosen = jnp.where(where == ids[kind : kind + 1, :count], 1.0, 0.0).astype(BF16)
        sums = sums + dot_nt(chosen, rows)
    wide = jnp.concatenate(
        [
            jnp.concatenate(
                [sums[t * KB : (t + 1) * KB, c * R : (c + 1) * R] for t in range(NT)], axis=1
            )
            for c in range(cands)
        ],
        axis=0,
    )
    high = wide.astype(BF16)
    low = (wide - high.astype(F32)).astype(BF16)
    tiles = NT // cands
    bank = jnp.concatenate(
        [
            packed_ref[c, tile_rows, t * PB : (t + 1) * PB]
            for c in range(cands)
            for t in range(tiles)
        ],
        axis=0,
    )
    feats = dot_nn(high, bank) + dot_nn(low, bank)
    out_ref[...] = jnp.broadcast_to(feats.astype(BF16)[None], out_ref.shape)


def score_kernel(place, parts_ref, *refs):
    mine_refs, other_refs, (out_ref, feats_ref) = refs[:2], refs[2:4], refs[4:]
    cands = out_ref.shape[0]
    eights, seeds, depth = mine_refs[0].shape
    per_part = depth // PB
    feats_ref[...] = jnp.sum(parts_ref[...].astype(F32), axis=0)
    totals = [[jnp.zeros((seeds, PB), F32) for _ in range(2)] for _ in range(cands)]
    for at in range(2 * eights):
        source = place[1] ^ (at % 2 * 8 + at // 2 % 2 * 4 + at // 4 % 2 * 2 + at // 8)
        for part in range(per_part):
            feat = [
                feats_ref[pl.ds(c * KB + source * per_part + part, 1), :] for c in range(cands)
            ]
            for half, seeds_ref in enumerate((mine_refs[at // eights], other_refs[at // eights])):
                seed = seeds_ref[at % eights, :, part * PB : (part + 1) * PB].astype(F32)
                for c in range(cands):
                    totals[c][half] = totals[c][half] + feat[c] * seed
    first_core = place[0] == 0
    for c in range(cands):
        mine = feats_ref[c * KB : (c + 1) * KB]
        square = jnp.sum(jnp.sum(mine * mine, axis=0, keepdims=True), axis=1, keepdims=True)
        here, there = totals[c]
        ordered = jnp.concatenate(
            [jnp.where(first_core, here, there), jnp.where(first_core, there, here)], axis=0
        )
        numerator = jnp.sum(ordered.T, axis=0, keepdims=True)
        out_ref[c : c + 1, :] = numerator * lax.rsqrt(square / K + EPS) * K ** (-0.5)


VMEM = pl.BlockSpec(memory_space=pltpu.VMEM)
SMEM = pl.BlockSpec(memory_space=pltpu.SMEM)
PARAMS = pltpu.CompilerParams(vmem_limit_bytes=40 << 20)


def local(
    hidden_in,
    query_act,
    key_act,
    value_act,
    ctx_grad,
    segment_ids,
    down_query,
    up_query,
    down_value,
    up_value,
    block_rows,
    tile_rows,
    block_value,
    tile_value,
    tile_bank,
    seed_feats,
):
    model_index = lax.axis_index("mp")
    data_size = lax.axis_size("dp")
    model_size = lax.axis_size("mp")
    cands, seq_len, width = query_act.shape
    heads = width // DH
    kv = (model_index * heads // (H // KVH)).astype(jnp.int32)
    kv_index = kv.reshape(1)
    seeds_dev = seed_feats.shape[0]
    out_seeds = data_size * seeds_dev // model_size

    levels = data_size // 2

    def to_column(block, flip):
        return lax.ppermute(
            block,
            ("dp", "mp"),
            [
                (d * model_size + m, ((m ^ flip) * 2 + d % 2) * model_size + d // 2)
                for d in range(data_size)
                for m in range(model_size)
            ],
        )

    def from_level(block, flip):
        return lax.ppermute(block, "dp", [(d, d ^ (2 * flip)) for d in range(data_size)])

    def from_core(block):
        return lax.ppermute(block, "dp", [(d, d ^ 1) for d in range(data_size)])

    chunk = 4 * R // model_size
    span = LONGEST + ROWS
    packed_rows = width + 2 * DH + 16
    tiles = NT // cands

    def per_cand(*shape):
        return pl.BlockSpec((1, *shape), lambda c, kv_ref: (c, 0, 0))

    def whole(*shape):
        return pl.BlockSpec(shape, lambda c, kv_ref: (0,) * len(shape))

    send, packed = pl.pallas_call(
        attention_kernel,
        name="attention_backward",
        out_shape=(
            jax.ShapeDtypeStruct((model_size, cands, chunk, seq_len), BF16),
            jax.ShapeDtypeStruct((cands, packed_rows, seq_len), BF16),
        ),
        grid_spec=pltpu.PrefetchScalarGridSpec(
            num_scalar_prefetch=1,
            grid=(cands,),
            in_specs=[
                per_cand(seq_len, hidden_in.shape[2]),
                per_cand(seq_len, width),
                per_cand(seq_len, width),
                pl.BlockSpec((1, seq_len, DH), lambda c, kv_ref: (c, 0, kv_ref[0])),
                pl.BlockSpec((1, seq_len, DH), lambda c, kv_ref: (c, 0, kv_ref[0])),
                whole(cands, seq_len),
                whole(*down_query.shape),
                whole(*down_value.shape),
                whole(*up_query.shape),
                pl.BlockSpec((R, DH), lambda c, kv_ref: (0, kv_ref[0])),
                whole(*block_rows.shape),
                whole(*tile_rows.shape),
                whole(KVH, DH),
                whole(KVH, DH),
                pl.BlockSpec((tiles, R, PB), lambda c, kv_ref: (c, 0, 0)),
            ],
            out_specs=[
                pl.BlockSpec((model_size, 1, chunk, seq_len), lambda c, kv_ref: (0, c, 0, 0)),
                per_cand(packed_rows, seq_len),
            ],
            scratch_shapes=[
                pltpu.VMEM((seq_len, DH), F32),
                pltpu.VMEM((2 * R, hidden_in.shape[2]), BF16),
                pltpu.VMEM((seq_len // ROWS, span, ROWS), F32),
                pltpu.VMEM((2, span, heads * ROWS), F32),
                pltpu.VMEM((2, span, heads * ROWS), F32),
                pltpu.VMEM((2, span, heads * ROWS), BF16),
                pltpu.VMEM((2, span, heads * ROWS), BF16),
            ],
        ),
        compiler_params=pltpu.CompilerParams(vmem_limit_bytes=60 << 20),
        cost_estimate=pl.CostEstimate(
            flops=5_000_000_000, bytes_accessed=8_000_000, transcendentals=2_000_000
        ),
    )(
        kv_index,
        hidden_in,
        query_act,
        ctx_grad,
        key_act,
        value_act,
        segment_ids,
        down_query,
        down_value,
        up_query,
        up_value,
        block_rows,
        tile_rows,
        block_value.reshape(KVH, DH),
        tile_value.reshape(KVH, DH),
        tile_bank,
    )

    send, seeds_own = lax.optimization_barrier((send, seed_feats))
    received = lax.all_to_all(send, "mp", 0, 0, tiled=True)
    half, quarter = levels // 2, levels // 4
    moved = [to_column(seeds_own, flip) for flip in (0, half, quarter, half + quarter)]
    received, *moved = lax.optimization_barrier((received, *moved))
    summed = pl.pallas_call(
        sum_kernel,
        name="lowrank_sum",
        out_shape=jax.ShapeDtypeStruct(received.shape, BF16),
        in_specs=[VMEM],
        out_specs=VMEM,
        compiler_params=PARAMS,
    )(received)
    lowrank = lax.all_to_all(summed, "mp", 0, 0, tiled=True)
    four = jnp.stack(moved)
    four_more = from_level(four, 2)
    lowrank, four, four_more = lax.optimization_barrier((lowrank, four, four_more))
    eight = jnp.concatenate([four, four_more])
    eight_more = from_level(eight, 1)

    feat_parts = pl.pallas_call(
        feature_kernel,
        name="partial_features",
        out_shape=jax.ShapeDtypeStruct((model_size, cands * KB, PB), BF16),
        in_specs=[VMEM] * 3,
        out_specs=VMEM,
        compiler_params=PARAMS,
    )(lowrank, hidden_in, packed)
    feat_parts, eight = lax.optimization_barrier((feat_parts, eight))
    feat_all = lax.all_to_all(feat_parts, "mp", 0, 0, tiled=True)
    other = [from_core(part) for part in (eight, eight_more)]
    place = jnp.stack([lax.axis_index("dp") % 2, lax.axis_index("dp") // 2]).astype(jnp.int32)

    return pl.pallas_call(
        score_kernel,
        name="scores",
        out_shape=jax.ShapeDtypeStruct((cands, out_seeds), F32),
        in_specs=[SMEM] + [VMEM] * 5,
        out_specs=VMEM,
        scratch_shapes=[pltpu.VMEM((cands * KB, PB), F32)],
        compiler_params=PARAMS,
    )(place, feat_all, eight, eight_more, *other)


def solution(mesh):
    return jax.shard_map(
        local,
        mesh=mesh,
        in_specs=(
            P("dp", None, "mp"),
            P("dp", None, "mp"),
            P("dp", None, None),
            P("dp", None, None),
            P("dp", None, "mp"),
            P("dp", None),
            P("mp", None),
            P(None, "mp"),
            P("mp", None),
            P(),
            P(None, "mp"),
            P(None, "mp"),
            P(),
            P(),
            P(),
            P("dp", "mp"),
        ),
        out_specs=P("dp", "mp"),
        check_vma=False,
    )
```

```python
import math

import jax
import jax.numpy as jnp
from jax import lax
from jax.experimental import pallas as pl
from jax.experimental.pallas import tpu as pltpu
from jax.sharding import PartitionSpec as P

H = 64
KVH = 8
DH = 128
R = 128
K = 8192
PB = 128
NT = 8
S = 512
KB = 64
EPS = 1e-06
LONGEST = 256
ROWS = 128
CHUNK = 32
F32 = jnp.float32
BF16 = jnp.bfloat16


def dot_nn(a, b):
    return lax.dot_general(a, b, (((1,), (0,)), ((), ())), preferred_element_type=F32)


def dot_nt(a, b):
    return lax.dot_general(a, b, (((1,), (1,)), ((), ())), preferred_element_type=F32)


def attention_kernel(
    kv_index,
    hidden_ref,
    query_ref,
    grad_ref,
    key_ref,
    value_ref,
    segment_ref,
    down_query_ref,
    down_value_ref,
    up_query_ref,
    up_value_ref,
    block_ref,
    tile_ref,
    block_value_ref,
    tile_value_ref,
    bank_ref,
    send_ref,
    packed_ref,
    value_sum,
    down_t,
    bias_ref,
    logit_ref,
    prob_grad_ref,
    prob_ref,
    logit_grad_ref,
):
    cand = pl.program_id(0)
    parts = send_ref.shape[0]
    chunk = send_ref.shape[2]
    quarter = R // chunk
    heads = query_ref.shape[2] // DH
    score_scale = 1.0 / math.sqrt(DH)
    exp_scale = score_scale * math.log2(math.e)

    @pl.when(cand == 0)
    def _():
        down_t[:R] = down_query_ref[...].T
        down_t[R:] = down_value_ref[...].T

    width = heads * DH
    kv = kv_index[0]
    for tile in range(bank_ref.shape[0]):
        packed_ref[0, width + DH : width + 2 * DH, tile * PB : (tile + 1) * PB] = bank_ref[tile]
    ids = [
        block_ref[...],
        jnp.concatenate([block_value_ref[pl.ds(kv, 1), :]] * heads, axis=1),
        tile_ref[...],
        jnp.concatenate([tile_value_ref[pl.ds(kv, 1), :]] * heads, axis=1),
        jnp.zeros((8, width), jnp.int32),
    ]
    ids = jnp.concatenate(ids, axis=0).astype(F32).astype(BF16)
    packed_ref[0, width + 2 * DH :] = ids

    lowrank_in = dot_nt(down_t[...], hidden_ref[0])
    send_ref[0 : 2 * quarter, 0] = lowrank_in.astype(BF16).reshape(2 * quarter, chunk, S)

    segment_row = segment_ref[pl.ds(cand, 1), :].astype(F32)
    segment_col = jnp.broadcast_to(segment_row, (8, S)).T[:, 0:1]
    key_t = key_ref[0].T
    value_sum[...] = jnp.zeros_like(value_sum)

    for block in range(S // ROWS):
        first = block * ROWS
        low = max(0, (first - LONGEST + 1) // ROWS * ROWS)
        high = first + ROWS
        reach = high - low
        for at in range(0, reach, ROWS):
            allowed = segment_col[low + at : low + at + ROWS] == segment_row[:, first:high]
            if low + at == first:
                key_pos = lax.broadcasted_iota(jnp.int32, (ROWS, ROWS), 0)
                row_pos = lax.broadcasted_iota(jnp.int32, (ROWS, ROWS), 1)
                allowed = allowed & (key_pos <= row_pos)
            bias_ref[block, at : at + ROWS] = jnp.where(allowed, 0.0, -1e30)
    for block in range(S // ROWS):
        first = block * ROWS
        low = max(0, (first - LONGEST + 1) // ROWS * ROWS)
        high = first + ROWS
        reach = high - low
        slot = block % 2

        def stacked(ref):
            return jnp.concatenate(
                [ref[0, first:high, h * DH : (h + 1) * DH] for h in range(heads)], axis=0
            )

        grad = stacked(grad_ref)
        logit_ref[slot, :reach] = dot_nt(key_ref[0, low:high], stacked(query_ref))
        prob_grad_ref[slot, :reach] = dot_nt(value_ref[0, low:high], grad)

        def logits(at):
            bias = bias_ref[block, at : at + CHUNK]
            return logit_ref[slot, at : at + CHUNK] + jnp.concatenate([bias] * heads, axis=1)

        lanes = heads * ROWS
        top = jnp.full((8, lanes), -3e38, F32)
        for at in range(0, reach, CHUNK):
            top = jnp.maximum(top, jnp.max(logits(at).reshape(CHUNK // 8, 8, lanes), axis=0))
        row_top = jnp.max(top, axis=0, keepdims=True)
        total = jnp.zeros((8, lanes), F32)
        delta = jnp.zeros((8, lanes), F32)
        for at in range(0, reach, CHUNK):
            terms = jnp.exp2((logits(at) - row_top) * exp_scale)
            total = total + jnp.sum(terms.reshape(CHUNK // 8, 8, lanes), axis=0)
            weighted = terms * prob_grad_ref[slot, at : at + CHUNK]
            delta = delta + jnp.sum(weighted.reshape(CHUNK // 8, 8, lanes), axis=0)
            logit_ref[slot, at : at + CHUNK] = terms
        inverse = 1.0 / jnp.sum(total, axis=0, keepdims=True)
        row_delta = jnp.sum(delta, axis=0, keepdims=True) * inverse
        for at in range(0, reach, CHUNK):
            probs = logit_ref[slot, at : at + CHUNK] * inverse
            prob_ref[slot, at : at + CHUNK] = probs.astype(BF16)
            logit_grad_ref[slot, at : at + CHUNK] = (
                probs * (prob_grad_ref[slot, at : at + CHUNK] - row_delta)
            ).astype(BF16)
        value_sum[low:high] += dot_nn(prob_ref[slot, :reach], grad)
        query_grad = dot_nn(key_t[:, low:high], logit_grad_ref[slot, :reach]) * score_scale
        query_grad = query_grad.astype(BF16)
        for h in range(heads):
            packed_ref[0, h * DH : (h + 1) * DH, first:high] = query_grad[
                :, h * ROWS : (h + 1) * ROWS
            ]

    value_grad = value_sum[...].T.astype(BF16)
    packed_ref[0, width : width + DH] = value_grad
    back_query = dot_nn(up_query_ref[...], packed_ref[0, :width])
    back_value = dot_nn(up_value_ref[...], value_grad)
    send_ref[2 * quarter : 3 * quarter, 0] = back_query.astype(BF16).reshape(quarter, chunk, S)
    send_ref[3 * quarter : parts, 0] = back_value.astype(BF16).reshape(quarter, chunk, S)


def sum_kernel(parts_ref, out_ref):
    total = jnp.sum(parts_ref[...].astype(F32), axis=0)
    out_ref[...] = jnp.broadcast_to(total.astype(BF16)[None], out_ref.shape)


def feature_kernel(lowrank_ref, hidden_ref, packed_ref, out_ref):
    cands = hidden_ref.shape[0]
    width = hidden_ref.shape[2]
    values = slice(width, width + DH)
    tile_rows = slice(width + DH, width + 2 * DH)
    pieces = [[], [], [], []]
    for cand in range(cands):
        lowrank = lowrank_ref[:, cand].reshape(4 * R, S)
        down = dot_nn(lowrank[2 * R :], hidden_ref[cand])
        pieces[0].append(down[:R])
        pieces[1].append(down[R:])
        pieces[2].append(dot_nt(lowrank[:R], packed_ref[cand, :width]))
        pieces[3].append(dot_nt(lowrank[R : 2 * R], packed_ref[cand, values]))
    buckets = KB * NT
    ids = packed_ref[0, width + 2 * DH :].astype(F32)
    ids = (ids[4:8] * KB + ids[0:4]).astype(jnp.int32)
    sums = jnp.zeros((buckets, cands * R), F32)
    for kind in range(4):
        rows = jnp.concatenate(pieces[kind], axis=0).astype(BF16)
        count = rows.shape[1]
        where = lax.broadcasted_iota(jnp.int32, (buckets, count), 0)
        chosen = jnp.where(where == ids[kind : kind + 1, :count], 1.0, 0.0).astype(BF16)
        sums = sums + dot_nt(chosen, rows)
    wide = jnp.concatenate(
        [
            jnp.concatenate(
                [sums[t * KB : (t + 1) * KB, c * R : (c + 1) * R] for t in range(NT)], axis=1
            )
            for c in range(cands)
        ],
        axis=0,
    )
    high = wide.astype(BF16)
    low = (wide - high.astype(F32)).astype(BF16)
    tiles = NT // cands
    bank = jnp.concatenate(
        [
            packed_ref[c, tile_rows, t * PB : (t + 1) * PB]
            for c in range(cands)
            for t in range(tiles)
        ],
        axis=0,
    )
    feats = dot_nn(high, bank) + dot_nn(low, bank)
    out_ref[...] = jnp.broadcast_to(feats.astype(BF16)[None], out_ref.shape)


def score_kernel(place, parts_ref, *refs):
    mine_refs, other_refs, (out_ref, feats_ref) = refs[:2], refs[2:4], refs[4:]
    cands = out_ref.shape[0]
    eights, seeds, depth = mine_refs[0].shape
    per_part = depth // PB
    feats_ref[...] = jnp.sum(parts_ref[...].astype(F32), axis=0)
    totals = [[jnp.zeros((seeds, PB), F32) for _ in range(2)] for _ in range(cands)]
    for at in range(2 * eights):
        source = place[1] ^ (at % 2 * 8 + at // 2 % 2 * 4 + at // 4 % 2 * 2 + at // 8)
        for part in range(per_part):
            feat = [
                feats_ref[pl.ds(c * KB + source * per_part + part, 1), :] for c in range(cands)
            ]
            for half, seeds_ref in enumerate((mine_refs[at // eights], other_refs[at // eights])):
                seed = seeds_ref[at % eights, :, part * PB : (part + 1) * PB].astype(F32)
                for c in range(cands):
                    totals[c][half] = totals[c][half] + feat[c] * seed
    first_core = place[0] == 0
    for c in range(cands):
        mine = feats_ref[c * KB : (c + 1) * KB]
        square = jnp.sum(jnp.sum(mine * mine, axis=0, keepdims=True), axis=1, keepdims=True)
        here, there = totals[c]
        ordered = jnp.concatenate(
            [jnp.where(first_core, here, there), jnp.where(first_core, there, here)], axis=0
        )
        numerator = jnp.sum(ordered.T, axis=0, keepdims=True)
        out_ref[c : c + 1, :] = numerator * lax.rsqrt(square / K + EPS) * K ** (-0.5)


VMEM = pl.BlockSpec(memory_space=pltpu.VMEM)
SMEM = pl.BlockSpec(memory_space=pltpu.SMEM)
PARAMS = pltpu.CompilerParams(vmem_limit_bytes=40 << 20)


def local(
    hidden_in,
    query_act,
    key_act,
    value_act,
    ctx_grad,
    segment_ids,
    down_query,
    up_query,
    down_value,
    up_value,
    block_rows,
    tile_rows,
    block_value,
    tile_value,
    tile_bank,
    seed_feats,
):
    model_index = lax.axis_index("mp")
    data_size = lax.axis_size("dp")
    model_size = lax.axis_size("mp")
    cands, seq_len, width = query_act.shape
    heads = width // DH
    kv = (model_index * heads // (H // KVH)).astype(jnp.int32)
    kv_index = kv.reshape(1)
    seeds_dev = seed_feats.shape[0]
    out_seeds = data_size * seeds_dev // model_size

    levels = data_size // 2

    def to_column(flip):
        return lax.ppermute(
            seed_feats,
            ("dp", "mp"),
            [
                (d * model_size + m, ((m ^ flip) * 2 + d % 2) * model_size + d // 2)
                for d in range(data_size)
                for m in range(model_size)
            ],
        )

    def from_level(block, flip):
        return lax.ppermute(block, "dp", [(d, d ^ (2 * flip)) for d in range(data_size)])

    def from_core(block):
        return lax.ppermute(block, "dp", [(d, d ^ 1) for d in range(data_size)])

    seed_near, seed_far = to_column(0), to_column(levels // 2)
    chunk = 4 * R // model_size
    span = LONGEST + ROWS
    packed_rows = width + 2 * DH + 16
    tiles = NT // cands

    def per_cand(*shape):
        return pl.BlockSpec((1, *shape), lambda c, kv_ref: (c, 0, 0))

    def whole(*shape):
        return pl.BlockSpec(shape, lambda c, kv_ref: (0,) * len(shape))

    send, packed = pl.pallas_call(
        attention_kernel,
        name="attention_backward",
        out_shape=(
            jax.ShapeDtypeStruct((model_size, cands, chunk, seq_len), BF16),
            jax.ShapeDtypeStruct((cands, packed_rows, seq_len), BF16),
        ),
        grid_spec=pltpu.PrefetchScalarGridSpec(
            num_scalar_prefetch=1,
            grid=(cands,),
            in_specs=[
                per_cand(seq_len, hidden_in.shape[2]),
                per_cand(seq_len, width),
                per_cand(seq_len, width),
                pl.BlockSpec((1, seq_len, DH), lambda c, kv_ref: (c, 0, kv_ref[0])),
                pl.BlockSpec((1, seq_len, DH), lambda c, kv_ref: (c, 0, kv_ref[0])),
                whole(cands, seq_len),
                whole(*down_query.shape),
                whole(*down_value.shape),
                whole(*up_query.shape),
                pl.BlockSpec((R, DH), lambda c, kv_ref: (0, kv_ref[0])),
                whole(*block_rows.shape),
                whole(*tile_rows.shape),
                whole(KVH, DH),
                whole(KVH, DH),
                pl.BlockSpec((tiles, R, PB), lambda c, kv_ref: (c, 0, 0)),
            ],
            out_specs=[
                pl.BlockSpec((model_size, 1, chunk, seq_len), lambda c, kv_ref: (0, c, 0, 0)),
                per_cand(packed_rows, seq_len),
            ],
            scratch_shapes=[
                pltpu.VMEM((seq_len, DH), F32),
                pltpu.VMEM((2 * R, hidden_in.shape[2]), BF16),
                pltpu.VMEM((seq_len // ROWS, span, ROWS), F32),
                pltpu.VMEM((2, span, heads * ROWS), F32),
                pltpu.VMEM((2, span, heads * ROWS), F32),
                pltpu.VMEM((2, span, heads * ROWS), BF16),
                pltpu.VMEM((2, span, heads * ROWS), BF16),
            ],
        ),
        compiler_params=pltpu.CompilerParams(vmem_limit_bytes=60 << 20),
        cost_estimate=pl.CostEstimate(
            flops=5_000_000_000, bytes_accessed=8_000_000, transcendentals=2_000_000
        ),
    )(
        kv_index,
        hidden_in,
        query_act,
        ctx_grad,
        key_act,
        value_act,
        segment_ids,
        down_query,
        down_value,
        up_query,
        up_value,
        block_rows,
        tile_rows,
        block_value.reshape(KVH, DH),
        tile_value.reshape(KVH, DH),
        tile_bank,
    )

    send, seed_near, seed_far = lax.optimization_barrier((send, seed_near, seed_far))
    received = lax.all_to_all(send, "mp", 0, 0, tiled=True)
    two = jnp.stack([seed_near, seed_far])
    two_more = from_level(two, 4)
    received, two, two_more = lax.optimization_barrier((received, two, two_more))
    summed = pl.pallas_call(
        sum_kernel,
        name="lowrank_sum",
        out_shape=jax.ShapeDtypeStruct(received.shape, BF16),
        in_specs=[VMEM],
        out_specs=VMEM,
        compiler_params=PARAMS,
    )(received)
    lowrank = lax.all_to_all(summed, "mp", 0, 0, tiled=True)
    four = jnp.concatenate([two, two_more])
    four_more = from_level(four, 2)
    eight = jnp.concatenate([four, four_more])
    eight_more = from_level(eight, 1)

    feat_parts = pl.pallas_call(
        feature_kernel,
        name="partial_features",
        out_shape=jax.ShapeDtypeStruct((model_size, cands * KB, PB), BF16),
        in_specs=[VMEM] * 3,
        out_specs=VMEM,
        compiler_params=PARAMS,
    )(lowrank, hidden_in, packed)
    feat_parts, eight = lax.optimization_barrier((feat_parts, eight))
    feat_all = lax.all_to_all(feat_parts, "mp", 0, 0, tiled=True)
    other = [from_core(part) for part in (eight, eight_more)]
    place = jnp.stack([lax.axis_index("dp") % 2, lax.axis_index("dp") // 2]).astype(jnp.int32)

    return pl.pallas_call(
        score_kernel,
        name="scores",
        out_shape=jax.ShapeDtypeStruct((cands, out_seeds), F32),
        in_specs=[SMEM] + [VMEM] * 5,
        out_specs=VMEM,
        scratch_shapes=[pltpu.VMEM((cands * KB, PB), F32)],
        compiler_params=PARAMS,
    )(place, feat_all, eight, eight_more, *other)


def solution(mesh):
    return jax.shard_map(
        local,
        mesh=mesh,
        in_specs=(
            P("dp", None, "mp"),
            P("dp", None, "mp"),
            P("dp", None, None),
            P("dp", None, None),
            P("dp", None, "mp"),
            P("dp", None),
            P("mp", None),
            P(None, "mp"),
            P("mp", None),
            P(),
            P(None, "mp"),
            P(None, "mp"),
            P(),
            P(),
            P(),
            P("dp", "mp"),
        ),
        out_specs=P("dp", "mp"),
        check_vma=False,
    )
```

```python
import math

import jax
import jax.numpy as jnp
from jax import lax
from jax.experimental import pallas as pl
from jax.experimental.pallas import tpu as pltpu
from jax.sharding import PartitionSpec as P

H = 64
KVH = 8
DH = 128
R = 128
K = 8192
PB = 128
NT = 8
S = 512
KB = 64
EPS = 1e-06
LONGEST = 256
ROWS = 128
CHUNK = 32
F32 = jnp.float32
BF16 = jnp.bfloat16


def dot_nn(a, b):
    return lax.dot_general(a, b, (((1,), (0,)), ((), ())), preferred_element_type=F32)


def dot_nt(a, b):
    return lax.dot_general(a, b, (((1,), (1,)), ((), ())), preferred_element_type=F32)


def attention_kernel(
    kv_index,
    hidden_ref,
    query_ref,
    grad_ref,
    key_ref,
    value_ref,
    segment_ref,
    down_query_ref,
    down_value_ref,
    up_query_ref,
    up_value_ref,
    block_ref,
    tile_ref,
    block_value_ref,
    tile_value_ref,
    bank_ref,
    send_ref,
    packed_ref,
    value_sum,
    down_t,
    bias_ref,
    logit_ref,
    prob_grad_ref,
    prob_ref,
    logit_grad_ref,
):
    cand = pl.program_id(0)
    parts = send_ref.shape[0]
    chunk = send_ref.shape[2]
    quarter = R // chunk
    heads = query_ref.shape[2] // DH
    score_scale = 1.0 / math.sqrt(DH)
    exp_scale = score_scale * math.log2(math.e)

    @pl.when(cand == 0)
    def _():
        down_t[:R] = down_query_ref[...].T
        down_t[R:] = down_value_ref[...].T

    width = heads * DH
    kv = kv_index[0]
    for tile in range(bank_ref.shape[0]):
        packed_ref[0, width + DH : width + 2 * DH, tile * PB : (tile + 1) * PB] = bank_ref[tile]
    ids = [
        block_ref[...],
        jnp.concatenate([block_value_ref[pl.ds(kv, 1), :]] * heads, axis=1),
        tile_ref[...],
        jnp.concatenate([tile_value_ref[pl.ds(kv, 1), :]] * heads, axis=1),
        jnp.zeros((8, width), jnp.int32),
    ]
    ids = jnp.concatenate(ids, axis=0).astype(F32).astype(BF16)
    packed_ref[0, width + 2 * DH :] = ids

    lowrank_in = dot_nt(down_t[...], hidden_ref[0])
    send_ref[0 : 2 * quarter, 0] = lowrank_in.astype(BF16).reshape(2 * quarter, chunk, S)

    segment_row = segment_ref[pl.ds(cand, 1), :].astype(F32)
    segment_col = jnp.broadcast_to(segment_row, (8, S)).T[:, 0:1]
    key_t = key_ref[0].T
    value_sum[...] = jnp.zeros_like(value_sum)

    for block in range(S // ROWS):
        first = block * ROWS
        low = max(0, (first - LONGEST + 1) // ROWS * ROWS)
        high = first + ROWS
        reach = high - low
        for at in range(0, reach, ROWS):
            allowed = segment_col[low + at : low + at + ROWS] == segment_row[:, first:high]
            if low + at == first:
                key_pos = lax.broadcasted_iota(jnp.int32, (ROWS, ROWS), 0)
                row_pos = lax.broadcasted_iota(jnp.int32, (ROWS, ROWS), 1)
                allowed = allowed & (key_pos <= row_pos)
            bias_ref[block, at : at + ROWS] = jnp.where(allowed, 0.0, -1e30)
    for block in range(S // ROWS):
        first = block * ROWS
        low = max(0, (first - LONGEST + 1) // ROWS * ROWS)
        high = first + ROWS
        reach = high - low
        slot = block % 2

        def stacked(ref):
            return jnp.concatenate(
                [ref[0, first:high, h * DH : (h + 1) * DH] for h in range(heads)], axis=0
            )

        grad = stacked(grad_ref)
        logit_ref[slot, :reach] = dot_nt(key_ref[0, low:high], stacked(query_ref))
        prob_grad_ref[slot, :reach] = dot_nt(value_ref[0, low:high], grad)

        def logits(at):
            bias = bias_ref[block, at : at + CHUNK]
            return logit_ref[slot, at : at + CHUNK] + jnp.concatenate([bias] * heads, axis=1)

        lanes = heads * ROWS
        top = jnp.full((8, lanes), -3e38, F32)
        for at in range(0, reach, CHUNK):
            top = jnp.maximum(top, jnp.max(logits(at).reshape(CHUNK // 8, 8, lanes), axis=0))
        row_top = jnp.max(top, axis=0, keepdims=True)
        total = jnp.zeros((8, lanes), F32)
        delta = jnp.zeros((8, lanes), F32)
        for at in range(0, reach, CHUNK):
            terms = jnp.exp2((logits(at) - row_top) * exp_scale)
            total = total + jnp.sum(terms.reshape(CHUNK // 8, 8, lanes), axis=0)
            weighted = terms * prob_grad_ref[slot, at : at + CHUNK]
            delta = delta + jnp.sum(weighted.reshape(CHUNK // 8, 8, lanes), axis=0)
            logit_ref[slot, at : at + CHUNK] = terms
        inverse = 1.0 / jnp.sum(total, axis=0, keepdims=True)
        row_delta = jnp.sum(delta, axis=0, keepdims=True) * inverse
        for at in range(0, reach, CHUNK):
            probs = logit_ref[slot, at : at + CHUNK] * inverse
            prob_ref[slot, at : at + CHUNK] = probs.astype(BF16)
            logit_grad_ref[slot, at : at + CHUNK] = (
                probs * (prob_grad_ref[slot, at : at + CHUNK] - row_delta)
            ).astype(BF16)
        value_sum[low:high] += dot_nn(prob_ref[slot, :reach], grad)
        query_grad = dot_nn(key_t[:, low:high], logit_grad_ref[slot, :reach]) * score_scale
        query_grad = query_grad.astype(BF16)
        for h in range(heads):
            packed_ref[0, h * DH : (h + 1) * DH, first:high] = query_grad[
                :, h * ROWS : (h + 1) * ROWS
            ]

    value_grad = value_sum[...].T.astype(BF16)
    packed_ref[0, width : width + DH] = value_grad
    back_query = dot_nn(up_query_ref[...], packed_ref[0, :width])
    back_value = dot_nn(up_value_ref[...], value_grad)
    send_ref[2 * quarter : 3 * quarter, 0] = back_query.astype(BF16).reshape(quarter, chunk, S)
    send_ref[3 * quarter : parts, 0] = back_value.astype(BF16).reshape(quarter, chunk, S)


def sum_kernel(parts_ref, out_ref):
    total = jnp.sum(parts_ref[...].astype(F32), axis=0)
    out_ref[...] = jnp.broadcast_to(total.astype(BF16)[None], out_ref.shape)


def stage_kernel(hidden_ref, packed_ref, out_ref):
    out_ref[...] = hidden_ref[...]


def feature_kernel(lowrank_ref, hidden_ref, packed_ref, out_ref):
    cands = hidden_ref.shape[0]
    width = hidden_ref.shape[2]
    values = slice(width, width + DH)
    tile_rows = slice(width + DH, width + 2 * DH)
    pieces = [[], [], [], []]
    for cand in range(cands):
        lowrank = lowrank_ref[:, cand].reshape(4 * R, S)
        down = dot_nn(lowrank[2 * R :], hidden_ref[cand])
        pieces[0].append(down[:R])
        pieces[1].append(down[R:])
        pieces[2].append(dot_nt(lowrank[:R], packed_ref[cand, :width]))
        pieces[3].append(dot_nt(lowrank[R : 2 * R], packed_ref[cand, values]))
    buckets = KB * NT
    ids = packed_ref[0, width + 2 * DH :].astype(F32)
    ids = (ids[4:8] * KB + ids[0:4]).astype(jnp.int32)
    sums = jnp.zeros((buckets, cands * R), F32)
    for kind in range(4):
        rows = jnp.concatenate(pieces[kind], axis=0).astype(BF16)
        count = rows.shape[1]
        where = lax.broadcasted_iota(jnp.int32, (buckets, count), 0)
        chosen = jnp.where(where == ids[kind : kind + 1, :count], 1.0, 0.0).astype(BF16)
        sums = sums + dot_nt(chosen, rows)
    wide = jnp.concatenate(
        [
            jnp.concatenate(
                [sums[t * KB : (t + 1) * KB, c * R : (c + 1) * R] for t in range(NT)], axis=1
            )
            for c in range(cands)
        ],
        axis=0,
    )
    high = wide.astype(BF16)
    low = (wide - high.astype(F32)).astype(BF16)
    tiles = NT // cands
    bank = jnp.concatenate(
        [
            packed_ref[c, tile_rows, t * PB : (t + 1) * PB]
            for c in range(cands)
            for t in range(tiles)
        ],
        axis=0,
    )
    feats = dot_nn(high, bank) + dot_nn(low, bank)
    out_ref[...] = jnp.broadcast_to(feats.astype(BF16)[None], out_ref.shape)


def score_kernel(place, parts_ref, *refs):
    mine_refs, other_refs, (out_ref, feats_ref) = refs[:2], refs[2:4], refs[4:]
    cands = out_ref.shape[0]
    eights, seeds, depth = mine_refs[0].shape
    per_part = depth // PB
    feats_ref[...] = jnp.sum(parts_ref[...].astype(F32), axis=0)
    totals = [[jnp.zeros((seeds, PB), F32) for _ in range(2)] for _ in range(cands)]
    for at in range(2 * eights):
        source = place[1] ^ (at % 2 * 8 + at // 2 % 2 * 4 + at // 4 % 2 * 2 + at // 8)
        for part in range(per_part):
            feat = [
                feats_ref[pl.ds(c * KB + source * per_part + part, 1), :] for c in range(cands)
            ]
            for half, seeds_ref in enumerate((mine_refs[at // eights], other_refs[at // eights])):
                seed = seeds_ref[at % eights, :, part * PB : (part + 1) * PB].astype(F32)
                for c in range(cands):
                    totals[c][half] = totals[c][half] + feat[c] * seed
    first_core = place[0] == 0
    for c in range(cands):
        mine = feats_ref[c * KB : (c + 1) * KB]
        square = jnp.sum(jnp.sum(mine * mine, axis=0, keepdims=True), axis=1, keepdims=True)
        here, there = totals[c]
        ordered = jnp.concatenate(
            [jnp.where(first_core, here, there), jnp.where(first_core, there, here)], axis=0
        )
        numerator = jnp.sum(ordered.T, axis=0, keepdims=True)
        out_ref[c : c + 1, :] = numerator * lax.rsqrt(square / K + EPS) * K ** (-0.5)


VMEM = pl.BlockSpec(memory_space=pltpu.VMEM)
SMEM = pl.BlockSpec(memory_space=pltpu.SMEM)
PARAMS = pltpu.CompilerParams(vmem_limit_bytes=40 << 20)


def local(
    hidden_in,
    query_act,
    key_act,
    value_act,
    ctx_grad,
    segment_ids,
    down_query,
    up_query,
    down_value,
    up_value,
    block_rows,
    tile_rows,
    block_value,
    tile_value,
    tile_bank,
    seed_feats,
):
    model_index = lax.axis_index("mp")
    data_size = lax.axis_size("dp")
    model_size = lax.axis_size("mp")
    cands, seq_len, width = query_act.shape
    heads = width // DH
    kv = (model_index * heads // (H // KVH)).astype(jnp.int32)
    kv_index = kv.reshape(1)
    seeds_dev = seed_feats.shape[0]
    out_seeds = data_size * seeds_dev // model_size

    levels = data_size // 2

    def to_column(flip):
        return lax.ppermute(
            seed_feats,
            ("dp", "mp"),
            [
                (d * model_size + m, ((m ^ flip) * 2 + d % 2) * model_size + d // 2)
                for d in range(data_size)
                for m in range(model_size)
            ],
        )

    def from_level(block, flip):
        return lax.ppermute(block, "dp", [(d, d ^ (2 * flip)) for d in range(data_size)])

    def from_core(block):
        return lax.ppermute(block, "dp", [(d, d ^ 1) for d in range(data_size)])

    seed_near, seed_far = to_column(0), to_column(levels // 2)
    chunk = 4 * R // model_size
    span = LONGEST + ROWS
    packed_rows = width + 2 * DH + 16
    tiles = NT // cands

    def per_cand(*shape):
        return pl.BlockSpec((1, *shape), lambda c, kv_ref: (c, 0, 0))

    def whole(*shape):
        return pl.BlockSpec(shape, lambda c, kv_ref: (0,) * len(shape))

    send, packed = pl.pallas_call(
        attention_kernel,
        name="attention_backward",
        out_shape=(
            jax.ShapeDtypeStruct((model_size, cands, chunk, seq_len), BF16),
            jax.ShapeDtypeStruct((cands, packed_rows, seq_len), BF16),
        ),
        grid_spec=pltpu.PrefetchScalarGridSpec(
            num_scalar_prefetch=1,
            grid=(cands,),
            in_specs=[
                per_cand(seq_len, hidden_in.shape[2]),
                per_cand(seq_len, width),
                per_cand(seq_len, width),
                pl.BlockSpec((1, seq_len, DH), lambda c, kv_ref: (c, 0, kv_ref[0])),
                pl.BlockSpec((1, seq_len, DH), lambda c, kv_ref: (c, 0, kv_ref[0])),
                whole(cands, seq_len),
                whole(*down_query.shape),
                whole(*down_value.shape),
                whole(*up_query.shape),
                pl.BlockSpec((R, DH), lambda c, kv_ref: (0, kv_ref[0])),
                whole(*block_rows.shape),
                whole(*tile_rows.shape),
                whole(KVH, DH),
                whole(KVH, DH),
                pl.BlockSpec((tiles, R, PB), lambda c, kv_ref: (c, 0, 0)),
            ],
            out_specs=[
                pl.BlockSpec((model_size, 1, chunk, seq_len), lambda c, kv_ref: (0, c, 0, 0)),
                per_cand(packed_rows, seq_len),
            ],
            scratch_shapes=[
                pltpu.VMEM((seq_len, DH), F32),
                pltpu.VMEM((2 * R, hidden_in.shape[2]), BF16),
                pltpu.VMEM((seq_len // ROWS, span, ROWS), F32),
                pltpu.VMEM((2, span, heads * ROWS), F32),
                pltpu.VMEM((2, span, heads * ROWS), F32),
                pltpu.VMEM((2, span, heads * ROWS), BF16),
                pltpu.VMEM((2, span, heads * ROWS), BF16),
            ],
        ),
        compiler_params=pltpu.CompilerParams(vmem_limit_bytes=60 << 20),
        cost_estimate=pl.CostEstimate(
            flops=5_000_000_000, bytes_accessed=8_000_000, transcendentals=2_000_000
        ),
    )(
        kv_index,
        hidden_in,
        query_act,
        ctx_grad,
        key_act,
        value_act,
        segment_ids,
        down_query,
        down_value,
        up_query,
        up_value,
        block_rows,
        tile_rows,
        block_value.reshape(KVH, DH),
        tile_value.reshape(KVH, DH),
        tile_bank,
    )

    send, seed_near, seed_far = lax.optimization_barrier((send, seed_near, seed_far))
    received = lax.all_to_all(send, "mp", 0, 0, tiled=True)
    two = jnp.stack([seed_near, seed_far])
    two_more = from_level(two, 4)
    received, two, two_more, hidden_later, packed = lax.optimization_barrier(
        (received, two, two_more, hidden_in, packed)
    )
    summed = pl.pallas_call(
        sum_kernel,
        name="lowrank_sum",
        out_shape=jax.ShapeDtypeStruct(received.shape, BF16),
        in_specs=[VMEM],
        out_specs=VMEM,
        compiler_params=PARAMS,
    )(received)
    lowrank = lax.all_to_all(summed, "mp", 0, 0, tiled=True)
    four = jnp.concatenate([two, two_more])
    four_more = from_level(four, 2)
    eight = jnp.concatenate([four, four_more])
    eight_more = from_level(eight, 1)

    hidden_near = pl.pallas_call(
        stage_kernel,
        name="stage_operands",
        out_shape=jax.ShapeDtypeStruct(hidden_in.shape, BF16),
        in_specs=[VMEM] * 2,
        out_specs=VMEM,
        compiler_params=PARAMS,
        cost_estimate=pl.CostEstimate(
            flops=10_000_000, bytes_accessed=4_000_000, transcendentals=0
        ),
    )(hidden_later, packed)
    feat_parts = pl.pallas_call(
        feature_kernel,
        name="partial_features",
        out_shape=jax.ShapeDtypeStruct((model_size, cands * KB, PB), BF16),
        in_specs=[VMEM] * 3,
        out_specs=VMEM,
        compiler_params=PARAMS,
    )(lowrank, hidden_near, packed)
    feat_parts, eight = lax.optimization_barrier((feat_parts, eight))
    feat_all = lax.all_to_all(feat_parts, "mp", 0, 0, tiled=True)
    other = [from_core(part) for part in (eight, eight_more)]
    place = jnp.stack([lax.axis_index("dp") % 2, lax.axis_index("dp") // 2]).astype(jnp.int32)

    return pl.pallas_call(
        score_kernel,
        name="scores",
        out_shape=jax.ShapeDtypeStruct((cands, out_seeds), F32),
        in_specs=[SMEM] + [VMEM] * 5,
        out_specs=VMEM,
        scratch_shapes=[pltpu.VMEM((cands * KB, PB), F32)],
        compiler_params=PARAMS,
    )(place, feat_all, eight, eight_more, *other)


def solution(mesh):
    return jax.shard_map(
        local,
        mesh=mesh,
        in_specs=(
            P("dp", None, "mp"),
            P("dp", None, "mp"),
            P("dp", None, None),
            P("dp", None, None),
            P("dp", None, "mp"),
            P("dp", None),
            P("mp", None),
            P(None, "mp"),
            P("mp", None),
            P(),
            P(None, "mp"),
            P(None, "mp"),
            P(),
            P(),
            P(),
            P("dp", "mp"),
        ),
        out_specs=P("dp", "mp"),
        check_vma=False,
    )
```

```python
import math

import jax
import jax.numpy as jnp
from jax import lax
from jax.experimental import pallas as pl
from jax.experimental.pallas import tpu as pltpu
from jax.sharding import PartitionSpec as P

H = 64
KVH = 8
DH = 128
R = 128
K = 8192
PB = 128
NT = 8
S = 512
KB = 64
EPS = 1e-06
LONGEST = 256
ROWS = 128
CHUNK = 32
F32 = jnp.float32
BF16 = jnp.bfloat16


def dot_nn(a, b):
    return lax.dot_general(a, b, (((1,), (0,)), ((), ())), preferred_element_type=F32)


def dot_nt(a, b):
    return lax.dot_general(a, b, (((1,), (1,)), ((), ())), preferred_element_type=F32)


def attention_kernel(
    kv_index,
    hidden_ref,
    query_ref,
    grad_ref,
    key_ref,
    value_ref,
    segment_ref,
    down_query_ref,
    down_value_ref,
    up_query_ref,
    up_value_ref,
    block_ref,
    tile_ref,
    block_value_ref,
    tile_value_ref,
    bank_ref,
    send_ref,
    packed_ref,
    value_sum,
    down_t,
    bias_ref,
    logit_ref,
    prob_grad_ref,
    prob_ref,
    logit_grad_ref,
):
    cand = pl.program_id(0)
    parts = send_ref.shape[0]
    chunk = send_ref.shape[2]
    quarter = R // chunk
    heads = query_ref.shape[2] // DH
    score_scale = 1.0 / math.sqrt(DH)
    exp_scale = score_scale * math.log2(math.e)

    @pl.when(cand == 0)
    def _():
        down_t[:R] = down_query_ref[...].T
        down_t[R:] = down_value_ref[...].T

    width = heads * DH
    kv = kv_index[0]
    for tile in range(bank_ref.shape[0]):
        packed_ref[0, width + DH : width + 2 * DH, tile * PB : (tile + 1) * PB] = bank_ref[tile]
    ids = [
        block_ref[...],
        jnp.concatenate([block_value_ref[pl.ds(kv, 1), :]] * heads, axis=1),
        tile_ref[...],
        jnp.concatenate([tile_value_ref[pl.ds(kv, 1), :]] * heads, axis=1),
        jnp.zeros((8, width), jnp.int32),
    ]
    ids = jnp.concatenate(ids, axis=0).astype(F32).astype(BF16)
    packed_ref[0, width + 2 * DH :] = ids

    lowrank_in = dot_nt(down_t[...], hidden_ref[0])
    send_ref[0 : 2 * quarter, 0] = lowrank_in.astype(BF16).reshape(2 * quarter, chunk, S)

    segment_row = segment_ref[pl.ds(cand, 1), :].astype(F32)
    segment_col = jnp.broadcast_to(segment_row, (8, S)).T[:, 0:1]
    key_t = key_ref[0].T
    value_sum[...] = jnp.zeros_like(value_sum)

    for block in range(S // ROWS):
        first = block * ROWS
        low = max(0, (first - LONGEST + 1) // ROWS * ROWS)
        high = first + ROWS
        reach = high - low
        for at in range(0, reach, ROWS):
            allowed = segment_col[low + at : low + at + ROWS] == segment_row[:, first:high]
            if low + at == first:
                key_pos = lax.broadcasted_iota(jnp.int32, (ROWS, ROWS), 0)
                row_pos = lax.broadcasted_iota(jnp.int32, (ROWS, ROWS), 1)
                allowed = allowed & (key_pos <= row_pos)
            bias_ref[block, at : at + ROWS] = jnp.where(allowed, 0.0, -1e30)
    for block in range(S // ROWS):
        first = block * ROWS
        low = max(0, (first - LONGEST + 1) // ROWS * ROWS)
        high = first + ROWS
        reach = high - low
        slot = block % 2

        def stacked(ref):
            return jnp.concatenate(
                [ref[0, first:high, h * DH : (h + 1) * DH] for h in range(heads)], axis=0
            )

        grad = stacked(grad_ref)
        logit_ref[slot, :reach] = dot_nt(key_ref[0, low:high], stacked(query_ref))
        prob_grad_ref[slot, :reach] = dot_nt(value_ref[0, low:high], grad)

        def logits(at):
            bias = bias_ref[block, at : at + CHUNK]
            return logit_ref[slot, at : at + CHUNK] + jnp.concatenate([bias] * heads, axis=1)

        lanes = heads * ROWS
        top = jnp.full((8, lanes), -3e38, F32)
        for at in range(0, reach, CHUNK):
            top = jnp.maximum(top, jnp.max(logits(at).reshape(CHUNK // 8, 8, lanes), axis=0))
        row_top = jnp.max(top, axis=0, keepdims=True)
        total = jnp.zeros((8, lanes), F32)
        delta = jnp.zeros((8, lanes), F32)
        for at in range(0, reach, CHUNK):
            terms = jnp.exp2((logits(at) - row_top) * exp_scale)
            total = total + jnp.sum(terms.reshape(CHUNK // 8, 8, lanes), axis=0)
            weighted = terms * prob_grad_ref[slot, at : at + CHUNK]
            delta = delta + jnp.sum(weighted.reshape(CHUNK // 8, 8, lanes), axis=0)
            logit_ref[slot, at : at + CHUNK] = terms
        inverse = 1.0 / jnp.sum(total, axis=0, keepdims=True)
        row_delta = jnp.sum(delta, axis=0, keepdims=True) * inverse
        for at in range(0, reach, CHUNK):
            probs = logit_ref[slot, at : at + CHUNK] * inverse
            prob_ref[slot, at : at + CHUNK] = probs.astype(BF16)
            logit_grad_ref[slot, at : at + CHUNK] = (
                probs * (prob_grad_ref[slot, at : at + CHUNK] - row_delta)
            ).astype(BF16)
        value_sum[low:high] += dot_nn(prob_ref[slot, :reach], grad)
        query_grad = dot_nn(key_t[:, low:high], logit_grad_ref[slot, :reach]) * score_scale
        query_grad = query_grad.astype(BF16)
        for h in range(heads):
            packed_ref[0, h * DH : (h + 1) * DH, first:high] = query_grad[
                :, h * ROWS : (h + 1) * ROWS
            ]

    value_grad = value_sum[...].T.astype(BF16)
    packed_ref[0, width : width + DH] = value_grad
    back_query = dot_nn(up_query_ref[...], packed_ref[0, :width])
    back_value = dot_nn(up_value_ref[...], value_grad)
    send_ref[2 * quarter : 3 * quarter, 0] = back_query.astype(BF16).reshape(quarter, chunk, S)
    send_ref[3 * quarter : parts, 0] = back_value.astype(BF16).reshape(quarter, chunk, S)


def sum_kernel(parts_ref, out_ref):
    total = jnp.sum(parts_ref[...].astype(F32), axis=0)
    out_ref[...] = jnp.broadcast_to(total.astype(BF16)[None], out_ref.shape)


def stage_kernel(hidden_ref, packed_ref, out_ref):
    out_ref[...] = hidden_ref[...]


def feature_kernel(
    lowrank_hbm, hidden_ref, packed_ref, out_ref, lowrank_ref, chosen_ref, lowrank_sem
):
    copy = pltpu.make_async_copy(lowrank_hbm, lowrank_ref, lowrank_sem)
    copy.start()
    cands = hidden_ref.shape[0]
    width = hidden_ref.shape[2]
    values = slice(width, width + DH)
    tile_rows = slice(width + DH, width + 2 * DH)
    buckets = KB * NT
    ids = packed_ref[0, width + 2 * DH :].astype(F32)
    ids = (ids[4:8] * KB + ids[0:4]).astype(jnp.int32)
    spans = [(kind * width, width if kind < 3 else DH) for kind in range(4)]
    for kind, (start, count) in enumerate(spans):
        where = lax.broadcasted_iota(jnp.int32, (buckets, count), 0)
        chosen = jnp.where(where == ids[kind : kind + 1, :count], 1.0, 0.0).astype(BF16)
        chosen_ref[:, start : start + count] = chosen
    copy.wait()
    pieces = [[], [], [], []]
    for cand in range(cands):
        lowrank = lowrank_ref[:, cand].reshape(4 * R, S)
        down = dot_nn(lowrank[2 * R :], hidden_ref[cand])
        pieces[0].append(down[:R])
        pieces[1].append(down[R:])
        pieces[2].append(dot_nt(lowrank[:R], packed_ref[cand, :width]))
        pieces[3].append(dot_nt(lowrank[R : 2 * R], packed_ref[cand, values]))
    sums = jnp.zeros((buckets, cands * R), F32)
    for kind, (start, count) in enumerate(spans):
        rows = jnp.concatenate(pieces[kind], axis=0).astype(BF16)
        sums = sums + dot_nt(chosen_ref[:, start : start + count], rows)
    wide = jnp.concatenate(
        [
            jnp.concatenate(
                [sums[t * KB : (t + 1) * KB, c * R : (c + 1) * R] for t in range(NT)], axis=1
            )
            for c in range(cands)
        ],
        axis=0,
    )
    high = wide.astype(BF16)
    low = (wide - high.astype(F32)).astype(BF16)
    tiles = NT // cands
    bank = jnp.concatenate(
        [
            packed_ref[c, tile_rows, t * PB : (t + 1) * PB]
            for c in range(cands)
            for t in range(tiles)
        ],
        axis=0,
    )
    feats = dot_nn(high, bank) + dot_nn(low, bank)
    out_ref[...] = jnp.broadcast_to(feats.astype(BF16)[None], out_ref.shape)


def score_kernel(place, parts_ref, *refs):
    mine_refs, other_refs, (out_ref, feats_ref) = refs[:2], refs[2:4], refs[4:]
    cands = out_ref.shape[0]
    eights, seeds, depth = mine_refs[0].shape
    per_part = depth // PB
    feats_ref[...] = jnp.sum(parts_ref[...].astype(F32), axis=0)
    totals = [[jnp.zeros((seeds, PB), F32) for _ in range(2)] for _ in range(cands)]
    for at in range(2 * eights):
        source = place[1] ^ (at % 2 * 8 + at // 2 % 2 * 4 + at // 4 % 2 * 2 + at // 8)
        for part in range(per_part):
            feat = [
                feats_ref[pl.ds(c * KB + source * per_part + part, 1), :] for c in range(cands)
            ]
            for half, seeds_ref in enumerate((mine_refs[at // eights], other_refs[at // eights])):
                seed = seeds_ref[at % eights, :, part * PB : (part + 1) * PB].astype(F32)
                for c in range(cands):
                    totals[c][half] = totals[c][half] + feat[c] * seed
    first_core = place[0] == 0
    for c in range(cands):
        mine = feats_ref[c * KB : (c + 1) * KB]
        square = jnp.sum(jnp.sum(mine * mine, axis=0, keepdims=True), axis=1, keepdims=True)
        here, there = totals[c]
        ordered = jnp.concatenate(
            [jnp.where(first_core, here, there), jnp.where(first_core, there, here)], axis=0
        )
        numerator = jnp.sum(ordered.T, axis=0, keepdims=True)
        out_ref[c : c + 1, :] = numerator * lax.rsqrt(square / K + EPS) * K ** (-0.5)


VMEM = pl.BlockSpec(memory_space=pltpu.VMEM)
SMEM = pl.BlockSpec(memory_space=pltpu.SMEM)
PARAMS = pltpu.CompilerParams(vmem_limit_bytes=40 << 20)


def local(
    hidden_in,
    query_act,
    key_act,
    value_act,
    ctx_grad,
    segment_ids,
    down_query,
    up_query,
    down_value,
    up_value,
    block_rows,
    tile_rows,
    block_value,
    tile_value,
    tile_bank,
    seed_feats,
):
    model_index = lax.axis_index("mp")
    data_size = lax.axis_size("dp")
    model_size = lax.axis_size("mp")
    cands, seq_len, width = query_act.shape
    heads = width // DH
    kv = (model_index * heads // (H // KVH)).astype(jnp.int32)
    kv_index = kv.reshape(1)
    seeds_dev = seed_feats.shape[0]
    out_seeds = data_size * seeds_dev // model_size

    levels = data_size // 2

    def to_column(flip):
        return lax.ppermute(
            seed_feats,
            ("dp", "mp"),
            [
                (d * model_size + m, ((m ^ flip) * 2 + d % 2) * model_size + d // 2)
                for d in range(data_size)
                for m in range(model_size)
            ],
        )

    def from_level(block, flip):
        return lax.ppermute(block, "dp", [(d, d ^ (2 * flip)) for d in range(data_size)])

    def from_core(block):
        return lax.ppermute(block, "dp", [(d, d ^ 1) for d in range(data_size)])

    seed_near, seed_far = to_column(0), to_column(levels // 2)
    chunk = 4 * R // model_size
    span = LONGEST + ROWS
    packed_rows = width + 2 * DH + 16
    tiles = NT // cands

    def per_cand(*shape):
        return pl.BlockSpec((1, *shape), lambda c, kv_ref: (c, 0, 0))

    def whole(*shape):
        return pl.BlockSpec(shape, lambda c, kv_ref: (0,) * len(shape))

    send, packed = pl.pallas_call(
        attention_kernel,
        name="attention_backward",
        out_shape=(
            jax.ShapeDtypeStruct((model_size, cands, chunk, seq_len), BF16),
            jax.ShapeDtypeStruct((cands, packed_rows, seq_len), BF16),
        ),
        grid_spec=pltpu.PrefetchScalarGridSpec(
            num_scalar_prefetch=1,
            grid=(cands,),
            in_specs=[
                per_cand(seq_len, hidden_in.shape[2]),
                per_cand(seq_len, width),
                per_cand(seq_len, width),
                pl.BlockSpec((1, seq_len, DH), lambda c, kv_ref: (c, 0, kv_ref[0])),
                pl.BlockSpec((1, seq_len, DH), lambda c, kv_ref: (c, 0, kv_ref[0])),
                whole(cands, seq_len),
                whole(*down_query.shape),
                whole(*down_value.shape),
                whole(*up_query.shape),
                pl.BlockSpec((R, DH), lambda c, kv_ref: (0, kv_ref[0])),
                whole(*block_rows.shape),
                whole(*tile_rows.shape),
                whole(KVH, DH),
                whole(KVH, DH),
                pl.BlockSpec((tiles, R, PB), lambda c, kv_ref: (c, 0, 0)),
            ],
            out_specs=[
                pl.BlockSpec((model_size, 1, chunk, seq_len), lambda c, kv_ref: (0, c, 0, 0)),
                per_cand(packed_rows, seq_len),
            ],
            scratch_shapes=[
                pltpu.VMEM((seq_len, DH), F32),
                pltpu.VMEM((2 * R, hidden_in.shape[2]), BF16),
                pltpu.VMEM((seq_len // ROWS, span, ROWS), F32),
                pltpu.VMEM((2, span, heads * ROWS), F32),
                pltpu.VMEM((2, span, heads * ROWS), F32),
                pltpu.VMEM((2, span, heads * ROWS), BF16),
                pltpu.VMEM((2, span, heads * ROWS), BF16),
            ],
        ),
        compiler_params=pltpu.CompilerParams(vmem_limit_bytes=60 << 20),
        cost_estimate=pl.CostEstimate(
            flops=5_000_000_000, bytes_accessed=8_000_000, transcendentals=2_000_000
        ),
    )(
        kv_index,
        hidden_in,
        query_act,
        ctx_grad,
        key_act,
        value_act,
        segment_ids,
        down_query,
        down_value,
        up_query,
        up_value,
        block_rows,
        tile_rows,
        block_value.reshape(KVH, DH),
        tile_value.reshape(KVH, DH),
        tile_bank,
    )

    send, seed_near, seed_far = lax.optimization_barrier((send, seed_near, seed_far))
    received = lax.all_to_all(send, "mp", 0, 0, tiled=True)
    two = jnp.stack([seed_near, seed_far])
    two_more = from_level(two, 4)
    received, two, two_more, hidden_later, packed = lax.optimization_barrier(
        (received, two, two_more, hidden_in, packed)
    )
    summed = pl.pallas_call(
        sum_kernel,
        name="lowrank_sum",
        out_shape=jax.ShapeDtypeStruct(received.shape, BF16),
        in_specs=[VMEM],
        out_specs=VMEM,
        compiler_params=PARAMS,
    )(received)
    lowrank = lax.all_to_all(summed, "mp", 0, 0, tiled=True)
    four = jnp.concatenate([two, two_more])
    four_more = from_level(four, 2)
    eight = jnp.concatenate([four, four_more])
    eight_more = from_level(eight, 1)

    hidden_near = pl.pallas_call(
        stage_kernel,
        name="stage_operands",
        out_shape=jax.ShapeDtypeStruct(hidden_in.shape, BF16),
        in_specs=[VMEM] * 2,
        out_specs=VMEM,
        compiler_params=PARAMS,
        cost_estimate=pl.CostEstimate(
            flops=10_000_000, bytes_accessed=4_000_000, transcendentals=0
        ),
    )(hidden_later, packed)
    feat_parts = pl.pallas_call(
        feature_kernel,
        name="partial_features",
        out_shape=jax.ShapeDtypeStruct((model_size, cands * KB, PB), BF16),
        in_specs=[pl.BlockSpec(memory_space=pl.ANY), VMEM, VMEM],
        out_specs=VMEM,
        scratch_shapes=[
            pltpu.VMEM(lowrank.shape, BF16),
            pltpu.VMEM((KB * NT, 3 * width + DH), BF16),
            pltpu.SemaphoreType.DMA,
        ],
        compiler_params=PARAMS,
    )(lowrank, hidden_near, packed)
    feat_parts, eight = lax.optimization_barrier((feat_parts, eight))
    feat_all = lax.all_to_all(feat_parts, "mp", 0, 0, tiled=True)
    other = [from_core(part) for part in (eight, eight_more)]
    place = jnp.stack([lax.axis_index("dp") % 2, lax.axis_index("dp") // 2]).astype(jnp.int32)

    return pl.pallas_call(
        score_kernel,
        name="scores",
        out_shape=jax.ShapeDtypeStruct((cands, out_seeds), F32),
        in_specs=[SMEM] + [VMEM] * 5,
        out_specs=VMEM,
        scratch_shapes=[pltpu.VMEM((cands * KB, PB), F32)],
        compiler_params=PARAMS,
    )(place, feat_all, eight, eight_more, *other)


def solution(mesh):
    return jax.shard_map(
        local,
        mesh=mesh,
        in_specs=(
            P("dp", None, "mp"),
            P("dp", None, "mp"),
            P("dp", None, None),
            P("dp", None, None),
            P("dp", None, "mp"),
            P("dp", None),
            P("mp", None),
            P(None, "mp"),
            P("mp", None),
            P(),
            P(None, "mp"),
            P(None, "mp"),
            P(),
            P(),
            P(),
            P("dp", "mp"),
        ),
        out_specs=P("dp", "mp"),
        check_vma=False,
    )
```

```python
import math

import jax
import jax.numpy as jnp
from jax import lax
from jax.experimental import pallas as pl
from jax.experimental.pallas import tpu as pltpu
from jax.sharding import PartitionSpec as P

H = 64
KVH = 8
DH = 128
R = 128
K = 8192
PB = 128
NT = 8
S = 512
KB = 64
EPS = 1e-06
LONGEST = 256
ROWS = 128
CHUNK = 32
F32 = jnp.float32
BF16 = jnp.bfloat16


def dot_nn(a, b):
    return lax.dot_general(a, b, (((1,), (0,)), ((), ())), preferred_element_type=F32)


def dot_nt(a, b):
    return lax.dot_general(a, b, (((1,), (1,)), ((), ())), preferred_element_type=F32)


def attention_kernel(
    kv_index,
    hidden_ref,
    query_ref,
    grad_ref,
    key_ref,
    value_ref,
    segment_ref,
    down_query_ref,
    down_value_ref,
    up_query_ref,
    up_value_ref,
    block_ref,
    tile_ref,
    block_value_ref,
    tile_value_ref,
    bank_ref,
    send_ref,
    packed_ref,
    value_sum,
    down_t,
    bias_ref,
    logit_ref,
    prob_grad_ref,
    prob_ref,
    logit_grad_ref,
):
    cand = pl.program_id(0)
    parts = send_ref.shape[0]
    chunk = send_ref.shape[2]
    quarter = R // chunk
    heads = query_ref.shape[2] // DH
    score_scale = 1.0 / math.sqrt(DH)
    exp_scale = score_scale * math.log2(math.e)

    @pl.when(cand == 0)
    def _():
        down_t[:R] = down_query_ref[...].T
        down_t[R:] = down_value_ref[...].T

    width = heads * DH
    kv = kv_index[0]
    for tile in range(bank_ref.shape[0]):
        packed_ref[0, width + DH : width + 2 * DH, tile * PB : (tile + 1) * PB] = bank_ref[tile]
    ids = [
        block_ref[...],
        jnp.concatenate([block_value_ref[pl.ds(kv, 1), :]] * heads, axis=1),
        tile_ref[...],
        jnp.concatenate([tile_value_ref[pl.ds(kv, 1), :]] * heads, axis=1),
        jnp.zeros((8, width), jnp.int32),
    ]
    ids = jnp.concatenate(ids, axis=0).astype(F32).astype(BF16)
    packed_ref[0, width + 2 * DH :] = ids

    lowrank_in = dot_nt(down_t[...], hidden_ref[0])
    send_ref[0 : 2 * quarter, 0] = lowrank_in.astype(BF16).reshape(2 * quarter, chunk, S)

    segment_row = segment_ref[pl.ds(cand, 1), :].astype(F32)
    segment_col = jnp.broadcast_to(segment_row, (8, S)).T[:, 0:1]
    key_t = key_ref[0].T
    value_sum[...] = jnp.zeros_like(value_sum)

    for block in range(S // ROWS):
        first = block * ROWS
        low = max(0, (first - LONGEST + 1) // ROWS * ROWS)
        high = first + ROWS
        reach = high - low
        for at in range(0, reach, ROWS):
            allowed = segment_col[low + at : low + at + ROWS] == segment_row[:, first:high]
            if low + at == first:
                key_pos = lax.broadcasted_iota(jnp.int32, (ROWS, ROWS), 0)
                row_pos = lax.broadcasted_iota(jnp.int32, (ROWS, ROWS), 1)
                allowed = allowed & (key_pos <= row_pos)
            bias_ref[block, at : at + ROWS] = jnp.where(allowed, 0.0, -1e30)
    for block in range(S // ROWS):
        first = block * ROWS
        low = max(0, (first - LONGEST + 1) // ROWS * ROWS)
        high = first + ROWS
        reach = high - low
        slot = block % 2

        def stacked(ref):
            return jnp.concatenate(
                [ref[0, first:high, h * DH : (h + 1) * DH] for h in range(heads)], axis=0
            )

        grad = stacked(grad_ref)
        logit_ref[slot, :reach] = dot_nt(key_ref[0, low:high], stacked(query_ref))
        prob_grad_ref[slot, :reach] = dot_nt(value_ref[0, low:high], grad)

        def logits(at):
            bias = bias_ref[block, at : at + CHUNK]
            return logit_ref[slot, at : at + CHUNK] + jnp.concatenate([bias] * heads, axis=1)

        lanes = heads * ROWS
        top = jnp.full((8, lanes), -3e38, F32)
        for at in range(0, reach, CHUNK):
            top = jnp.maximum(top, jnp.max(logits(at).reshape(CHUNK // 8, 8, lanes), axis=0))
        row_top = jnp.max(top, axis=0, keepdims=True)
        total = jnp.zeros((8, lanes), F32)
        delta = jnp.zeros((8, lanes), F32)
        for at in range(0, reach, CHUNK):
            terms = jnp.exp2((logits(at) - row_top) * exp_scale)
            total = total + jnp.sum(terms.reshape(CHUNK // 8, 8, lanes), axis=0)
            weighted = terms * prob_grad_ref[slot, at : at + CHUNK]
            delta = delta + jnp.sum(weighted.reshape(CHUNK // 8, 8, lanes), axis=0)
            logit_ref[slot, at : at + CHUNK] = terms
        inverse = 1.0 / jnp.sum(total, axis=0, keepdims=True)
        row_delta = jnp.sum(delta, axis=0, keepdims=True) * inverse
        for at in range(0, reach, CHUNK):
            probs = logit_ref[slot, at : at + CHUNK] * inverse
            prob_ref[slot, at : at + CHUNK] = probs.astype(BF16)
            logit_grad_ref[slot, at : at + CHUNK] = (
                probs * (prob_grad_ref[slot, at : at + CHUNK] - row_delta)
            ).astype(BF16)
        value_sum[low:high] += dot_nn(prob_ref[slot, :reach], grad)
        query_grad = dot_nn(key_t[:, low:high], logit_grad_ref[slot, :reach]) * score_scale
        query_grad = query_grad.astype(BF16)
        for h in range(heads):
            packed_ref[0, h * DH : (h + 1) * DH, first:high] = query_grad[
                :, h * ROWS : (h + 1) * ROWS
            ]

    value_grad = value_sum[...].T.astype(BF16)
    packed_ref[0, width : width + DH] = value_grad
    back_query = dot_nn(up_query_ref[...], packed_ref[0, :width])
    back_value = dot_nn(up_value_ref[...], value_grad)
    send_ref[2 * quarter : 3 * quarter, 0] = back_query.astype(BF16).reshape(quarter, chunk, S)
    send_ref[3 * quarter : parts, 0] = back_value.astype(BF16).reshape(quarter, chunk, S)


def sum_kernel(parts_ref, out_ref):
    total = jnp.sum(parts_ref[...].astype(F32), axis=0)
    out_ref[...] = jnp.broadcast_to(total.astype(BF16)[None], out_ref.shape)


def stage_kernel(hidden_ref, packed_ref, out_ref):
    out_ref[...] = hidden_ref[...]


def feature_kernel(
    lowrank_hbm, hidden_ref, packed_ref, out_ref, lowrank_ref, chosen_ref, lowrank_sems
):
    cands = hidden_ref.shape[0]
    copies = [
        pltpu.make_async_copy(lowrank_hbm.at[:, c], lowrank_ref.at[c], lowrank_sems.at[c])
        for c in range(cands)
    ]
    for copy in copies:
        copy.start()
    width = hidden_ref.shape[2]
    values = slice(width, width + DH)
    tile_rows = slice(width + DH, width + 2 * DH)
    buckets = KB * NT
    ids = packed_ref[0, width + 2 * DH :].astype(F32)
    ids = (ids[4:8] * KB + ids[0:4]).astype(jnp.int32)
    spans = [(kind * width, width if kind < 3 else DH) for kind in range(4)]
    for kind, (start, count) in enumerate(spans):
        where = lax.broadcasted_iota(jnp.int32, (buckets, count), 0)
        chosen = jnp.where(where == ids[kind : kind + 1, :count], 1.0, 0.0).astype(BF16)
        chosen_ref[:, start : start + count] = chosen
    pieces = [[], [], [], []]
    for cand in range(cands):
        copies[cand].wait()
        lowrank = lowrank_ref[cand].reshape(4 * R, S)
        down = dot_nn(lowrank[2 * R :], hidden_ref[cand])
        pieces[0].append(down[:R])
        pieces[1].append(down[R:])
        pieces[2].append(dot_nt(lowrank[:R], packed_ref[cand, :width]))
        pieces[3].append(dot_nt(lowrank[R : 2 * R], packed_ref[cand, values]))
    sums = jnp.zeros((buckets, cands * R), F32)
    for kind, (start, count) in enumerate(spans):
        rows = jnp.concatenate(pieces[kind], axis=0).astype(BF16)
        sums = sums + dot_nt(chosen_ref[:, start : start + count], rows)
    wide = jnp.concatenate(
        [
            jnp.concatenate(
                [sums[t * KB : (t + 1) * KB, c * R : (c + 1) * R] for t in range(NT)], axis=1
            )
            for c in range(cands)
        ],
        axis=0,
    )
    high = wide.astype(BF16)
    low = (wide - high.astype(F32)).astype(BF16)
    tiles = NT // cands
    bank = jnp.concatenate(
        [
            packed_ref[c, tile_rows, t * PB : (t + 1) * PB]
            for c in range(cands)
            for t in range(tiles)
        ],
        axis=0,
    )
    feats = dot_nn(high, bank) + dot_nn(low, bank)
    out_ref[...] = jnp.broadcast_to(feats.astype(BF16)[None], out_ref.shape)


def score_kernel(place, parts_ref, *refs):
    mine_refs, other_refs, (out_ref, feats_ref) = refs[:2], refs[2:4], refs[4:]
    cands = out_ref.shape[0]
    eights, seeds, depth = mine_refs[0].shape
    per_part = depth // PB
    feats_ref[...] = jnp.sum(parts_ref[...].astype(F32), axis=0)
    totals = [[jnp.zeros((seeds, PB), F32) for _ in range(2)] for _ in range(cands)]
    for at in range(2 * eights):
        source = place[1] ^ (at % 2 * 8 + at // 2 % 2 * 4 + at // 4 % 2 * 2 + at // 8)
        for part in range(per_part):
            feat = [
                feats_ref[pl.ds(c * KB + source * per_part + part, 1), :] for c in range(cands)
            ]
            for half, seeds_ref in enumerate((mine_refs[at // eights], other_refs[at // eights])):
                seed = seeds_ref[at % eights, :, part * PB : (part + 1) * PB].astype(F32)
                for c in range(cands):
                    totals[c][half] = totals[c][half] + feat[c] * seed
    first_core = place[0] == 0
    for c in range(cands):
        mine = feats_ref[c * KB : (c + 1) * KB]
        square = jnp.sum(jnp.sum(mine * mine, axis=0, keepdims=True), axis=1, keepdims=True)
        here, there = totals[c]
        ordered = jnp.concatenate(
            [jnp.where(first_core, here, there), jnp.where(first_core, there, here)], axis=0
        )
        numerator = jnp.sum(ordered.T, axis=0, keepdims=True)
        out_ref[c : c + 1, :] = numerator * lax.rsqrt(square / K + EPS) * K ** (-0.5)


VMEM = pl.BlockSpec(memory_space=pltpu.VMEM)
SMEM = pl.BlockSpec(memory_space=pltpu.SMEM)
PARAMS = pltpu.CompilerParams(vmem_limit_bytes=40 << 20)


def local(
    hidden_in,
    query_act,
    key_act,
    value_act,
    ctx_grad,
    segment_ids,
    down_query,
    up_query,
    down_value,
    up_value,
    block_rows,
    tile_rows,
    block_value,
    tile_value,
    tile_bank,
    seed_feats,
):
    model_index = lax.axis_index("mp")
    data_size = lax.axis_size("dp")
    model_size = lax.axis_size("mp")
    cands, seq_len, width = query_act.shape
    heads = width // DH
    kv = (model_index * heads // (H // KVH)).astype(jnp.int32)
    kv_index = kv.reshape(1)
    seeds_dev = seed_feats.shape[0]
    out_seeds = data_size * seeds_dev // model_size

    levels = data_size // 2

    def to_column(flip):
        return lax.ppermute(
            seed_feats,
            ("dp", "mp"),
            [
                (d * model_size + m, ((m ^ flip) * 2 + d % 2) * model_size + d // 2)
                for d in range(data_size)
                for m in range(model_size)
            ],
        )

    def from_level(block, flip):
        return lax.ppermute(block, "dp", [(d, d ^ (2 * flip)) for d in range(data_size)])

    def from_core(block):
        return lax.ppermute(block, "dp", [(d, d ^ 1) for d in range(data_size)])

    seed_near, seed_far = to_column(0), to_column(levels // 2)
    chunk = 4 * R // model_size
    span = LONGEST + ROWS
    packed_rows = width + 2 * DH + 16
    tiles = NT // cands

    def per_cand(*shape):
        return pl.BlockSpec((1, *shape), lambda c, kv_ref: (c, 0, 0))

    def whole(*shape):
        return pl.BlockSpec(shape, lambda c, kv_ref: (0,) * len(shape))

    send, packed = pl.pallas_call(
        attention_kernel,
        name="attention_backward",
        out_shape=(
            jax.ShapeDtypeStruct((model_size, cands, chunk, seq_len), BF16),
            jax.ShapeDtypeStruct((cands, packed_rows, seq_len), BF16),
        ),
        grid_spec=pltpu.PrefetchScalarGridSpec(
            num_scalar_prefetch=1,
            grid=(cands,),
            in_specs=[
                per_cand(seq_len, hidden_in.shape[2]),
                per_cand(seq_len, width),
                per_cand(seq_len, width),
                pl.BlockSpec((1, seq_len, DH), lambda c, kv_ref: (c, 0, kv_ref[0])),
                pl.BlockSpec((1, seq_len, DH), lambda c, kv_ref: (c, 0, kv_ref[0])),
                whole(cands, seq_len),
                whole(*down_query.shape),
                whole(*down_value.shape),
                whole(*up_query.shape),
                pl.BlockSpec((R, DH), lambda c, kv_ref: (0, kv_ref[0])),
                whole(*block_rows.shape),
                whole(*tile_rows.shape),
                whole(KVH, DH),
                whole(KVH, DH),
                pl.BlockSpec((tiles, R, PB), lambda c, kv_ref: (c, 0, 0)),
            ],
            out_specs=[
                pl.BlockSpec((model_size, 1, chunk, seq_len), lambda c, kv_ref: (0, c, 0, 0)),
                per_cand(packed_rows, seq_len),
            ],
            scratch_shapes=[
                pltpu.VMEM((seq_len, DH), F32),
                pltpu.VMEM((2 * R, hidden_in.shape[2]), BF16),
                pltpu.VMEM((seq_len // ROWS, span, ROWS), F32),
                pltpu.VMEM((2, span, heads * ROWS), F32),
                pltpu.VMEM((2, span, heads * ROWS), F32),
                pltpu.VMEM((2, span, heads * ROWS), BF16),
                pltpu.VMEM((2, span, heads * ROWS), BF16),
            ],
        ),
        compiler_params=pltpu.CompilerParams(vmem_limit_bytes=60 << 20),
        cost_estimate=pl.CostEstimate(
            flops=5_000_000_000, bytes_accessed=8_000_000, transcendentals=2_000_000
        ),
    )(
        kv_index,
        hidden_in,
        query_act,
        ctx_grad,
        key_act,
        value_act,
        segment_ids,
        down_query,
        down_value,
        up_query,
        up_value,
        block_rows,
        tile_rows,
        block_value.reshape(KVH, DH),
        tile_value.reshape(KVH, DH),
        tile_bank,
    )

    send, seed_near, seed_far = lax.optimization_barrier((send, seed_near, seed_far))
    received = lax.all_to_all(send, "mp", 0, 0, tiled=True)
    two = jnp.stack([seed_near, seed_far])
    two_more = from_level(two, 4)
    received, two, two_more, hidden_later, packed = lax.optimization_barrier(
        (received, two, two_more, hidden_in, packed)
    )
    summed = pl.pallas_call(
        sum_kernel,
        name="lowrank_sum",
        out_shape=jax.ShapeDtypeStruct(received.shape, BF16),
        in_specs=[VMEM],
        out_specs=VMEM,
        compiler_params=PARAMS,
    )(received)
    lowrank = lax.all_to_all(summed, "mp", 0, 0, tiled=True)
    four = jnp.concatenate([two, two_more])
    four_more = from_level(four, 2)
    eight = jnp.concatenate([four, four_more])
    eight_more = from_level(eight, 1)

    hidden_near = pl.pallas_call(
        stage_kernel,
        name="stage_operands",
        out_shape=jax.ShapeDtypeStruct(hidden_in.shape, BF16),
        in_specs=[VMEM] * 2,
        out_specs=VMEM,
        compiler_params=PARAMS,
        cost_estimate=pl.CostEstimate(
            flops=10_000_000, bytes_accessed=4_000_000, transcendentals=0
        ),
    )(hidden_later, packed)
    feat_parts = pl.pallas_call(
        feature_kernel,
        name="partial_features",
        out_shape=jax.ShapeDtypeStruct((model_size, cands * KB, PB), BF16),
        in_specs=[pl.BlockSpec(memory_space=pl.ANY), VMEM, VMEM],
        out_specs=VMEM,
        scratch_shapes=[
            pltpu.VMEM((cands, model_size, chunk, seq_len), BF16),
            pltpu.VMEM((KB * NT, 3 * width + DH), BF16),
            pltpu.SemaphoreType.DMA((cands,)),
        ],
        compiler_params=PARAMS,
    )(lowrank, hidden_near, packed)
    feat_parts, eight = lax.optimization_barrier((feat_parts, eight))
    feat_all = lax.all_to_all(feat_parts, "mp", 0, 0, tiled=True)
    other = [from_core(part) for part in (eight, eight_more)]
    place = jnp.stack([lax.axis_index("dp") % 2, lax.axis_index("dp") // 2]).astype(jnp.int32)

    return pl.pallas_call(
        score_kernel,
        name="scores",
        out_shape=jax.ShapeDtypeStruct((cands, out_seeds), F32),
        in_specs=[SMEM] + [VMEM] * 5,
        out_specs=VMEM,
        scratch_shapes=[pltpu.VMEM((cands * KB, PB), F32)],
        compiler_params=PARAMS,
    )(place, feat_all, eight, eight_more, *other)


def solution(mesh):
    return jax.shard_map(
        local,
        mesh=mesh,
        in_specs=(
            P("dp", None, "mp"),
            P("dp", None, "mp"),
            P("dp", None, None),
            P("dp", None, None),
            P("dp", None, "mp"),
            P("dp", None),
            P("mp", None),
            P(None, "mp"),
            P("mp", None),
            P(),
            P(None, "mp"),
            P(None, "mp"),
            P(),
            P(),
            P(),
            P("dp", "mp"),
        ),
        out_specs=P("dp", "mp"),
        check_vma=False,
    )
```
